32 devices in a mesh: fsdp: 4 (over z), ctx: 4 (over x, core), tp: 2 (over y).
Axes of the slice: x: 2, y: 2, z: 4, core: 2. Of those that a mesh axis runs over, the one named last changes fastest.
Arguments:
- layer_input: bfloat16 [16384, 1024], P(('fsdp', 'ctx')), may hold values from -6 to 6
- seq_lengths: int32 [4, 2], P('fsdp'), may hold values from 1 to 3072, 4096 in all within a row
- deal_order: int32 [16384], P(('fsdp', 'ctx')), may hold values from 0 to 16383, as said below
- qkv_weight: bfloat16 [1024, 3, 1024], P('fsdp', None, 'tp'), may hold values from -0.1875 to 0.1875
- qkv_bias: bfloat16 [3, 1024], P(None, ('tp', 'fsdp')), may hold values from -0.3125 to 0.3125
- out_weight: bfloat16 [1024, 1024], P(('tp', 'fsdp')), may hold values from -3 to 3
- out_bias: bfloat16 [1024], P('fsdp'), may hold values from -1.75 to 1.75
- first_gain: bfloat16 [1024], P('fsdp'), may hold values from 0.5 to 1.5
- first_shift: bfloat16 [1024], P('fsdp'), may hold values from -1.75 to 1.75
- up_weight: bfloat16 [1024, 4096], P('fsdp', 'tp'), may hold values from -0.1875 to 0.1875
- up_bias: bfloat16 [4096], P(('tp', 'fsdp')), may hold values from -1.75 to 1.75
- down_weight: bfloat16 [4096, 1024], P(('tp', 'fsdp')), may hold values from -0.09375 to 0.09375
- down_bias: bfloat16 [1024], P('fsdp'), may hold values from -1.75 to 1.75
- second_gain: bfloat16 [1024], P('fsdp'), may hold values from 0.5 to 1.5
- second_shift: bfloat16 [1024], P('fsdp'), may hold values from -1.75 to 1.75
- proj_weight: bfloat16 [1024, 288], P('fsdp'), may hold values from -0.1875 to 0.1875
- cot_output: bfloat16 [16384, 1024], P(('fsdp', 'ctx')), may hold values from -6 to 6
- cot_embed: bfloat16 [16384, 288], P(('fsdp', 'ctx')), may hold values from -6 to 6
Outputs:
- output: bfloat16 [16384, 1024], P(('fsdp', 'ctx'))
- embed_out: bfloat16 [16384, 288], P(('fsdp', 'ctx'))
- input_grad: bfloat16 [16384, 1024], P(('fsdp', 'ctx'))
- qkv_weight_grad: float32 [1024, 3, 1024], P('fsdp', None, 'tp')
- qkv_bias_grad: float32 [3, 1024], P(None, ('tp', 'fsdp'))
- out_weight_grad: float32 [1024, 1024], P(('tp', 'fsdp'))
- out_bias_grad: float32 [1024], P('fsdp')
- first_gain_grad: float32 [1024], P('fsdp')
- first_shift_grad: float32 [1024], P('fsdp')
- up_weight_grad: float32 [1024, 4096], P('fsdp', 'tp')
- up_bias_grad: float32 [4096], P(('tp', 'fsdp'))
- down_weight_grad: float32 [4096, 1024], P(('tp', 'fsdp'))
- down_bias_grad: float32 [1024], P('fsdp')
- second_gain_grad: float32 [1024], P('fsdp')
- second_shift_grad: float32 [1024], P('fsdp')
- proj_weight_grad: float32 [1024, 288], P('fsdp')
The draws below stay inside these ranges and needn't reach their ends.
Inputs may be any that keep to these rules, and one draw needn't show every extreme that they name: Each row of seq_lengths holds the lengths of the 2 sequences of one group; they sum to 4096 and the longest is at most 3072. `deal_order`: each aligned block of 4096 entries holds every row index of that same block exactly once.
All inputs are finite; a program needn't handle non-finite values.
Results may differ from the reference program's by a relative error of at most 0.025.
Values may be sent and summed in bfloat16 or wider, within the bound.
No kernel may reach another device: no remote copies, remote signals or barrier semaphores. Data moves between devices by JAX's collectives and lax.ppermute only.
A program may use at most 192 MiB of HBM per device.

```python
import math
import jax
import jax.numpy as jnp
import numpy as np
from jax import lax

D = 1024
HEADS = 16
HEAD_DIM = 64
FF = 4096
PROJ_A = 128
PROJ_B = 96
PROJ_C = 64
EMB = 288
SEQS = 2
GROUPS = 4
GROUP_TOK = 4096
LONGEST = 3072
TOKENS = 16384


def draw_deal_order(key, part):
    group_keys = jax.random.split(key, GROUPS)
    local_order = jax.vmap(lambda group_key: jax.random.permutation(group_key, GROUP_TOK))(group_keys)
    offsets = (jnp.arange(GROUPS, dtype=jnp.int32) * GROUP_TOK)[:, None]
    return (local_order.astype(jnp.int32) + offsets).reshape(TOKENS)


def block_levels(key, extent, cuts, smallest, largest):
    gain, own = 1.0, jax.random.fold_in(key, 6)
    for dim, shards_of in cuts:
        heights = jnp.exp(jax.random.uniform(jax.random.fold_in(own, dim), (shards_of,), jnp.float32, smallest / len(cuts), largest / len(cuts)))
        gain = gain * jnp.repeat(heights, extent[dim] // shards_of).reshape([-1 if axis == dim else 1 for axis in range(len(extent))])
    return gain


def profile(number_of, total, limit, slope):
    portions = [(1 << 20) // math.isqrt(grade ** slope) + 1 for grade in range(2, number_of + 1)]
    spare, given = total - limit - (number_of - 1), [1] * (number_of - 1)
    while spare > 0:
        candidates = [i for i in range(number_of - 1) if given[i] < limit]
        pool, remaining = sum([portions[i] for i in candidates]), spare
        for i in candidates:
            more = min(limit - given[i], max(1, remaining * portions[i] // pool), spare)
            given[i] = given[i] + more
            spare = spare - more
    return np.array([limit] + given)


def ragged(own_key, count, total, most, slope):
    if count == 2:
        one = jax.random.randint(own_key, (), max(1, total - most), min(most, total - 1) + 1)
        return jnp.stack([one, total - one])
    lengths = jnp.asarray(profile(count, total, most, slope), jnp.int32)
    twos = (count - 1) // 2
    source_of, sink = lengths[1:1 + 2 * twos:2], lengths[2:2 + 2 * twos:2]
    room = jnp.minimum(source_of - 1, most - sink)
    passed = jax.random.randint(jax.random.fold_in(own_key, 1), (twos,), 0, 1 << 20) % (room + 1)
    lengths = lengths.at[1:1 + 2 * twos:2].set(source_of - passed).at[2:2 + 2 * twos:2].set(sink + passed)
    return lengths[jax.random.permutation(jax.random.fold_in(own_key, 2), count)]


def bell_draw(key, shape, scale, most, cuts=(), kind=jnp.bfloat16):
    level = block_levels(key, shape, cuts, -0.22, 0.18) if cuts else 1.0
    array = jax.random.normal(key, shape, jnp.float32) * scale * level
    return jnp.minimum(jnp.maximum(array, -most), most).astype(kind)


def setup_inputs(seed: int = 0) -> dict:
    splits = jax.random.split(jax.random.key(seed), 19)
    return {
        "layer_input": bell_draw(splits[0], (TOKENS, D), 1.0, 6.0, ((0, 16),)),
        "seq_lengths": jax.vmap(lambda own: ragged(own, SEQS, GROUP_TOK, LONGEST, 2))(jax.random.split(splits[1], GROUPS)).reshape((GROUPS, SEQS)).astype(jnp.int32),
        "deal_order": draw_deal_order(jax.random.fold_in(splits[18], 71), 0),
        "qkv_weight": bell_draw(splits[3], (D, 3, D), D ** -0.5, 0.1875, ((0, 4), (2, 2))),
        "qkv_bias": bell_draw(splits[4], (3, D), 0.05, 0.3125, ((1, 8),)),
        "out_weight": bell_draw(splits[5], (D, D), (D // 256) ** -0.5, 3.0, ((0, 8),)),
        "out_bias": bell_draw(splits[6], (D,), 0.3, 1.75, ((0, 4),)),
        "first_gain": jnp.clip(1.0 + 0.1 * jax.random.normal(splits[7], (D,), jnp.float32), 0.5, 1.5).astype(jnp.bfloat16),
        "first_shift": bell_draw(splits[8], (D,), 0.3, 1.75, ((0, 4),)),
        "up_weight": bell_draw(splits[9], (D, FF), D ** -0.5, 0.1875, ((0, 4), (1, 2))),
        "up_bias": bell_draw(splits[10], (FF,), 0.3, 1.75, ((0, 8),)),
        "down_weight": bell_draw(splits[11], (FF, D), FF ** -0.5, 0.09375, ((0, 8),)),
        "down_bias": bell_draw(splits[12], (D,), 0.3, 1.75, ((0, 4),)),
        "second_gain": jnp.clip(1.0 + 0.1 * jax.random.normal(splits[13], (D,), jnp.float32), 0.5, 1.5).astype(jnp.bfloat16),
        "second_shift": bell_draw(splits[14], (D,), 0.3, 1.75, ((0, 4),)),
        "proj_weight": bell_draw(splits[15], (D, EMB), D ** -0.5, 0.1875, ((0, 4),)),
        "cot_output": bell_draw(splits[16], (TOKENS, D), 1.0, 6.0, ((0, 16),)),
        "cot_embed": bell_draw(splits[17], (TOKENS, EMB), 1.0, 6.0, ((0, 16),)),
    }


@jax.custom_vjp
def low(v):
    return lax.optimization_barrier(v.astype(jnp.bfloat16)).astype(jnp.float32)

@jax.custom_vjp
def low_back(v):
    return v

def low_keep(v):
    return (low(v), None)

def low_pass(kept, grad):
    return (grad,)

def back_keep(v):
    return (v, None)

def back_low(kept, grad):
    return (low(grad),)
low.defvjp(low_keep, low_pass)
low_back.defvjp(back_keep, back_low)
norm_eps = 1e-05
embed_eps = 1e-06
rope_base = 10000.0
masked_score = -1e+30

def matmul(left, right):
    return jnp.dot(left, right, precision=lax.Precision.HIGHEST, preferred_element_type=jnp.float32)

def layer_norm(values, norm_gain, norm_shift):
    centred = values - lax.optimization_barrier(jnp.mean(values, axis=-1, keepdims=True))
    variance = lax.optimization_barrier(jnp.mean(centred * centred, axis=-1, keepdims=True))
    return centred * lax.rsqrt(variance + norm_eps) * norm_gain + norm_shift

def rotate(values, cos_table, sin_table):
    half_dim = values.shape[-1] // 2
    front_half = values[..., :half_dim]
    back_half = values[..., half_dim:]
    return jnp.concatenate([front_half * cos_table - back_half * sin_table, back_half * cos_table + front_half * sin_table], axis=-1)

def rope_tables(position, head_width):
    half_dim = head_width // 2
    frequency = jnp.exp(jnp.arange(half_dim, dtype=jnp.float32) * (-2.0 * math.log(rope_base) / head_width))
    angles = position.astype(jnp.float32)[:, None] * frequency[None, :]
    return (jnp.cos(angles)[:, None, :], jnp.sin(angles)[:, None, :])

def sequence_layout(seq_lengths, row_ids):
    seq_ends = jnp.cumsum(seq_lengths).astype(jnp.int32)
    segment = lax.optimization_barrier(jnp.sum((row_ids[:, None] >= seq_ends[None, :]).astype(jnp.int32), axis=1)).astype(jnp.int32)
    seq_starts = seq_ends - seq_lengths
    picked = (segment[:, None] == jnp.arange(seq_lengths.shape[0], dtype=jnp.int32)[None, :]).astype(jnp.int32)
    position = (row_ids - lax.optimization_barrier(jnp.sum(picked * seq_starts[None, :], axis=1))).astype(jnp.int32)
    return (segment, position)

def embed_heads(projected):
    pieces = []
    column_start = 0
    for head_width in (PROJ_A, PROJ_B, PROJ_C):
        head_cols = projected[:, column_start:column_start + head_width]
        pieces.append(head_cols * lax.rsqrt(lax.optimization_barrier(jnp.sum(head_cols * head_cols, axis=1, keepdims=True)) + embed_eps))
        column_start += head_width
    return jnp.concatenate(pieces, axis=1)

def head_attention(query_rows, key_rows, value_rows, same_seq):
    scores = low_back(matmul(query_rows, key_rows.T) * HEAD_DIM ** (-0.5))
    scores = jnp.where(same_seq, scores, masked_score)
    row_top = lax.optimization_barrier(jnp.max(scores, axis=1, keepdims=True))
    weights = jnp.exp(scores - row_top)
    row_probs = weights / lax.optimization_barrier(jnp.sum(weights, axis=1, keepdims=True))
    return matmul(low(row_probs), value_rows)

def group_attention(query_all, key_all, value_all, segment):
    same_seq = segment[:, None] == segment[None, :]
    one_head = jax.checkpoint(lambda head_index: head_attention(query_all[:, head_index], key_all[:, head_index], value_all[:, head_index], same_seq))
    return lax.map(one_head, jnp.arange(HEADS))

def forward(layer_input, qkv_weight, qkv_bias, out_weight, out_bias, first_gain, first_shift, up_weight, up_bias, down_weight, down_bias, second_gain, second_shift, proj_weight, deal_order, segment, position):
    packed = layer_input[deal_order]
    mixed = jnp.einsum('td,dwe->twe', packed, qkv_weight, precision=lax.Precision.HIGHEST)
    qkv = low_back(mixed) + qkv_bias[None]
    cos_table, sin_table = rope_tables(position, HEAD_DIM)
    query_all = low(rotate(qkv[:, 0].reshape(TOKENS, HEADS, HEAD_DIM), cos_table, sin_table))
    key_all = low(rotate(qkv[:, 1].reshape(TOKENS, HEADS, HEAD_DIM), cos_table, sin_table))
    value_all = low(qkv[:, 2].reshape(TOKENS, HEADS, HEAD_DIM))
    checked = jax.checkpoint(group_attention)
    attended = lax.map(lambda group_parts: checked(*group_parts), (query_all.reshape(GROUPS, GROUP_TOK, HEADS, HEAD_DIM), key_all.reshape(GROUPS, GROUP_TOK, HEADS, HEAD_DIM), value_all.reshape(GROUPS, GROUP_TOK, HEADS, HEAD_DIM), segment.reshape(GROUPS, GROUP_TOK)))
    attended = jnp.transpose(attended, (0, 2, 1, 3)).reshape(TOKENS, D)
    first_sum = packed + low_back(matmul(low(attended), out_weight)) + out_bias
    normed = layer_norm(first_sum, first_gain, first_shift)
    up_out = low_back(matmul(low(normed), up_weight)) + up_bias
    activated = jax.nn.gelu(up_out, approximate=False)
    second_sum = normed + low_back(matmul(low(activated), down_weight)) + down_bias
    final = layer_norm(second_sum, second_gain, second_shift)
    projected = low_back(matmul(low(final), proj_weight))
    embedded = embed_heads(projected)
    ordered = jnp.zeros_like(final).at[deal_order].set(final)
    ordered_embed = jnp.zeros_like(embedded).at[deal_order].set(embedded)
    return (ordered, ordered_embed)

def reference(layer_input, seq_lengths, deal_order, qkv_weight, qkv_bias, out_weight, out_bias, first_gain, first_shift, up_weight, up_bias, down_weight, down_bias, second_gain, second_shift, proj_weight, cot_output, cot_embed):
    row_ids = jnp.arange(GROUP_TOK, dtype=jnp.int32)
    segment, position = jax.vmap(lambda group_lengths: sequence_layout(group_lengths, row_ids))(seq_lengths)
    segment = segment.reshape(TOKENS)
    position = position.reshape(TOKENS)
    float_args = [weight_arg.astype(jnp.float32) for weight_arg in (layer_input, qkv_weight, qkv_bias, out_weight, out_bias, first_gain, first_shift, up_weight, up_bias, down_weight, down_bias, second_gain, second_shift, proj_weight)]
    outputs, pullback = jax.vjp(lambda *layer_args: forward(*layer_args, deal_order, segment, position), *float_args)
    grads = pullback((cot_output.astype(jnp.float32), cot_embed.astype(jnp.float32)))
    return (outputs[0].astype(jnp.bfloat16), outputs[1].astype(jnp.bfloat16), grads[0].astype(jnp.bfloat16), grads[1], grads[2], grads[3], grads[4], grads[5], grads[6], grads[7], grads[8], grads[9], grads[10], grads[11], grads[12], grads[13])
```

```python
from functools import partial
import math

import jax
import jax.numpy as jnp
from jax import lax
from jax.sharding import PartitionSpec as P

HEAD_DIM = 64
PROJ_A = 128
PROJ_B = 96
PROJ_C = 64


norm_eps = 1e-05
embed_eps = 1e-06
rope_base = 10000.0
masked_score = -1e30


def layer_norm(values, norm_gain, norm_shift):
    centred = values - jnp.mean(values, axis=-1, keepdims=True)
    variance = jnp.mean(centred * centred, axis=-1, keepdims=True)
    return centred * lax.rsqrt(variance + norm_eps) * norm_gain + norm_shift


def rotate(values, cos_table, sin_table):
    half_dim = values.shape[-1] // 2
    front_half = values[..., :half_dim]
    back_half = values[..., half_dim:]
    return jnp.concatenate(
        [
            front_half * cos_table - back_half * sin_table,
            back_half * cos_table + front_half * sin_table,
        ],
        axis=-1,
    )


def rope_tables(position, head_width):
    half_dim = head_width // 2
    frequency = jnp.exp(
        jnp.arange(half_dim, dtype=jnp.float32) * (-2.0 * math.log(rope_base) / head_width)
    )
    angles = position.astype(jnp.float32)[:, None] * frequency[None, :]
    return (jnp.cos(angles)[:, None, :], jnp.sin(angles)[:, None, :])


def sequence_layout(seq_lengths, row_ids):
    seq_index = jnp.arange(seq_lengths.shape[0], dtype=jnp.int32)
    up_to = (seq_index[None, :] <= seq_index[:, None]).astype(jnp.int32)
    seq_ends = jnp.sum(up_to * seq_lengths[None, :], axis=1)
    segment = jnp.sum((row_ids[:, None] >= seq_ends[None, :]).astype(jnp.int32), axis=1)
    seq_starts = seq_ends - seq_lengths
    picked = (
        segment[:, None] == jnp.arange(seq_lengths.shape[0], dtype=jnp.int32)[None, :]
    ).astype(jnp.int32)
    position = row_ids - jnp.sum(picked * seq_starts[None, :], axis=1)
    return (segment, position)


def embed_heads(projected):
    pieces = []
    column_start = 0
    for head_width in (PROJ_A, PROJ_B, PROJ_C):
        head_cols = projected[:, column_start : column_start + head_width]
        pieces.append(
            head_cols * lax.rsqrt(jnp.sum(head_cols * head_cols, axis=1, keepdims=True) + embed_eps)
        )
        column_start += head_width
    return jnp.concatenate(pieces, axis=1)


def contract(left, right, left_dim, right_dim):
    return lax.dot_general(
        left, right, (((left_dim,), (right_dim,)), ((), ())), preferred_element_type=jnp.float32
    )


def shards(
    layer_input,
    seq_lengths,
    deal_order,
    qkv_weight,
    qkv_bias,
    out_weight,
    out_bias,
    first_gain,
    first_shift,
    up_weight,
    up_bias,
    down_weight,
    down_bias,
    second_gain,
    second_shift,
    proj_weight,
    cot_output,
    cot_embed,
):
    own_rows = layer_input.shape[0]
    group_rows = own_rows * lax.axis_size("ctx")
    group_lengths = seq_lengths[0]
    local_source = deal_order % group_rows
    group_input, group_cot, group_cot_embed = (
        lax.all_gather(layer_input, "ctx", axis=0, tiled=True),
        lax.all_gather(cot_output, "ctx", axis=0, tiled=True),
        lax.all_gather(cot_embed, "ctx", axis=0, tiled=True),
    )
    packed = group_input[local_source]
    packed_cot = group_cot[local_source].astype(jnp.float32)
    packed_cot_embed = group_cot_embed[local_source].astype(jnp.float32)
    row_ids = lax.axis_index("ctx") * own_rows + jnp.arange(own_rows, dtype=jnp.int32)
    segment, position = sequence_layout(group_lengths, row_ids)
    (
        qkv_full,
        qkv_bias_full,
        out_full,
        out_bias_full,
        first_gain_full,
        first_shift_full,
        up_full,
        up_bias_full,
        down_full,
        down_bias_full,
        second_gain_full,
        second_shift_full,
        proj_full,
    ) = (
        lax.all_gather(qkv_weight, "fsdp", axis=0, tiled=True),
        lax.all_gather(qkv_bias, "fsdp", axis=1, tiled=True),
        lax.all_gather(out_weight, "fsdp", axis=0, tiled=True),
        lax.all_gather(out_bias, "fsdp", axis=0, tiled=True),
        lax.all_gather(first_gain, "fsdp", axis=0, tiled=True),
        lax.all_gather(first_shift, "fsdp", axis=0, tiled=True),
        lax.all_gather(up_weight, "fsdp", axis=0, tiled=True),
        lax.all_gather(up_bias, "fsdp", axis=0, tiled=True),
        lax.all_gather(down_weight, "fsdp", axis=0, tiled=True),
        lax.all_gather(down_bias, "fsdp", axis=0, tiled=True),
        lax.all_gather(second_gain, "fsdp", axis=0, tiled=True),
        lax.all_gather(second_shift, "fsdp", axis=0, tiled=True),
        lax.all_gather(proj_weight, "fsdp", axis=0, tiled=True),
    )
    local_width = qkv_full.shape[2]
    local_heads = local_width // HEAD_DIM
    score_scale = HEAD_DIM ** (-0.5)
    mixed = (
        jnp.einsum("td,dwe->twe", packed, qkv_full, preferred_element_type=jnp.float32)
        + qkv_bias_full.astype(jnp.float32)[None]
    )
    shaped = mixed.reshape(own_rows, 3, local_heads, HEAD_DIM)
    cos_table, sin_table = rope_tables(position, HEAD_DIM)

    def rope_pair(query_pre, key_pre):
        return (rotate(query_pre, cos_table, sin_table), rotate(key_pre, cos_table, sin_table))

    (query_rot, key_rot), rope_back = jax.vjp(rope_pair, shaped[:, 0], shaped[:, 1])
    query_heads = jnp.transpose(query_rot.astype(jnp.bfloat16), (1, 0, 2))
    key_low = key_rot.astype(jnp.bfloat16).reshape(own_rows, local_width)
    value_low = shaped[:, 2].astype(jnp.bfloat16).reshape(own_rows, local_width)

    def key_mask(count):
        key_segment = sequence_layout(group_lengths, jnp.arange(count, dtype=jnp.int32))[0]
        return segment[:, None] == key_segment[None, :]

    start_state = (
        jnp.full((local_heads, own_rows), masked_score, jnp.float32),
        jnp.zeros((local_heads, own_rows), jnp.float32),
        jnp.zeros((local_heads, own_rows, HEAD_DIM), jnp.float32),
    )
    key_piece = lax.all_gather(key_low, "ctx", axis=0, tiled=True)
    value_piece = lax.all_gather(value_low, "ctx", axis=0, tiled=True)
    count = key_piece.shape[0]
    same_seq = key_mask(count)
    key_heads = key_piece.reshape(count, local_heads, HEAD_DIM)
    value_heads = value_piece.reshape(count, local_heads, HEAD_DIM)

    def forward_one_head(head_args):
        head_index, run_top, run_total, run_acc = head_args
        scores = (
            jnp.einsum(
                "qd,kd->qk",
                query_heads[head_index],
                key_heads[:, head_index],
                preferred_element_type=jnp.float32,
            )
            * score_scale
        )
        scores = jnp.where(same_seq, scores, masked_score)
        new_top = jnp.maximum(run_top, jnp.max(scores, axis=1))
        scale_old = jnp.exp(run_top - new_top)
        weights = jnp.exp(scores - new_top[:, None])
        new_total = run_total * scale_old + jnp.sum(weights, axis=1)
        new_acc = run_acc * scale_old[:, None] + jnp.dot(
            weights.astype(jnp.bfloat16),
            value_heads[:, head_index],
            preferred_element_type=jnp.float32,
        )
        return (new_top, new_total, new_acc)

    run_top, run_total, run_acc = lax.map(
        forward_one_head, (jnp.arange(local_heads), start_state[0], start_state[1], start_state[2])
    )
    attended = run_acc / run_total[:, :, None]
    row_lse = run_top + jnp.log(run_total)
    attended_low = (
        jnp.transpose(attended, (1, 0, 2)).reshape(own_rows, local_width).astype(jnp.bfloat16)
    )
    branch = lax.psum(
        jnp.dot(attended_low, out_full, preferred_element_type=jnp.float32).astype(jnp.bfloat16),
        "tp",
    ).astype(jnp.float32)
    first_sum = packed.astype(jnp.float32) + branch + out_bias_full.astype(jnp.float32)
    normed, first_back = jax.vjp(
        layer_norm,
        first_sum,
        first_gain_full.astype(jnp.float32),
        first_shift_full.astype(jnp.float32),
    )
    normed_low = normed.astype(jnp.bfloat16)
    up_out = jnp.dot(normed_low, up_full, preferred_element_type=jnp.float32) + up_bias_full.astype(
        jnp.float32
    )
    activated, gelu_back = jax.vjp(partial(jax.nn.gelu, approximate=False), up_out)
    activated_low = activated.astype(jnp.bfloat16)
    down_out = lax.psum(
        jnp.dot(activated_low, down_full, preferred_element_type=jnp.float32).astype(jnp.bfloat16),
        "tp",
    ).astype(jnp.float32)
    second_sum = normed + down_out + down_bias_full.astype(jnp.float32)
    final, second_back = jax.vjp(
        layer_norm,
        second_sum,
        second_gain_full.astype(jnp.float32),
        second_shift_full.astype(jnp.float32),
    )
    final_low = final.astype(jnp.bfloat16)
    projected = jnp.dot(final_low, proj_full, preferred_element_type=jnp.float32)
    embedded, embed_back = jax.vjp(embed_heads, projected)
    proj_low = embed_back(packed_cot_embed)[0].astype(jnp.bfloat16)
    proj_weight_grad = contract(final_low, proj_low, 0, 0)
    final_grad = packed_cot + contract(proj_low, proj_full, 1, 1)
    second_grad, second_gain_grad, second_shift_grad = second_back(final_grad)
    down_bias_grad = jnp.sum(second_grad, axis=0)
    down_low = second_grad.astype(jnp.bfloat16)
    down_weight_grad = contract(activated_low, down_low, 0, 0)
    up_grad = gelu_back(contract(down_low, down_full, 1, 1))[0]
    up_bias_grad = jnp.sum(up_grad, axis=0)
    up_low = up_grad.astype(jnp.bfloat16)
    up_weight_grad = contract(normed_low, up_low, 0, 0)
    normed_grad = second_grad + lax.psum(
        contract(up_low, up_full, 1, 1).astype(jnp.bfloat16), "tp"
    ).astype(jnp.float32)
    first_grad, first_gain_grad, first_shift_grad = first_back(normed_grad)
    out_bias_grad = jnp.sum(first_grad, axis=0)
    branch_low = first_grad.astype(jnp.bfloat16)
    out_weight_grad = contract(attended_low, branch_low, 0, 0)
    attended_grad = contract(branch_low, out_full, 1, 1).astype(jnp.bfloat16)
    grad_heads = jnp.transpose(attended_grad.reshape(own_rows, local_heads, HEAD_DIM), (1, 0, 2))
    row_delta = jnp.sum(grad_heads.astype(jnp.float32) * attended, axis=2)
    query_grad = jnp.zeros((local_heads, own_rows, HEAD_DIM), jnp.float32)
    key_piece = lax.all_gather(key_low, "ctx", axis=0, tiled=True)
    value_piece = lax.all_gather(value_low, "ctx", axis=0, tiled=True)
    count = key_piece.shape[0]
    backward_same_seq = key_mask(count)
    backward_key_heads = key_piece.reshape(count, local_heads, HEAD_DIM)
    backward_value_heads = value_piece.reshape(count, local_heads, HEAD_DIM)

    def backward_one_head(head_args):
        head_index, head_query_grad = head_args
        query_rows = query_heads[head_index]
        key_rows = backward_key_heads[:, head_index]
        value_rows = backward_value_heads[:, head_index]
        grad_rows = grad_heads[head_index]
        scores = (
            jnp.einsum("qd,kd->qk", query_rows, key_rows, preferred_element_type=jnp.float32)
            * score_scale
        )
        scores = jnp.where(backward_same_seq, scores, masked_score)
        row_probs = jnp.exp(scores - row_lse[head_index][:, None])
        value_grad = contract(row_probs.astype(jnp.bfloat16), grad_rows, 0, 0)
        prob_grad = contract(grad_rows, value_rows, 1, 1)
        score_grad = (row_probs * (prob_grad - row_delta[head_index][:, None])).astype(jnp.bfloat16)
        new_query_grad = head_query_grad + score_scale * jnp.dot(
            score_grad, key_rows, preferred_element_type=jnp.float32
        )
        key_grad = score_scale * contract(score_grad, query_rows, 0, 0)
        return (new_query_grad, key_grad, value_grad)

    new_query_grad, key_grads, value_grads = lax.map(
        backward_one_head, (jnp.arange(local_heads), query_grad)
    )
    key_rows_grad = jnp.transpose(key_grads, (1, 0, 2)).reshape(count, local_width)
    value_rows_grad = jnp.transpose(value_grads, (1, 0, 2)).reshape(count, local_width)
    key_grad_all = key_rows_grad
    value_grad_all = value_rows_grad
    query_grad, key_grad_all, value_grad_all = (new_query_grad, key_grad_all, value_grad_all)
    key_grad, value_grad = (
        lax.psum_scatter(
            key_grad_all.astype(jnp.bfloat16), "ctx", scatter_dimension=0, tiled=True
        ).astype(jnp.float32),
        lax.psum_scatter(
            value_grad_all.astype(jnp.bfloat16), "ctx", scatter_dimension=0, tiled=True
        ).astype(jnp.float32),
    )
    query_pre_grad, key_pre_grad = rope_back(
        (jnp.transpose(query_grad, (1, 0, 2)), key_grad.reshape(own_rows, local_heads, HEAD_DIM))
    )
    mixed_grad = jnp.stack(
        [query_pre_grad, key_pre_grad, value_grad.reshape(own_rows, local_heads, HEAD_DIM)], axis=1
    ).reshape(own_rows, 3, local_width)
    qkv_bias_grad = jnp.sum(mixed_grad, axis=0)
    mixed_low = mixed_grad.astype(jnp.bfloat16)
    qkv_weight_grad = jnp.einsum(
        "td,twe->dwe", packed, mixed_low, preferred_element_type=jnp.float32
    )
    input_grad = first_grad + lax.psum(
        jnp.einsum("twe,dwe->td", mixed_low, qkv_full, preferred_element_type=jnp.float32).astype(
            jnp.bfloat16
        ),
        "tp",
    ).astype(jnp.float32)
    embedded_low = embedded.astype(jnp.bfloat16)
    input_grad_low = input_grad.astype(jnp.bfloat16)
    group_order = lax.all_gather(deal_order, "ctx", axis=0, tiled=True) % group_rows
    inverse_order = (
        jnp.zeros((group_rows,), jnp.int32)
        .at[group_order]
        .set(jnp.arange(group_rows, dtype=jnp.int32))
    )
    chosen_rows = inverse_order[row_ids]
    rows_output, rows_embed, rows_grad = (
        lax.all_gather(final_low, "ctx", axis=0, tiled=True),
        lax.all_gather(embedded_low, "ctx", axis=0, tiled=True),
        lax.all_gather(input_grad_low, "ctx", axis=0, tiled=True),
    )
    ordered_output = rows_output[chosen_rows]
    ordered_embed = rows_embed[chosen_rows]
    ordered_grad = rows_grad[chosen_rows]
    (
        qkv_weight_grad,
        qkv_bias_grad,
        out_weight_grad,
        out_bias_grad,
        first_gain_grad,
        first_shift_grad,
        up_weight_grad,
        up_bias_grad,
        down_weight_grad,
        down_bias_grad,
        second_gain_grad,
        second_shift_grad,
        proj_weight_grad,
    ) = (
        lax.psum_scatter(
            qkv_weight_grad.astype(jnp.bfloat16), "fsdp", scatter_dimension=0, tiled=True
        ).astype(jnp.float32),
        lax.psum_scatter(
            qkv_bias_grad.astype(jnp.bfloat16), "fsdp", scatter_dimension=1, tiled=True
        ).astype(jnp.float32),
        lax.psum_scatter(
            out_weight_grad.astype(jnp.bfloat16), "fsdp", scatter_dimension=0, tiled=True
        ).astype(jnp.float32),
        lax.psum_scatter(
            out_bias_grad.astype(jnp.bfloat16), "fsdp", scatter_dimension=0, tiled=True
        ).astype(jnp.float32),
        lax.psum_scatter(
            first_gain_grad.astype(jnp.bfloat16), "fsdp", scatter_dimension=0, tiled=True
        ).astype(jnp.float32),
        lax.psum_scatter(
            first_shift_grad.astype(jnp.bfloat16), "fsdp", scatter_dimension=0, tiled=True
        ).astype(jnp.float32),
        lax.psum_scatter(
            up_weight_grad.astype(jnp.bfloat16), "fsdp", scatter_dimension=0, tiled=True
        ).astype(jnp.float32),
        lax.psum_scatter(
            up_bias_grad.astype(jnp.bfloat16), "fsdp", scatter_dimension=0, tiled=True
        ).astype(jnp.float32),
        lax.psum_scatter(
            down_weight_grad.astype(jnp.bfloat16), "fsdp", scatter_dimension=0, tiled=True
        ).astype(jnp.float32),
        lax.psum_scatter(
            down_bias_grad.astype(jnp.bfloat16), "fsdp", scatter_dimension=0, tiled=True
        ).astype(jnp.float32),
        lax.psum_scatter(
            second_gain_grad.astype(jnp.bfloat16), "fsdp", scatter_dimension=0, tiled=True
        ).astype(jnp.float32),
        lax.psum_scatter(
            second_shift_grad.astype(jnp.bfloat16), "fsdp", scatter_dimension=0, tiled=True
        ).astype(jnp.float32),
        lax.psum_scatter(
            proj_weight_grad.astype(jnp.bfloat16), "fsdp", scatter_dimension=0, tiled=True
        ).astype(jnp.float32),
    )
    (
        qkv_weight_grad,
        qkv_bias_grad,
        out_weight_grad,
        out_bias_grad,
        first_gain_grad,
        first_shift_grad,
        up_weight_grad,
        up_bias_grad,
        down_weight_grad,
        down_bias_grad,
        second_gain_grad,
        second_shift_grad,
        proj_weight_grad,
    ) = (
        lax.psum(qkv_weight_grad.astype(jnp.bfloat16), "ctx").astype(jnp.float32),
        lax.psum(qkv_bias_grad.astype(jnp.bfloat16), "ctx").astype(jnp.float32),
        lax.psum(out_weight_grad.astype(jnp.bfloat16), "ctx").astype(jnp.float32),
        lax.psum(out_bias_grad.astype(jnp.bfloat16), "ctx").astype(jnp.float32),
        lax.psum(first_gain_grad.astype(jnp.bfloat16), "ctx").astype(jnp.float32),
        lax.psum(first_shift_grad.astype(jnp.bfloat16), "ctx").astype(jnp.float32),
        lax.psum(up_weight_grad.astype(jnp.bfloat16), "ctx").astype(jnp.float32),
        lax.psum(up_bias_grad.astype(jnp.bfloat16), "ctx").astype(jnp.float32),
        lax.psum(down_weight_grad.astype(jnp.bfloat16), "ctx").astype(jnp.float32),
        lax.psum(down_bias_grad.astype(jnp.bfloat16), "ctx").astype(jnp.float32),
        lax.psum(second_gain_grad.astype(jnp.bfloat16), "ctx").astype(jnp.float32),
        lax.psum(second_shift_grad.astype(jnp.bfloat16), "ctx").astype(jnp.float32),
        lax.psum(proj_weight_grad.astype(jnp.bfloat16), "ctx").astype(jnp.float32),
    )
    return (
        ordered_output,
        ordered_embed,
        ordered_grad,
        qkv_weight_grad,
        qkv_bias_grad,
        out_weight_grad,
        out_bias_grad,
        first_gain_grad,
        first_shift_grad,
        up_weight_grad,
        up_bias_grad,
        down_weight_grad,
        down_bias_grad,
        second_gain_grad,
        second_shift_grad,
        proj_weight_grad,
    )


def solution(mesh):
    placed = (
        P(("fsdp", "ctx"), None),
        P("fsdp", None),
        P(("fsdp", "ctx")),
        P("fsdp", None, "tp"),
        P(None, ("tp", "fsdp")),
        P(("tp", "fsdp"), None),
        P("fsdp"),
        P("fsdp"),
        P("fsdp"),
        P("fsdp", "tp"),
        P(("tp", "fsdp")),
        P(("tp", "fsdp"), None),
        P("fsdp"),
        P("fsdp"),
        P("fsdp"),
        P("fsdp", None),
        P(("fsdp", "ctx"), None),
        P(("fsdp", "ctx"), None),
    )
    return jax.shard_map(
        shards,
        mesh=mesh,
        in_specs=placed,
        out_specs=(
            P(("fsdp", "ctx"), None),
            P(("fsdp", "ctx"), None),
            P(("fsdp", "ctx"), None),
            P("fsdp", None, "tp"),
            P(None, ("tp", "fsdp")),
            P(("tp", "fsdp"), None),
            P("fsdp"),
            P("fsdp"),
            P("fsdp"),
            P("fsdp", "tp"),
            P(("tp", "fsdp")),
            P(("tp", "fsdp"), None),
            P("fsdp"),
            P("fsdp"),
            P("fsdp"),
            P("fsdp", None),
        ),
        check_vma=False,
    )
```

```python
import math
from functools import partial
import jax, jax.numpy as jnp
from jax import lax
from jax.experimental import pallas as pl
from jax.experimental.pallas import tpu as pltpu
from jax.sharding import Mesh
from jax.sharding import PartitionSpec as P

f32, bf16 = jnp.float32, jnp.bfloat16
HEAD_DIM = 64
VMEM_CAP = 56 * 1024 * 1024
MASKED = -1e30
TS = 256
FQ, FK = 1024, 512
BQ, BK = 512, 512


def nt(a, b):
    return lax.dot_general(a, b, (((1,), (1,)), ((), ())), preferred_element_type=f32)


def nn(a, b):
    return lax.dot_general(a, b, (((1,), (0,)), ((), ())), preferred_element_type=f32)


def run(kernel, out_shape, name, scalars=0, scratch=(), flops=2_000_000_000):
    def call(*args):
        vm = pl.BlockSpec(memory_space=pltpu.VMEM)
        sm = pl.BlockSpec(memory_space=pltpu.SMEM)
        outs = jax.tree.map(lambda _: vm, out_shape)
        return pl.pallas_call(
            kernel, out_shape=out_shape,
            in_specs=[sm] * scalars + [vm] * (len(args) - scalars), out_specs=outs,
            scratch_shapes=list(scratch),
            compiler_params=pltpu.CompilerParams(vmem_limit_bytes=VMEM_CAP),
            cost_estimate=pl.CostEstimate(flops=flops, transcendentals=0, bytes_accessed=8_000_000),
            name=name)(*args)
    return call


def one_hot(rank_ref, tile, start, width):
    want = lax.broadcasted_iota(jnp.int32, (TS, width), 0) + tile * TS
    return jnp.where(rank_ref[:, pl.ds(start, width)] == want, 1.0, 0.0).astype(bf16)


def key_span(start, size, first_len, tile, total):
    lo = jnp.where(start >= first_len, first_len // tile, 0)
    hi = jnp.where(start + size <= first_len, (first_len + tile - 1) // tile, total // tile)
    return lo, hi


def code_lanes(base, rows, first_len):
    row = lax.broadcasted_iota(jnp.int32, (rows, 128), 0) + base
    lane = lax.broadcasted_iota(jnp.int32, (rows, 128), 1)
    bad = jnp.where(row < first_len, 1, 0)
    return jnp.where(lane == bad, MASKED, jnp.where((lane >= 2) & (lane < 5), 1.0, 0.0)).astype(bf16)


def code_rows(base, cols, first_len):
    row = lax.broadcasted_iota(jnp.int32, (128, cols), 0)
    col = lax.broadcasted_iota(jnp.int32, (128, cols), 1) + base
    return (jnp.where(row == jnp.where(col < first_len, 0, 1), 1.0, 0.0), row)


def head_rows(values, head):
    row = lax.broadcasted_iota(jnp.int32, values.shape, 0)
    return jnp.where((row // HEAD_DIM) == head, values, 0.0)


def head_lanes(values, head):
    lane = lax.broadcasted_iota(jnp.int32, values.shape, 1)
    return jnp.where((lane // HEAD_DIM) == head, values, 0.0)


def forward_kernel(len_ref, meet_ref, dest_ref, rank_ref, near_ref, far_ref, att_ref, sorted_ref, att_t_ref, lse_ref,
                   k_ext, q_ext, arr_t):
    rows = rank_ref.shape[1]
    block = rows // 4
    first_len = len_ref[0]
    scale = HEAD_DIM ** -0.5

    def sort_tile(tile, carry):
        at = pl.multiple_of(tile * TS, TS)
        arr_t[:, pl.ds(0, TS)] = jnp.zeros((384, TS), f32)
        for d in range(4):
            @pl.when(meet_ref[tile * 4 + d] > 0)
            def _():
                hot = one_hot(rank_ref, tile, d * block, block)
                mixed_ref = near_ref if d < 2 else far_ref
                arr_t[:, pl.ds(0, TS)] += nt(mixed_ref[:, pl.ds((d % 2) * block, block)], hot)
        low = arr_t[:, pl.ds(0, TS)].astype(bf16)
        sorted_ref[:, pl.ds(at, TS)] = low
        wide = low.astype(f32)
        query = wide[0:128] * scale
        code, _ = code_rows(at, TS, first_len)
        for h in range(2):
            q_ext[h, 0:128, pl.ds(at, TS)] = head_rows(query, h).astype(bf16)
            q_ext[h, 128:256, pl.ds(at, TS)] = code.astype(bf16)
        k_ext[pl.ds(at, TS), 0:128] = wide[128:256].T.astype(bf16)
        k_ext[pl.ds(at, TS), 128:256] = code_lanes(at, TS, first_len)
        return carry

    lax.fori_loop(0, rows // TS, sort_tile, 0)

    def query_tile(i, carry):
        at = pl.multiple_of(i * FQ, FQ)
        lo, hi = key_span(at, FQ, first_len, FK, rows)

        def key_tile(j, state):
            kat = pl.multiple_of(j * FK, FK)
            keys = k_ext[pl.ds(kat, FK), :]
            out = []
            for h in range(2):
                top, total, acc = state[h]
                scores = nn(keys, q_ext[h, :, pl.ds(at, FQ)])
                new_top = jnp.maximum(top, jnp.max(scores, axis=0, keepdims=True))
                fade = jnp.exp(top - new_top)
                weights = jnp.exp(scores - new_top)
                total = total * fade + jnp.sum(weights, axis=0, keepdims=True)
                value = sorted_ref[256 + h * 64:320 + h * 64, pl.ds(kat, FK)]
                acc = acc * fade + nn(value, weights.astype(bf16))
                out.append((new_top, total, acc))
            return tuple(out)

        start = (jnp.full((1, FQ), MASKED, f32), jnp.zeros((1, FQ), f32), jnp.zeros((64, FQ), f32))
        state = lax.fori_loop(lo, hi, key_tile, (start, start))
        lse_rows = []
        for h in range(2):
            top, total, acc = state[h]
            att_t_ref[h * 64:(h + 1) * 64, pl.ds(at, FQ)] = (acc / total).astype(bf16)
            lse_ref[h:h + 1, pl.ds(at, FQ)] = top + jnp.log(total)
        return carry

    lax.fori_loop(0, rows // FQ, query_tile, 0)

    for d in range(4):
        arr_t[0:128, :] = jnp.zeros((128, block), f32)

        def back_tile(tile, carry):
            @pl.when(meet_ref[tile * 4 + d] > 0)
            def _():
                at = pl.multiple_of(tile * TS, TS)
                hot = one_hot(rank_ref, tile, d * block, block)
                arr_t[0:128, :] += nn(att_t_ref[:, pl.ds(at, TS)], hot)
            return carry

        lax.fori_loop(0, rows // TS, back_tile, 0)
        low = arr_t[0:128, :].T.astype(bf16)
        att_ref[dest_ref[2 * d]] = low[:block // 2]
        att_ref[dest_ref[2 * d + 1]] = low[block // 2:]


def attention_forward(first_len, meet, dest, rank, near, far):
    rows = rank.shape[1]
    return pl.pallas_call(
        forward_kernel,
        out_shape=(
            jax.ShapeDtypeStruct((8, rows // 8, 128), bf16),
            jax.ShapeDtypeStruct((384, rows), bf16),
            jax.ShapeDtypeStruct((128, rows), bf16),
            jax.ShapeDtypeStruct((8, rows), f32),
        ),
        in_specs=[
            pl.BlockSpec(memory_space=pltpu.SMEM),
            pl.BlockSpec(memory_space=pltpu.SMEM),
            pl.BlockSpec(memory_space=pltpu.SMEM),
            pl.BlockSpec(memory_space=pltpu.VMEM),
            pl.BlockSpec(memory_space=pltpu.VMEM),
            pl.BlockSpec(memory_space=pltpu.VMEM),
        ],
        out_specs=tuple(pl.BlockSpec(memory_space=pltpu.VMEM) for _ in range(4)),
        scratch_shapes=[
            pltpu.VMEM((rows, 256), bf16),
            pltpu.VMEM((2, 256, rows), bf16),
            pltpu.VMEM((384, rows // 4), f32),
        ],
        compiler_params=pltpu.CompilerParams(vmem_limit_bytes=VMEM_CAP),
        cost_estimate=pl.CostEstimate(flops=60_000_000_000, transcendentals=16_000_000, bytes_accessed=16_000_000),
        name="attention_forward",
    )(first_len, meet, dest, rank, near, far)


def split3(v):
    hi = v.astype(bf16).astype(f32)
    mid = (v - hi).astype(bf16).astype(f32)
    return hi, mid, v - hi - mid


def backward_kernel(len_ref, meet_ref, dest_ref, rank_ref, sorted_ref, att_t_ref, lse_ref, cos_ref, sin_ref,
                    grad_ref, *refs):
    (out_ref, bias_ref, k_ext, q_ext, v_ext, g_ext, q_nat, g_nat, dq_t, arr_t, ds_low) = refs
    rows = rank_ref.shape[1]
    block = rows // 4
    first_len = len_ref[0]
    scale = HEAD_DIM ** -0.5

    def sort_tile(tile, carry):
        at = pl.multiple_of(tile * TS, TS)
        q_t = sorted_ref[0:128, pl.ds(at, TS)].astype(f32) * scale
        k_ext[pl.ds(at, TS), 0:128] = sorted_ref[128:256, pl.ds(at, TS)].astype(f32).T.astype(bf16)
        k_ext[pl.ds(at, TS), 128:256] = code_lanes(at, TS, first_len)
        v_ext[pl.ds(at, TS), 0:128] = sorted_ref[256:384, pl.ds(at, TS)].astype(f32).T.astype(bf16)
        v_ext[pl.ds(at, TS), 128:256] = code_lanes(at, TS, first_len)
        arr_t[0:TS, 0:128] = jnp.zeros((TS, 128), f32)
        for d in range(4):
            @pl.when(meet_ref[tile * 4 + d] > 0)
            def _():
                hot = one_hot(rank_ref, tile, d * block, block)
                half = block // 2
                arr_t[0:TS, 0:128] += (nn(hot[:, :half], grad_ref[dest_ref[2 * d]])
                                       + nn(hot[:, half:], grad_ref[dest_ref[2 * d + 1]]))
        grad = arr_t[0:TS, 0:128]
        grad_t = grad.T
        q = q_t.T
        code, row = code_rows(at, TS, first_len)
        prod = grad_t * att_t_ref[:, pl.ds(at, TS)].astype(f32)
        for h in range(2):
            delta = jnp.sum(prod[h * 64:(h + 1) * 64], axis=0, keepdims=True)
            lse = lse_ref[h:h + 1, pl.ds(at, TS)]
            l0, l1, l2 = split3(-lse)
            d0, d1, d2 = split3(-delta)
            q_ext[h, 0:128, pl.ds(at, TS)] = head_rows(q_t, h).astype(bf16)
            q_ext[h, 128:256, pl.ds(at, TS)] = jnp.where(
                row == 2, l0, jnp.where(row == 3, l1, jnp.where(row == 4, l2, code))).astype(bf16)
            g_ext[h, 0:128, pl.ds(at, TS)] = head_rows(grad_t, h).astype(bf16)
            g_ext[h, 128:256, pl.ds(at, TS)] = jnp.where(
                row == 2, d0, jnp.where(row == 3, d1, jnp.where(row == 4, d2, 0.0))).astype(bf16)
            q_nat[h, pl.ds(at, TS), :] = head_lanes(q, h).astype(bf16)
            g_nat[h, pl.ds(at, TS), :] = head_lanes(grad, h).astype(bf16)
        return carry

    lax.fori_loop(0, rows // TS, sort_tile, 0)
    dq_t[...] = jnp.zeros(dq_t.shape, f32)

    def key_tile(j, carry):
        kat = pl.multiple_of(j * BK, BK)
        lo, hi = key_span(kat, BK, first_len, BQ, rows)

        def query_tile(i, state):
            dk, dv = state
            at = pl.multiple_of(i * BQ, BQ)
            keys = k_ext[pl.ds(kat, BK), :]
            values = v_ext[pl.ds(kat, BK), :]
            for h in range(2):
                probs = jnp.exp(nn(keys, q_ext[h, :, pl.ds(at, BQ)]))
                dprob = nn(values, g_ext[h, :, pl.ds(at, BQ)])
                dscore = (probs * dprob).astype(bf16)
                dv = dv + nn(probs.astype(bf16), g_nat[h, pl.ds(at, BQ), :])
                dk = dk + nn(dscore, q_nat[h, pl.ds(at, BQ), :])
                dq_t[h * 64:(h + 1) * 64, pl.ds(at, BQ)] += nn(
                    sorted_ref[128 + h * 64:192 + h * 64, pl.ds(kat, BK)], dscore)
            return dk, dv

        zero = jnp.zeros((BK, 128), f32)
        dk, dv = lax.fori_loop(lo, hi, query_tile, (zero, zero))
        ds_low[128:256, pl.ds(kat, BK)] = dk.T.astype(bf16)
        ds_low[256:384, pl.ds(kat, BK)] = dv.T.astype(bf16)
        return carry

    lax.fori_loop(0, rows // BK, key_tile, 0)
    ds_low[0:128, :] = (dq_t[...] * scale).astype(bf16)
    bias = jnp.zeros((384, 1), f32)
    for d in range(4):
        arr_t[...] = jnp.zeros((384, block), f32)

        def back_tile(tile, carry):
            @pl.when(meet_ref[tile * 4 + d] > 0)
            def _():
                at = pl.multiple_of(tile * TS, TS)
                hot = one_hot(rank_ref, tile, d * block, block)
                arr_t[...] += nn(ds_low[:, pl.ds(at, TS)], hot)
            return carry

        lax.fori_loop(0, rows // TS, back_tile, 0)
        cos, sin = cos_ref[:, pl.ds(d * block, block)], sin_ref[:, pl.ds(d * block, block)]
        for base in (0, 64, 128, 192):
            front, back = arr_t[base:base + 32, :], arr_t[base + 32:base + 64, :]
            arr_t[base:base + 32, :] = front * cos + back * sin
            arr_t[base + 32:base + 64, :] = back * cos - front * sin
        bias = bias + jnp.sum(arr_t[...], axis=1, keepdims=True)
        out_ref[dest_ref[2 * d]] = arr_t[:, 0:block // 2].astype(bf16)
        out_ref[dest_ref[2 * d + 1]] = arr_t[:, block // 2:block].astype(bf16)
    bias_ref[...] = bias


def attention_backward(first_len, meet, dest, rank, sorted_t, att_t, lse, cos_t, sin_t, grad):
    rows = rank.shape[1]
    vm = pl.BlockSpec(memory_space=pltpu.VMEM)
    sm = pl.BlockSpec(memory_space=pltpu.SMEM)
    return pl.pallas_call(
        backward_kernel,
        out_shape=(
            jax.ShapeDtypeStruct((8, 384, rows // 8), bf16),
            jax.ShapeDtypeStruct((384, 1), f32),
        ),
        in_specs=[sm, sm, sm] + [vm] * 7,
        out_specs=(vm, vm),
        scratch_shapes=[
            pltpu.VMEM((rows, 256), bf16),
            pltpu.VMEM((2, 256, rows), bf16),
            pltpu.VMEM((rows, 256), bf16),
            pltpu.VMEM((2, 256, rows), bf16),
            pltpu.VMEM((2, rows, 128), bf16),
            pltpu.VMEM((2, rows, 128), bf16),
            pltpu.VMEM((128, rows), f32),
            pltpu.VMEM((384, rows // 4), f32),
            pltpu.VMEM((384, rows), bf16),
        ],
        compiler_params=pltpu.CompilerParams(vmem_limit_bytes=VMEM_CAP),
        cost_estimate=pl.CostEstimate(flops=90_000_000_000, transcendentals=16_000_000, bytes_accessed=16_000_000),
        name="attention_backward",
    )(first_len, meet, dest, rank, sorted_t, att_t, lse, cos_t, sin_t, grad)


def qkv_kernel(ctx_ref, cos_ref, sin_ref, w_ref, *refs):
    out_ref = refs[-1]
    size, _, lanes = w_ref.shape
    bias = jnp.zeros((1, 384), f32)
    for f in range(size):
        bias_row = jnp.concatenate(
            [w_ref[f, 384 + i:385 + i, :].astype(f32) for i in range(-(-384 // lanes))], axis=1)[:, :384]
        bias = jnp.where(ctx_ref[0] == f, bias_row, bias) if size == 4 else jnp.where(f == 0, bias_row, bias)
    bias = jnp.broadcast_to(bias, (128, 384)).T[:, 0:1]
    start = 0
    for x_ref in refs[:-1]:
        count = x_ref.shape[0]
        span = slice(start, start + count)
        mixed = jnp.broadcast_to(bias, (384, count))
        for f in range(size):
            mixed = mixed + nt(w_ref[f, 0:384], x_ref[:, f * lanes:(f + 1) * lanes])
        cos, sin = cos_ref[:, span], sin_ref[:, span]
        for base in (0, 64, 128, 192):
            front, back = mixed[base:base + 32], mixed[base + 32:base + 64]
            out_ref[base:base + 32, span] = (front * cos - back * sin).astype(bf16)
            out_ref[base + 32:base + 64, span] = (back * cos + front * sin).astype(bf16)
        out_ref[256:384, span] = mixed[256:384].astype(bf16)
        start += count


def qkv_rope(ctx, pieces, weights, cos_t, sin_t):
    rows = sum(p.shape[0] for p in pieces)
    return run(qkv_kernel, jax.ShapeDtypeStruct((384, rows), bf16), "qkv_rope", 1)(
        ctx, cos_t, sin_t, weights, *pieces)


def row_places(order, packed, lengths, arrival):
    rows = order.shape[0]
    first_len = lengths[0]
    place = jnp.sum(
        jnp.where(order[:, None] == arrival[None, :], packed[:, None], 0), axis=0)
    in_first = place < first_len
    position = jnp.where(in_first, place, place - first_len)
    flags = in_first.astype(f32).reshape(rows // 128, 128)
    before = jnp.arange(128)[:, None] < jnp.arange(128)[None, :]
    within = jnp.dot(flags.astype(bf16), before.astype(bf16), preferred_element_type=f32)
    sums = jnp.sum(flags, axis=1)
    n = rows // 128
    earlier = jnp.arange(n)[None, :] < jnp.arange(n)[:, None]
    offset = jnp.sum(jnp.where(earlier, sums[None, :], 0.0), axis=1)
    firsts = (within + offset[:, None]).reshape(rows).astype(jnp.int32)
    index = jnp.arange(rows, dtype=jnp.int32)
    rank = jnp.where(in_first, firsts, first_len + index - firsts)
    counts = jnp.sum(in_first.astype(jnp.int32).reshape(4, rows // 4), axis=1)
    d = jnp.arange(4)
    lo0 = jnp.sum(jnp.where(d[None, :] < d[:, None], counts[None, :], 0), axis=1)
    hi0 = lo0 + counts
    lo1 = first_len + d * (rows // 4) - lo0
    hi1 = lo1 + rows // 4 - counts
    t0 = jnp.arange(rows // TS)[:, None] * TS
    t1 = t0 + TS
    meet = (((lo0[None] < t1) & (hi0[None] > t0) & (hi0 > lo0)[None])
            | ((lo1[None] < t1) & (hi1[None] > t0) & (hi1 > lo1)[None])).astype(jnp.int32)
    return position, rank, meet.reshape(-1)


def rope_tables_t(position):
    frequency = jnp.exp(jnp.arange(32, dtype=f32) * (-2.0 * math.log(10000.0) / 64))
    angles = frequency[:, None] * position.astype(f32)[None, :]
    return jnp.cos(angles), jnp.sin(angles)


norm_eps = 1e-05
embed_eps = 1e-06
WIDTHS = (128, 96, 64)
CT = ("cx", "core", "tp")
CTX = ("cx", "core")


def tn(a, b):
    return lax.dot_general(a, b, (((0,), (0,)), ((), ())), preferred_element_type=f32)


def head_rows_of(device):
    return ((device & 1) * 4 + (device >> 1)) * 128


def row_mean(v):
    return jnp.mean(v, axis=1, keepdims=True)


def norm_parts(v):
    centred = v - row_mean(v)
    rstd = lax.rsqrt(row_mean(centred * centred) + norm_eps)
    return centred * rstd, rstd


def norm_back(grad, x_hat, rstd, gain):
    e = grad * gain
    return (e - row_mean(e) - x_hat * row_mean(e * x_hat)) * rstd


def col_sum(v):
    return jnp.sum(v, axis=0, keepdims=True)


def out_proj_kernel(w_ref, x_ref, att_ref, bias_ref, gain_ref, shift_ref,
                    normed_ref, hat_ref, rstd_ref, low_ref):
    acc = x_ref[...].astype(f32) + bias_ref[...]
    for j in range(8):
        at = head_rows_of(j)
        acc = acc + nn(att_ref[j], w_ref[at:at + 128, 0:acc.shape[1]])
    x_hat, rstd = norm_parts(acc)
    normed = x_hat * gain_ref[...] + shift_ref[...]
    normed_ref[...] = normed
    hat_ref[...] = x_hat
    rstd_ref[...] = rstd
    low_ref[...] = normed.astype(bf16)


def hidden_refs(refs):
    first = refs[3].shape[0]
    return [(lambda f, r=r: (r, f)) for r in refs[0:3]] + [
        lambda f: (refs[3], f) if f < first else (refs[4], f - first)]


def up_rows(block, f, shard):
    ref, i = block(f)
    return ref[i, 0:shard]


def down_rows(block, group, strip, shard, side):
    parts = []
    for f in group:
        ref, i = block(f)
        at = shard + side * strip
        parts.append(ref[i, at:at + strip])
    return jnp.concatenate(parts, axis=0) if len(parts) > 1 else parts[0]


def hidden_sizes(refs, width):
    size, _, units = refs[0].shape
    strip = units // size
    step = max(1, 256 // strip)
    groups = [range(g, g + step) for g in range(0, size, step)]
    return size, units, strip, width // size, width // units, groups


def mlp_kernel(own_ref, peer_ref, bias_ref, *refs):
    act_ref, slope_ref, own_out, peer_out = refs[5:]
    half, width = own_ref.shape
    size, units, strip, shard, sides, groups = hidden_sizes(refs, width)
    blocks = hidden_refs(refs)
    for r, x_ref in enumerate((own_ref, peer_ref)):
        rows = slice(r * half, (r + 1) * half)
        out = [jnp.zeros((half, units), f32) for _ in range(sides)]
        for v in range(4):
            cols = slice(v * units, (v + 1) * units)
            up = jnp.broadcast_to(bias_ref[:, cols], (half, units))
            for f in range(size):
                up = up + nn(x_ref[:, f * shard:(f + 1) * shard], up_rows(blocks[v], f, shard))
            phi_int = 0.5 * (1.0 + lax.erf(up * (0.5 ** 0.5)))
            density = jnp.exp(-0.5 * up * up) * ((2.0 * math.pi) ** -0.5)
            act = (up * phi_int).astype(bf16)
            act_ref[rows, cols] = act
            slope_ref[rows, cols] = (phi_int + up * density).astype(bf16)
            for g in groups:
                at = g[0] * strip
                part = act[:, at:at + len(g) * strip]
                for s in range(sides):
                    out[s] = out[s] + nn(part, down_rows(blocks[v], g, strip, shard, s))
        for s in range(sides):
            if r == 0:
                own_out[:, s * units:(s + 1) * units] = out[s]
            else:
                peer_out[:, s * units:(s + 1) * units] = out[s].astype(bf16)


def head_kernel(strip_rows, normed_ref, own_ref, recv_ref, bias_ref, gain_ref, shift_ref, dense_ref, cot_ref, cot_embed_ref,
                final_ref, embed_ref, grad_ref, low_ref, proj_grad_ref, vec_ref, proj_ref):
    width, emb = proj_ref.shape
    strip = strip_rows
    for f in range(width // (2 * strip)):
        for t in range(2):
            at = (f * 2 + t) * strip
            src = (t * (width // (2 * strip)) + f) * strip
            proj_ref[at:at + strip, :] = dense_ref[src:src + strip, width:width + emb]
    second = normed_ref[...] + own_ref[...] + recv_ref[...].astype(f32) + bias_ref[...]
    x_hat, rstd = norm_parts(second)
    final = (x_hat * gain_ref[...] + shift_ref[...]).astype(bf16)
    final_ref[...] = final
    projected = nn(final, proj_ref[...])
    cot = cot_embed_ref[...].astype(f32)
    col = lax.broadcasted_iota(jnp.int32, projected.shape, 1)
    embedded = jnp.zeros(projected.shape, f32)
    grad_proj = jnp.zeros(projected.shape, f32)
    start = 0
    for width in WIDTHS:
        here = (col >= start) & (col < start + width)
        part = jnp.where(here, projected, 0.0)
        r = lax.rsqrt(jnp.sum(part * part, axis=1, keepdims=True) + embed_eps)
        n = part * r
        along = jnp.sum(n * cot, axis=1, keepdims=True)
        embedded = embedded + n
        grad_proj = jnp.where(here, r * (cot - n * along), grad_proj)
        start += width
    embed_ref[...] = embedded.astype(bf16)
    proj_low = grad_proj.astype(bf16)
    proj_grad_ref[...] = tn(final, proj_low).astype(bf16)
    grad_final = cot_ref[...].astype(f32) + nt(proj_low, proj_ref[...])
    grad_second = norm_back(grad_final, x_hat, rstd, gain_ref[...])
    grad_ref[...] = grad_second
    low_ref[...] = grad_second.astype(bf16)
    vec_ref[...] = jnp.zeros(vec_ref.shape, f32)
    vec_ref[0:1] = col_sum(grad_final * x_hat)
    vec_ref[1:2] = col_sum(grad_final)
    vec_ref[2:3] = col_sum(grad_second)


def mlp_back_kernel(own_ref, peer_ref, slope_ref, *refs):
    g1_ref, bias_ref, own_out, peer_out = refs[5:]
    half, width = own_ref.shape
    size, units, strip, shard, sides, groups = hidden_sizes(refs, width)
    blocks = hidden_refs(refs)
    for r, g_ref in enumerate((own_ref, peer_ref)):
        rows = slice(r * half, (r + 1) * half)
        out = [jnp.zeros((half, shard), f32) for _ in range(size)]
        for v in range(4):
            for g in groups:
                at = v * units + g[0] * strip
                cols = slice(at, at + len(g) * strip)
                grad_up = nt(g_ref[:, 0:units], down_rows(blocks[v], g, strip, shard, 0))
                for s in range(1, sides):
                    grad_up = grad_up + nt(
                        g_ref[:, s * units:(s + 1) * units], down_rows(blocks[v], g, strip, shard, s))
                grad_up = grad_up * slope_ref[rows, cols].astype(f32)
                sums = col_sum(grad_up)
                bias_ref[:, cols] = sums if r == 0 else bias_ref[:, cols] + sums
                g1_ref[rows, cols] = grad_up.astype(bf16)
            g1 = g1_ref[rows, v * units:(v + 1) * units]
            for f in range(size):
                out[f] = out[f] + nt(g1, up_rows(blocks[v], f, shard))
        for f in range(size):
            if r == 0:
                own_out[:, f * shard:(f + 1) * shard] = out[f]
            else:
                peer_out[:, f * shard:(f + 1) * shard] = out[f].astype(bf16)


def mlp_weights_kernel(place_ref, own_n, peer_n, own_g, peer_g, act_ref, g1_ref, bias_ref, dense_ref, recv_ref,
                       up0, up1, up2, up3, down_ref):
    size, _, units = up0.shape
    strip, shard = down_ref.shape[2], own_n.shape[1] // size
    normed = jnp.concatenate([own_n[...], peer_n[...]], axis=0)
    g2 = jnp.concatenate([own_g[...], peer_g[...]], axis=0)
    for v, up_ref in enumerate((up0, up1, up2, up3)):
        q = place_ref[0] ^ v
        cols = slice(v * units, (v + 1) * units)
        up = tn(normed, g1_ref[:, cols]).astype(bf16)
        down = tn(act_ref[:, cols], g2).astype(bf16)
        bias = jnp.broadcast_to(bias_ref[:, cols], (16, units)).astype(bf16)
        for f in range(size):
            up_ref[f, 0:shard] = up[f * shard:(f + 1) * shard]
            up_ref[f, shard:shard + 16] = bias
            up_ref[f, shard + 16:] = (dense_ref[q, f].astype(f32) + recv_ref[q, f].astype(f32)).astype(bf16)
            down_ref[f, q] = down[f * strip:(f + 1) * strip]


def sum_kernel(index_ref, p0, p1, p2, p3, down_ref, up_out, *down_outs):
    size = up_out.shape[0]
    for f in range(size):
        total = p0[f].astype(f32) + p1[f].astype(f32) + p2[f].astype(f32) + p3[f].astype(f32)
        up_out[(f - index_ref[0] + size) % size] = total.astype(bf16)
    for v, out in enumerate(down_outs):
        total = down_ref[0, index_ref[1] ^ v].astype(f32)
        for f in range(1, size):
            total = total + down_ref[f, index_ref[1] ^ v].astype(f32)
        out[...] = total.astype(bf16)


def pick_kernel(index_ref, up_ref, down_ref, dense_ref, proj_ref, *refs):
    vecs, outs = refs[:7], refs[7:]
    place, core, tp = (index_ref[i] for i in range(3))
    strip = down_ref.shape[0] // 4
    shard, units = up_ref.shape[0], up_ref.shape[1] // 4
    for n in range(2):
        q = place ^ n
        for f in range(units // strip):
            at = pl.multiple_of((f * 4 + q) * strip, strip)
            outs[n][0:shard, f * strip:(f + 1) * strip] = up_ref[:, pl.ds(at, strip)]
        rows = pl.multiple_of(q * strip, strip)
        for s in range(down_ref.shape[1] // units):
            at = shard + s * strip
            outs[n][at:at + strip] = down_ref[pl.ds(rows, strip), s * units:(s + 1) * units]
    count, width = dense_ref.shape[0] // 2, dense_ref.shape[1]
    half = outs[2]
    half[0:count, 0:width] = dense_ref[pl.ds(pl.multiple_of(core * count, count), count), :]
    half[0:count, width:] = proj_ref[pl.ds(pl.multiple_of((tp * 2 + core) * count, count), count), :]
    lines, line = [], []
    for v in vecs:
        line.append(v[...].astype(f32))
        if sum(p.shape[1] for p in line) == width:
            lines.append(jnp.concatenate(line, axis=1))
            line = []
    block = jnp.concatenate(lines + [jnp.zeros((16 - len(lines), width), f32)], axis=0)
    half[count:count + 16, 0:width] = block.astype(bf16)
    half[count:count + 16, width:] = jnp.zeros((16, half.shape[1] - width), bf16)


def dense_natural_kernel(index_ref, own_ref, core_ref, out_ref, vec_ref, up_ref):
    core, place = (index_ref[i] for i in range(2))
    size, rows = own_ref.shape[0] // 2, own_ref.shape[1] - 16
    units = up_ref.shape[1] // 4
    strip, quarter = units // size, vec_ref.shape[1] // size
    for f in range(size):
        for t in range(2):
            own, other = own_ref[t * size + f, 0:rows], core_ref[t * size + f, 0:rows]
            for k in range(2):
                at = ((t * size + f) * 2 + k) * rows
                out_ref[at:at + rows, :] = jnp.where(core == k, own, other)
        vecs = own_ref[f, rows:rows + 16].astype(f32)
        far = own_ref[size + f, rows:rows + 16].astype(f32)
        cut = 4 * strip
        ups = jnp.where(core == 0, vecs[0:1, 0:cut], far[0:1, 0:cut])
        for i in range(6):
            r, c = divmod(cut + i * quarter, 4 * quarter)
            vec_ref[i:i + 1, f * quarter:(f + 1) * quarter] = vecs[r:r + 1, c:c + quarter]
        for v in range(4):
            picked = jnp.zeros((1, strip), f32)
            for q in range(4):
                picked = jnp.where((place ^ v) == q, ups[:, q * strip:(q + 1) * strip], picked)
            up_ref[:, v * units + f * strip:v * units + (f + 1) * strip] = picked


def hidden_join_kernel(part_ref, up_ref, down_ref):
    strip = down_ref.shape[0] // 4
    shard, units = up_ref.shape[0], part_ref.shape[2]
    for q in range(4):
        for f in range(units // strip):
            at = (f * 4 + q) * strip
            up_ref[:, at:at + strip] = part_ref[q, 0:shard, f * strip:(f + 1) * strip].astype(f32)
        for s in range(down_ref.shape[1] // units):
            at = shard + 16 + s * strip
            down_ref[q * strip:(q + 1) * strip, s * units:(s + 1) * units] = part_ref[q, at:at + strip].astype(f32)


def first_back_kernel(second_ref, own_ref, recv_ref, hat_ref, rstd_ref, gain_ref, w_ref,
                      grad_ref, low_ref, att_grad_ref, vec_ref):
    grad_normed = second_ref[...] + own_ref[...] + recv_ref[...].astype(f32)
    x_hat = hat_ref[...]
    grad_first = norm_back(grad_normed, x_hat, rstd_ref[...], gain_ref[...])
    grad_ref[...] = grad_first
    low = grad_first.astype(bf16)
    low_ref[...] = low
    for j in range(8):
        at = head_rows_of(j)
        att_grad_ref[j] = nt(low, w_ref[at:at + 128, 0:low.shape[1]]).astype(bf16)
    vec_ref[...] = jnp.zeros(vec_ref.shape, f32)
    vec_ref[0:1] = col_sum(grad_normed * x_hat)
    vec_ref[1:2] = col_sum(grad_normed)
    vec_ref[2:3] = col_sum(grad_first)


def out_weight_kernel(low_ref, att_ref, proj_grad_ref, vec2_ref, vec1_ref, out_ref):
    width = low_ref.shape[1]
    _, _, size, rows, cols = out_ref.shape
    shard = width // (2 * size)
    thin, tail_rows = shard // 4, shard // 8
    sides = width // cols

    def store(t, f, part, at, value):
        for s in range(sides):
            first = at * sides + s * value.shape[0]
            out_ref[part % 2, part // 2 * 2 + t, f, first:first + value.shape[0]] = value[:, s * cols:(s + 1) * cols]

    for j in range(8):
        grad = tn(att_ref[j], low_ref[...]).astype(bf16)
        for start in range(0, 128, thin):
            block, rest = divmod(head_rows_of(j) + start, shard)
            store(block // size, block % size, rest // thin, 0, grad[start:start + thin])
    vecs = jnp.concatenate([vec2_ref[0:3], vec1_ref[0:3], jnp.zeros((122, width), f32)], axis=0).T
    tail = jnp.concatenate([proj_grad_ref[...].astype(f32), vecs[:, 0:96]], axis=1).astype(bf16)
    for f in range(size):
        for t in range(2):
            part = tail[(f * 2 + t) * shard:(f * 2 + t + 1) * shard]
            for b in range(4):
                if b < 3:
                    value = jnp.concatenate(
                        [part[g * tail_rows:(g + 1) * tail_rows, b * 128:(b + 1) * 128] for g in range(8)], axis=1)
                else:
                    value = jnp.zeros((tail_rows, width), bf16)
                store(t, f, b, thin, value)


def qkv_weight_kernel(dest_ref, d_ref, bias_ref, *refs):
    out_ref = refs[-1]
    size, _, lanes = out_ref.shape
    acc = jnp.zeros((384, size * lanes), f32)
    start, part = 0, d_ref.shape[2]
    for x_ref in refs[:-1]:
        done = 0
        while done < x_ref.shape[0]:
            count = min(x_ref.shape[0] - done, part)
            u, at = start // part, start % part
            acc = acc + nn(d_ref[dest_ref[u], :, at:at + count], x_ref[done:done + count])
            start, done = start + count, done + count
    row = jnp.broadcast_to(bias_ref[...], (384, 128)).T[0:1]
    row = jnp.concatenate([row, jnp.zeros((1, max(0, -(-384 // lanes) * lanes - 384)), f32)], axis=1) if 384 % lanes else row
    count = row.shape[1] // lanes
    lines = [row[:, i * lanes:(i + 1) * lanes] for i in range(count)]
    block = jnp.concatenate(lines + [jnp.zeros((16 - count, lanes), f32)], axis=0).astype(bf16)
    for f in range(size):
        s = (f - dest_ref[8] + size) % size
        out_ref[s, 0:384] = acc[:, f * lanes:(f + 1) * lanes].astype(bf16)
        out_ref[s, 384:400] = block


def input_grad_kernel(dev_ref, first_ref, d_ref, *refs):
    out_ref = refs[-1]
    parts, _, lanes = refs[0].shape
    for f in range(parts):
        cols = slice(f * lanes, (f + 1) * lanes)
        acc = first_ref[:, cols]
        for n, w_ref in enumerate(refs[:-1]):
            mask = (0, 1, 4, 5, 2, 3, 6, 7)[n]
            acc = acc + tn(d_ref[dev_ref[0] ^ mask], w_ref[f, 0:384])
        out_ref[:, cols] = acc.astype(bf16)


def hop(value, u):
    return lax.ppermute(value, CT, [(i, i ^ u) for i in range(8)])


def hop_core(value):
    return lax.ppermute(value, "core", [(0, 1), (1, 0)])


def hop_x(value):
    return lax.ppermute(value, "cx", [(0, 1), (1, 0)])


def hop_y(value):
    return lax.ppermute(value, "tp", [(0, 1), (1, 0)])


def shift_z(value, count, size):
    return lax.ppermute(value, "fsdp", [(i, (i + count) % size) for i in range(size)])


def trade(value, axes):
    return lax.all_to_all(value, axes, 0, 0, tiled=True)


def gather(value, axes, count):
    return trade(jnp.broadcast_to(value[None], (count,) + value.shape), axes)


def add_all(parts):
    total = parts[0].astype(f32)
    for p in parts[1:]:
        total = total + p.astype(f32)
    return total.astype(bf16)


def collect_z(value):
    size = lax.axis_size("fsdp")
    if size > 4:
        return add_all(trade(value, "fsdp"))
    return add_all([value[0]] + [
        lax.ppermute(value[s], "fsdp", [(i, (i + s) % size) for i in range(size)]) for s in range(1, size)])


def around_ctx(value, ctx):
    far = hop_x(value)
    return by_xor([value, hop_core(value), far, hop_core(far)], ctx)


def by_xor(parts, own):
    stacked = jnp.stack(parts)
    return jnp.stack([lax.dynamic_index_in_dim(stacked, own ^ i, 0, keepdims=False) for i in range(len(parts))])


def pair_rows(own, peer, tp):
    return jnp.concatenate([jnp.where(tp == 0, own, peer), jnp.where(tp == 0, peer, own)], axis=0)


def shards(
    layer_input,
    seq_lengths,
    deal_order,
    qkv_weight,
    qkv_bias,
    out_weight,
    out_bias,
    first_gain,
    first_shift,
    up_weight,
    up_bias,
    down_weight,
    down_bias,
    second_gain,
    second_shift,
    proj_weight,
    cot_output,
    cot_embed,
):
    own_rows, width = layer_input.shape
    half = own_rows // 2
    rows = own_rows * 4
    fs, cx, core, tp = (lax.axis_index(n) for n in ("fsdp", "cx", "core", "tp"))
    size = lax.axis_size("fsdp")
    ctx = cx * 2 + core
    dev = ctx * 2 + tp
    dev_ref = dev.astype(jnp.int32).reshape(1)
    shape = jax.ShapeDtypeStruct

    def own_half(value, which):
        return lax.dynamic_slice_in_dim(value, which * half, half, axis=0)

    def after(value, *others):
        return lax.optimization_barrier((value,) + others)[0]

    place = cx * 2 + tp
    strip = down_weight.shape[0] // 4
    units = size * strip
    shard = up_weight.shape[0]
    place_ref = place.astype(jnp.int32).reshape(1)
    ctx_ref = ctx.astype(jnp.int32).reshape(1)
    sides = width // units
    hidden_rows = shard + sides * strip
    emb = proj_weight.shape[1]
    shard_rows = out_weight.shape[0]
    vectors = [up_bias, out_bias, first_gain, first_shift, down_bias, second_gain, second_shift]
    if size > 4:
        def hidden_block(q):
            wide = up_weight.reshape(shard, size, 4, strip)
            up = lax.dynamic_index_in_dim(wide, q, 2, keepdims=False).reshape(shard, units)
            down = lax.dynamic_slice_in_dim(down_weight, q * strip, strip, axis=0)
            return jnp.concatenate([up] + [down[:, s * units:(s + 1) * units] for s in range(sides)], axis=0)

        blocks = [hidden_block(place), hidden_block(place ^ 1)]
        half_rows = shard_rows // 2
        part = lax.dynamic_slice_in_dim(proj_weight, tp * shard_rows, shard_rows, axis=0)
        vec_block = jnp.concatenate(vectors).reshape(-1, 4 * shard)
        vec_block = jnp.pad(vec_block, ((0, 16 - vec_block.shape[0]), (0, width + emb - 4 * shard)))
        beside = jnp.concatenate([out_weight, part], axis=1)
        dense_half = jnp.concatenate(
            [lax.dynamic_slice_in_dim(beside, core * half_rows, half_rows, axis=0), vec_block], axis=0)
    else:
        *blocks, dense_half = run(
            pick_kernel, (shape((hidden_rows, units), bf16),) * 2 + (shape((shard_rows // 2 + 16, width + emb), bf16),),
            "pick", 1)(jnp.stack([place, core, tp]).astype(jnp.int32), up_weight, down_weight, out_weight, proj_weight,
                       *[v.reshape(1, -1) for v in vectors])

    lanes = shard
    own_qkv = lax.dynamic_slice_in_dim(qkv_weight, ctx * 128, 128, axis=2)
    own_qkv = jnp.transpose(own_qkv, (1, 2, 0)).reshape(384, lanes)
    spare = 16 * lanes
    if size == 4:
        bias_own = qkv_bias.reshape(-1)
    else:
        bias_all = lax.all_gather(qkv_bias, "fsdp", axis=1, tiled=True)
        bias_own = lax.dynamic_slice_in_dim(bias_all, ctx * 128, 128, axis=1).reshape(-1)
    bias_block = jnp.pad(bias_own, (0, spare - 384)).reshape(16, lanes)
    weights = gather(jnp.concatenate([own_qkv, bias_block], axis=0), "fsdp", size)
    if size > 4:
        weights = jnp.concatenate(
            [jnp.transpose(weights[:, :384], (1, 0, 2)).reshape(384, width),
             jnp.pad(bias_own, (0, 16 * width - 384)).reshape(16, width)], axis=0)[None]

    x0 = own_half(layer_input, tp)
    quarter = half // 2
    x4 = [hop_x(x0[:quarter]), hop_x(x0[quarter:])]
    other = hop_y(blocks[1])
    near = [layer_input, hop_core(layer_input)]
    pair = jnp.stack([deal_order, hop_core(deal_order)])
    order = jnp.concatenate([pair, hop_x(pair)]).reshape(-1) % rows
    x5 = [hop_y(p) for p in x4]
    far = x4 + x5 + [hop_core(p) for p in x4 + x5]
    u = jnp.arange(8, dtype=jnp.int32)
    dest = dev ^ jnp.where(u < 4, (u & 6) | ((u & 1) ^ tp), u)
    slot = jnp.arange(rows, dtype=jnp.int32)
    dest_of = dev ^ jnp.where(slot < 4 * half, ((slot // half) & 6) | (((slot // half) & 1) ^ tp), slot // half)
    arrival = dest_of * half + slot % half
    first_len = seq_lengths[0, :1]
    packed_index = (ctx ^ (slot // own_rows)) * own_rows + slot % own_rows
    position, rank, meet = row_places(order, packed_index, seq_lengths[0], arrival)
    rank = rank[None]
    cos_t, sin_t = rope_tables_t(position)

    hidden_own = jnp.where(tp == core, blocks[0], other)
    hidden_own, weights = lax.optimization_barrier((hidden_own, weights))
    hidden0 = gather(hidden_own, "fsdp", size)

    near_mixed = qkv_rope(ctx_ref, near, weights, cos_t[:, :rows // 2], sin_t[:, :rows // 2])
    far, near_mixed, dense_half = lax.optimization_barrier((far, near_mixed, dense_half))
    dense_parts = lax.all_gather(dense_half, ("tp", "fsdp"), axis=0)
    far_mixed = qkv_rope(ctx_ref, far, weights, cos_t[:, rows // 2:], sin_t[:, rows // 2:])
    hidden0, far_mixed = lax.optimization_barrier((hidden0, far_mixed))
    cut = size // 2
    hiddens = [hidden0, hop_y(hidden0), hop_x(hidden0), hop(hidden0[:cut], 5), None]
    att, sorted_t, att_t, lse = attention_forward(first_len, meet, dest, rank, near_mixed, far_mixed)
    att, dense_parts, hiddens[1:4] = lax.optimization_barrier((att, dense_parts, hiddens[1:4]))
    att = trade(att, CT)
    dense, vec, up_b = run(
        dense_natural_kernel,
        (shape((width, width + emb), bf16), shape((8, width), f32), shape((1, 4 * units), f32)), "dense_natural", 1)(
        jnp.stack([core, place]).astype(jnp.int32), dense_parts, hop_core(dense_parts))
    out_b, gain1, shift1, down_b, gain2, shift2 = (vec[i:i + 1] for i in range(6))
    hiddens[4] = hop(after(hidden0[cut:], att), 5)

    f_rows, b_rows = shape((half, width), f32), shape((half, width), bf16)
    normed, hat1, rstd1, normed_low = run(
        out_proj_kernel, (f_rows, f_rows, shape((half, 1), f32), b_rows), "out_proj")(
        dense, x0, att, out_b, gain1, shift1)
    normed_peer = hop_core(normed_low)
    hidden = shape((own_rows, 4 * units), bf16)
    act, slope, own_down, peer_down = run(mlp_kernel, (hidden, hidden, f_rows, b_rows), "mlp", flops=8_000_000_000)(
        normed_low, normed_peer, up_b, *hiddens)
    w_own = after(weights, normed_low)
    w_y, w_x = hop_y(w_own), hop_x(w_own)
    own_down, peer_down, w_y, w_x = lax.optimization_barrier((own_down, peer_down, w_y, w_x))
    w_cut = max(1, w_own.shape[0] // 2)
    w_xy = [hop(after(w_own[:w_cut], own_down), 5)]
    vec_shape = shape((8, width), f32)
    final_low, embed_low, grad_second, g2, proj_grad, vec2 = run(
        partial(head_kernel, shard_rows),
        (b_rows, shape((half, emb), bf16), f_rows, b_rows, shape((width, emb), bf16), vec_shape), "heads",
        scratch=[pltpu.VMEM((width, emb), bf16)])(
        normed, own_down, hop_core(peer_down), down_b, gain2, shift2, dense,
        own_half(cot_output, tp), own_half(cot_embed, tp))
    g2, w_xy[0] = lax.optimization_barrier((g2, w_xy[0]))
    g2_peer = hop_core(g2)
    if w_cut < w_own.shape[0]:
        w_xy.append(hop(after(w_own[w_cut:], w_xy[0]), 5))
    final_halves = [hop_y(after(final_low[:half // 2], g2))]
    g1, up_bias_part, own_normed, peer_normed = run(
        mlp_back_kernel, (hidden, shape((1, 4 * units), f32), f_rows, b_rows), "mlp_back", flops=16_000_000_000)(
        g2, g2_peer, slope, *hiddens)
    own_normed, final_halves[0], w_xy = lax.optimization_barrier((own_normed, final_halves[0], w_xy))
    w_near = [w_own, w_y, w_x, jnp.concatenate(w_xy, axis=0)]
    w_all = w_near + [hop_core(after(w, own_normed)) for w in w_near]
    grad_first, g0, att_grad, vec1 = run(
        first_back_kernel, (f_rows, b_rows, shape((8, half, 128), bf16), vec_shape), "first_back")(
        grad_second, own_normed, hop_core(peer_normed), hat1, rstd1, gain1, dense)
    att_grad, w_all = lax.optimization_barrier((att_grad, w_all))
    att_grad = lax.all_to_all(att_grad, CT, 0, 0, tiled=True)
    dense_rows = (shard_rows // 4 + shard_rows // 8) * sides
    dense_grad = run(out_weight_kernel, shape((2, 4, size, dense_rows, units), bf16), "out_weight")(
        g0, att, proj_grad, vec2, vec1)
    dense_own = lax.dynamic_index_in_dim(dense_grad, core, 0, keepdims=False)
    dense_recv = hop_core(lax.dynamic_index_in_dim(dense_grad, 1 - core, 0, keepdims=False))
    *up_grads, down_grad = run(
        mlp_weights_kernel,
        (shape((size, shard + 16 + dense_rows, units), bf16),) * 4 + (shape((size, 4, strip, width), bf16),),
        "mlp_weights", 1, flops=16_000_000_000)(
        place_ref, normed_low, normed_peer, g2, g2_peer, act, g1, up_bias_part, dense_own, dense_recv)
    att_grad, up_grads, down_grad = lax.optimization_barrier((att_grad, up_grads, down_grad))
    XY = ("cx", "tp")
    down_parts = trade(down_grad, "fsdp")
    up_parts = [up_grads[0], hop_y(up_grads[1]), hop_x(up_grads[2]), hop(up_grads[3], 5)]
    final_rest, embed_late = after(final_low[half // 2:], att_grad), after(embed_low, att_grad)
    final_halves.append(hop_y(final_rest))
    embed_peer = hop_y(embed_late)
    grad_qkv, qkv_bias_part = attention_backward(
        first_len, meet, dest, rank, sorted_t, att_t, lse, cos_t, sin_t, att_grad)
    grad_qkv, up_parts, down_parts, final_halves, embed_peer = lax.optimization_barrier(
        (grad_qkv, up_parts, down_parts, final_halves, embed_peer))
    final_peer = jnp.concatenate(final_halves, axis=0)
    grad_rows = trade(grad_qkv, CT)

    base = fs if size <= 4 else jnp.zeros_like(fs)
    up_sum, *down_sums = run(
        sum_kernel, (shape(up_grads[0].shape, bf16),) + (shape((strip, width), bf16),) * 4, "sums", 1)(
        jnp.stack([base, place]).astype(jnp.int32), *up_parts, down_parts)
    up_own = collect_z(up_sum)
    down_own = add_all([down_sums[0], hop_y(down_sums[1]), hop_x(down_sums[2]), hop(down_sums[3], 5)])

    own_q = collect_z(run(qkv_weight_kernel, shape((size, 400, lanes), bf16), "qkv_weight", 1)(
        jnp.concatenate([dest, base[None]]).astype(jnp.int32), grad_qkv, qkv_bias_part, *near, *far))
    q_all = around_ctx(own_q, ctx)
    dense_all = around_ctx(up_own[shard + 16:], ctx)

    input_low = run(input_grad_kernel, b_rows, "input_grad", 1)(dev_ref, grad_first, grad_rows, *w_all)
    input_peer = hop_y(input_low)

    hidden_grad = jnp.concatenate(
        [up_own[:shard + 16]] + [down_own[:, s * units:(s + 1) * units] for s in range(sides)], axis=0)
    hidden_core = hop_core(hidden_grad)
    halves = jnp.stack([jnp.where(core == 0, hidden_grad, hidden_core), jnp.where(core == 0, hidden_core, hidden_grad)])
    joined = trade(jnp.concatenate([halves, halves], axis=0), XY)
    up_weight_grad, down_weight_grad = run(
        hidden_join_kernel, (shape(up_weight.shape, f32), shape(down_weight.shape, f32)), "hidden_join")(joined)
    up_bias_grad = lax.dynamic_slice_in_dim(joined[:, shard], fs * strip, strip, axis=1).reshape(-1).astype(f32)

    qkv_weight_grad = jnp.transpose(q_all[:, :384].reshape(4, 3, 128, lanes), (3, 1, 0, 2)).reshape(
        lanes, 3, 512).astype(f32)
    qb = jnp.transpose(q_all[:, 384:].reshape(4, -1)[:, :384].reshape(4, 3, 128), (1, 0, 2)).reshape(3, 512)
    bias_width = qkv_bias.shape[1]
    qkv_bias_grad = lax.dynamic_slice_in_dim(qb, fs * bias_width, bias_width, axis=1).astype(f32)

    thin, tail_rows = shard_rows // 4, shard_rows // 8
    out_weight_grad = jnp.transpose(
        dense_all[:, :thin * sides].reshape(4, sides, thin, units), (0, 2, 1, 3)).reshape(shard_rows, width).astype(f32)
    rest = dense_all[:, thin * sides:].reshape(4, sides, tail_rows, units // 128, 128)[:3]
    rest = jnp.transpose(rest, (1, 3, 2, 0, 4)).reshape(shard_rows, 384)
    rest = pair_rows(rest, hop_y(rest), tp).astype(f32)
    proj_weight_grad = rest[:, :emb]
    sums = jnp.transpose(rest[:, emb:emb + 6])

    return (
        pair_rows(final_low, final_peer, tp),
        pair_rows(embed_low, embed_peer, tp),
        pair_rows(input_low, input_peer, tp),
        qkv_weight_grad,
        qkv_bias_grad,
        out_weight_grad,
        sums[5],
        sums[3],
        sums[4],
        up_weight_grad,
        up_bias_grad,
        down_weight_grad,
        sums[2],
        sums[0],
        sums[1],
        proj_weight_grad,
    )


def solution(mesh):
    fine = Mesh(
        mesh.devices.reshape(mesh.shape["fsdp"], mesh.shape["ctx"] // 2, 2, mesh.shape["tp"]),
        ("fsdp", "cx", "core", "tp"))
    by_rows = ("fsdp", "cx", "core")
    placed = (
        P(by_rows, None),
        P("fsdp", None),
        P(by_rows),
        P("fsdp", None, "tp"),
        P(None, ("tp", "fsdp")),
        P(("tp", "fsdp"), None),
        P("fsdp"),
        P("fsdp"),
        P("fsdp"),
        P("fsdp", "tp"),
        P(("tp", "fsdp")),
        P(("tp", "fsdp"), None),
        P("fsdp"),
        P("fsdp"),
        P("fsdp"),
        P("fsdp", None),
        P(by_rows, None),
        P(by_rows, None),
    )
    outs = (P(by_rows, None), P(by_rows, None), P(by_rows, None)) + placed[3:16]
    return jax.shard_map(shards, mesh=fine, in_specs=placed, out_specs=outs, check_vma=False)
```

```python
import math
from functools import partial
import jax, jax.numpy as jnp
from jax import lax
from jax.experimental import pallas as pl
from jax.experimental.pallas import tpu as pltpu
from jax.sharding import Mesh
from jax.sharding import PartitionSpec as P

f32, bf16 = jnp.float32, jnp.bfloat16
HEAD_DIM = 64
VMEM_CAP = 56 * 1024 * 1024
MASKED = -1e30
SMALL_GRANT = ("mlp", "mlp_weights", "out_proj", "sums", "out_weight", "dense_natural")
SPARE = 14
TS = 256
FQ, FK = 1024, 512
BQ, BK = 512, 512


def nt(a, b):
    return lax.dot_general(a, b, (((1,), (1,)), ((), ())), preferred_element_type=f32)


def nn(a, b):
    return lax.dot_general(a, b, (((1,), (0,)), ((), ())), preferred_element_type=f32)


def run(kernel, out_shape, name, scalars=0, scratch=(), flops=1_000_000):
    def call(*args):
        vm = pl.BlockSpec(memory_space=pltpu.VMEM)
        sm = pl.BlockSpec(memory_space=pltpu.SMEM)
        outs = jax.tree.map(lambda _: vm, out_shape)
        need = sum(x.size * x.dtype.itemsize for x in list(args) + jax.tree.leaves(out_shape))
        limit = min(VMEM_CAP, need + (SPARE << 20)) if name in SMALL_GRANT else VMEM_CAP
        return pl.pallas_call(
            kernel, out_shape=out_shape,
            in_specs=[sm] * scalars + [vm] * (len(args) - scalars), out_specs=outs,
            scratch_shapes=list(scratch),
            compiler_params=pltpu.CompilerParams(vmem_limit_bytes=limit),
            cost_estimate=pl.CostEstimate(flops=flops, transcendentals=0, bytes_accessed=10_000 if flops < 2_000_000 else 8_000_000),
            name=name)(*args)
    return call


def one_hot(rank_ref, tile, start, width):
    want = lax.broadcasted_iota(jnp.int32, (TS, width), 0) + tile * TS
    return jnp.where(rank_ref[:, pl.ds(start, width)] == want, 1.0, 0.0).astype(bf16)


def key_span(start, size, first_len, tile, total):
    lo = jnp.where(start >= first_len, first_len // tile, 0)
    hi = jnp.where(start + size <= first_len, (first_len + tile - 1) // tile, total // tile)
    return lo, hi


def code_lanes(base, rows, first_len):
    row = lax.broadcasted_iota(jnp.int32, (rows, 128), 0) + base
    lane = lax.broadcasted_iota(jnp.int32, (rows, 128), 1)
    bad = jnp.where(row < first_len, 1, 0)
    return jnp.where(lane == bad, MASKED, jnp.where((lane >= 2) & (lane < 5), 1.0, 0.0)).astype(bf16)


def code_rows(base, cols, first_len):
    row = lax.broadcasted_iota(jnp.int32, (128, cols), 0)
    col = lax.broadcasted_iota(jnp.int32, (128, cols), 1) + base
    return (jnp.where(row == jnp.where(col < first_len, 0, 1), 1.0, 0.0), row)


def head_rows(values, head):
    row = lax.broadcasted_iota(jnp.int32, values.shape, 0)
    return jnp.where((row // HEAD_DIM) == head, values, 0.0)


def head_lanes(values, head):
    lane = lax.broadcasted_iota(jnp.int32, values.shape, 1)
    return jnp.where((lane // HEAD_DIM) == head, values, 0.0)


def forward_kernel(len_ref, meet_ref, dest_ref, rank_ref, near_ref, far_ref, att_ref, sorted_ref, att_t_ref, lse_ref,
                   k_ext, q_ext, arr_t):
    rows = rank_ref.shape[1]
    block = rows // 4
    first_len = len_ref[0]
    scale = HEAD_DIM ** -0.5

    def sort_tile(tile, carry):
        at = pl.multiple_of(tile * TS, TS)
        arr_t[:, pl.ds(0, TS)] = jnp.zeros((384, TS), f32)
        for d in range(4):
            @pl.when(meet_ref[tile * 4 + d] > 0)
            def _():
                hot = one_hot(rank_ref, tile, d * block, block)
                mixed_ref = near_ref if d < 2 else far_ref
                arr_t[:, pl.ds(0, TS)] += nt(mixed_ref[:, pl.ds((d % 2) * block, block)], hot)
        low = arr_t[:, pl.ds(0, TS)].astype(bf16)
        sorted_ref[:, pl.ds(at, TS)] = low
        wide = low.astype(f32)
        query = wide[0:128] * scale
        code, _ = code_rows(at, TS, first_len)
        for h in range(2):
            q_ext[h, 0:128, pl.ds(at, TS)] = head_rows(query, h).astype(bf16)
            q_ext[h, 128:256, pl.ds(at, TS)] = code.astype(bf16)
        k_ext[pl.ds(at, TS), 0:128] = wide[128:256].T.astype(bf16)
        k_ext[pl.ds(at, TS), 128:256] = code_lanes(at, TS, first_len)
        return carry

    lax.fori_loop(0, rows // TS, sort_tile, 0)

    def query_tile(i, carry):
        at = pl.multiple_of(i * FQ, FQ)
        lo, hi = key_span(at, FQ, first_len, FK, rows)

        def key_tile(j, state):
            kat = pl.multiple_of(j * FK, FK)
            keys = k_ext[pl.ds(kat, FK), :]
            out = []
            for h in range(2):
                top, total, acc = state[h]
                scores = nn(keys, q_ext[h, :, pl.ds(at, FQ)])
                new_top = jnp.maximum(top, jnp.max(scores, axis=0, keepdims=True))
                fade = jnp.exp(top - new_top)
                weights = jnp.exp(scores - new_top)
                total = total * fade + jnp.sum(weights, axis=0, keepdims=True)
                value = sorted_ref[256 + h * 64:320 + h * 64, pl.ds(kat, FK)]
                acc = acc * fade + nn(value, weights.astype(bf16))
                out.append((new_top, total, acc))
            return tuple(out)

        start = (jnp.full((1, FQ), MASKED, f32), jnp.zeros((1, FQ), f32), jnp.zeros((64, FQ), f32))
        state = lax.fori_loop(lo, hi, key_tile, (start, start))
        lse_rows = []
        for h in range(2):
            top, total, acc = state[h]
            att_t_ref[h * 64:(h + 1) * 64, pl.ds(at, FQ)] = (acc / total).astype(bf16)
            lse_ref[h:h + 1, pl.ds(at, FQ)] = top + jnp.log(total)
        return carry

    lax.fori_loop(0, rows // FQ, query_tile, 0)

    for d in range(4):
        arr_t[0:128, :] = jnp.zeros((128, block), f32)

        def back_tile(tile, carry):
            @pl.when(meet_ref[tile * 4 + d] > 0)
            def _():
                at = pl.multiple_of(tile * TS, TS)
                hot = one_hot(rank_ref, tile, d * block, block)
                arr_t[0:128, :] += nn(att_t_ref[:, pl.ds(at, TS)], hot)
            return carry

        lax.fori_loop(0, rows // TS, back_tile, 0)
        low = arr_t[0:128, :].T.astype(bf16)
        att_ref[dest_ref[2 * d]] = low[:block // 2]
        att_ref[dest_ref[2 * d + 1]] = low[block // 2:]


def attention_forward(first_len, meet, dest, rank, near, far):
    rows = rank.shape[1]
    return pl.pallas_call(
        forward_kernel,
        out_shape=(
            jax.ShapeDtypeStruct((8, rows // 8, 128), bf16),
            jax.ShapeDtypeStruct((384, rows), bf16),
            jax.ShapeDtypeStruct((128, rows), bf16),
            jax.ShapeDtypeStruct((8, rows), f32),
        ),
        in_specs=[
            pl.BlockSpec(memory_space=pltpu.SMEM),
            pl.BlockSpec(memory_space=pltpu.SMEM),
            pl.BlockSpec(memory_space=pltpu.SMEM),
            pl.BlockSpec(memory_space=pltpu.VMEM),
            pl.BlockSpec(memory_space=pltpu.VMEM),
            pl.BlockSpec(memory_space=pltpu.VMEM),
        ],
        out_specs=tuple(pl.BlockSpec(memory_space=pltpu.VMEM) for _ in range(4)),
        scratch_shapes=[
            pltpu.VMEM((rows, 256), bf16),
            pltpu.VMEM((2, 256, rows), bf16),
            pltpu.VMEM((384, rows // 4), f32),
        ],
        compiler_params=pltpu.CompilerParams(vmem_limit_bytes=VMEM_CAP),
        cost_estimate=pl.CostEstimate(flops=60_000_000_000, transcendentals=0, bytes_accessed=10_000),
        name="attention_forward",
    )(first_len, meet, dest, rank, near, far)


def split3(v):
    hi = v.astype(bf16).astype(f32)
    mid = (v - hi).astype(bf16).astype(f32)
    return hi, mid, v - hi - mid


def backward_kernel(len_ref, meet_ref, dest_ref, rank_ref, sorted_ref, att_t_ref, lse_ref, cos_ref, sin_ref,
                    grad_ref, *refs):
    (out_ref, bias_ref, k_ext, q_ext, v_ext, g_ext, q_nat, g_nat, dq_t, arr_t, ds_low) = refs
    rows = rank_ref.shape[1]
    block = rows // 4
    first_len = len_ref[0]
    scale = HEAD_DIM ** -0.5

    def sort_tile(tile, carry):
        at = pl.multiple_of(tile * TS, TS)
        q_t = sorted_ref[0:128, pl.ds(at, TS)].astype(f32) * scale
        k_ext[pl.ds(at, TS), 0:128] = sorted_ref[128:256, pl.ds(at, TS)].astype(f32).T.astype(bf16)
        k_ext[pl.ds(at, TS), 128:256] = code_lanes(at, TS, first_len)
        v_ext[pl.ds(at, TS), 0:128] = sorted_ref[256:384, pl.ds(at, TS)].astype(f32).T.astype(bf16)
        v_ext[pl.ds(at, TS), 128:256] = code_lanes(at, TS, first_len)
        arr_t[0:TS, 0:128] = jnp.zeros((TS, 128), f32)
        for d in range(4):
            @pl.when(meet_ref[tile * 4 + d] > 0)
            def _():
                hot = one_hot(rank_ref, tile, d * block, block)
                half = block // 2
                arr_t[0:TS, 0:128] += (nn(hot[:, :half], grad_ref[dest_ref[2 * d]])
                                       + nn(hot[:, half:], grad_ref[dest_ref[2 * d + 1]]))
        grad = arr_t[0:TS, 0:128]
        grad_t = grad.T
        q = q_t.T
        code, row = code_rows(at, TS, first_len)
        prod = grad_t * att_t_ref[:, pl.ds(at, TS)].astype(f32)
        for h in range(2):
            delta = jnp.sum(prod[h * 64:(h + 1) * 64], axis=0, keepdims=True)
            lse = lse_ref[h:h + 1, pl.ds(at, TS)]
            l0, l1, l2 = split3(-lse)
            d0, d1, d2 = split3(-delta)
            q_ext[h, 0:128, pl.ds(at, TS)] = head_rows(q_t, h).astype(bf16)
            q_ext[h, 128:256, pl.ds(at, TS)] = jnp.where(
                row == 2, l0, jnp.where(row == 3, l1, jnp.where(row == 4, l2, code))).astype(bf16)
            g_ext[h, 0:128, pl.ds(at, TS)] = head_rows(grad_t, h).astype(bf16)
            g_ext[h, 128:256, pl.ds(at, TS)] = jnp.where(
                row == 2, d0, jnp.where(row == 3, d1, jnp.where(row == 4, d2, 0.0))).astype(bf16)
            q_nat[h, pl.ds(at, TS), :] = head_lanes(q, h).astype(bf16)
            g_nat[h, pl.ds(at, TS), :] = head_lanes(grad, h).astype(bf16)
        return carry

    lax.fori_loop(0, rows // TS, sort_tile, 0)
    dq_t[...] = jnp.zeros(dq_t.shape, f32)

    def key_tile(j, carry):
        kat = pl.multiple_of(j * BK, BK)
        lo, hi = key_span(kat, BK, first_len, BQ, rows)

        def query_tile(i, state):
            dk, dv = state
            at = pl.multiple_of(i * BQ, BQ)
            keys = k_ext[pl.ds(kat, BK), :]
            values = v_ext[pl.ds(kat, BK), :]
            for h in range(2):
                probs = jnp.exp(nn(keys, q_ext[h, :, pl.ds(at, BQ)]))
                dprob = nn(values, g_ext[h, :, pl.ds(at, BQ)])
                dscore = (probs * dprob).astype(bf16)
                dv = dv + nn(probs.astype(bf16), g_nat[h, pl.ds(at, BQ), :])
                dk = dk + nn(dscore, q_nat[h, pl.ds(at, BQ), :])
                dq_t[h * 64:(h + 1) * 64, pl.ds(at, BQ)] += nn(
                    sorted_ref[128 + h * 64:192 + h * 64, pl.ds(kat, BK)], dscore)
            return dk, dv

        zero = jnp.zeros((BK, 128), f32)
        dk, dv = lax.fori_loop(lo, hi, query_tile, (zero, zero))
        ds_low[128:256, pl.ds(kat, BK)] = dk.T.astype(bf16)
        ds_low[256:384, pl.ds(kat, BK)] = dv.T.astype(bf16)
        return carry

    lax.fori_loop(0, rows // BK, key_tile, 0)
    ds_low[0:128, :] = (dq_t[...] * scale).astype(bf16)
    bias = jnp.zeros((384, 1), f32)
    for d in range(4):
        arr_t[...] = jnp.zeros((384, block), f32)

        def back_tile(tile, carry):
            @pl.when(meet_ref[tile * 4 + d] > 0)
            def _():
                at = pl.multiple_of(tile * TS, TS)
                hot = one_hot(rank_ref, tile, d * block, block)
                arr_t[...] += nn(ds_low[:, pl.ds(at, TS)], hot)
            return carry

        lax.fori_loop(0, rows // TS, back_tile, 0)
        cos, sin = cos_ref[:, pl.ds(d * block, block)], sin_ref[:, pl.ds(d * block, block)]
        for base in (0, 64, 128, 192):
            front, back = arr_t[base:base + 32, :], arr_t[base + 32:base + 64, :]
            arr_t[base:base + 32, :] = front * cos + back * sin
            arr_t[base + 32:base + 64, :] = back * cos - front * sin
        bias = bias + jnp.sum(arr_t[...], axis=1, keepdims=True)
        out_ref[dest_ref[2 * d]] = arr_t[:, 0:block // 2].astype(bf16)
        out_ref[dest_ref[2 * d + 1]] = arr_t[:, block // 2:block].astype(bf16)
    bias_ref[...] = bias


def attention_backward(first_len, meet, dest, rank, sorted_t, att_t, lse, cos_t, sin_t, grad):
    rows = rank.shape[1]
    vm = pl.BlockSpec(memory_space=pltpu.VMEM)
    sm = pl.BlockSpec(memory_space=pltpu.SMEM)
    return pl.pallas_call(
        backward_kernel,
        out_shape=(
            jax.ShapeDtypeStruct((8, 384, rows // 8), bf16),
            jax.ShapeDtypeStruct((384, 1), f32),
        ),
        in_specs=[sm, sm, sm] + [vm] * 7,
        out_specs=(vm, vm),
        scratch_shapes=[
            pltpu.VMEM((rows, 256), bf16),
            pltpu.VMEM((2, 256, rows), bf16),
            pltpu.VMEM((rows, 256), bf16),
            pltpu.VMEM((2, 256, rows), bf16),
            pltpu.VMEM((2, rows, 128), bf16),
            pltpu.VMEM((2, rows, 128), bf16),
            pltpu.VMEM((128, rows), f32),
            pltpu.VMEM((384, rows // 4), f32),
            pltpu.VMEM((384, rows), bf16),
        ],
        compiler_params=pltpu.CompilerParams(vmem_limit_bytes=VMEM_CAP),
        cost_estimate=pl.CostEstimate(flops=90_000_000_000, transcendentals=0, bytes_accessed=10_000),
        name="attention_backward",
    )(first_len, meet, dest, rank, sorted_t, att_t, lse, cos_t, sin_t, grad)


def qkv_kernel(ctx_ref, cos_ref, sin_ref, w_ref, *refs, first):
    out_ref = refs[-1]
    size, _, lanes = w_ref.shape
    bias = jnp.zeros((1, 384), f32)
    for f in range(size):
        bias_row = jnp.concatenate(
            [w_ref[f, 384 + i:385 + i, :].astype(f32) for i in range(-(-384 // lanes))], axis=1)[:, :384]
        bias = jnp.where(ctx_ref[0] == f, bias_row, bias) if size == 4 else jnp.where(f == 0, bias_row, bias)
    bias = jnp.broadcast_to(bias, (128, 384)).T[:, 0:1]
    start = 0
    for x_ref in refs[:-1]:
        count = x_ref.shape[0]
        span = slice(start, start + count)
        mixed = jnp.broadcast_to(bias, (384, count))
        for f in range(size):
            mixed = mixed + nt(w_ref[f, 0:384], x_ref[:, f * lanes:(f + 1) * lanes])
        table = slice(first + start, first + start + count)
        cos, sin = cos_ref[:, table], sin_ref[:, table]
        for base in (0, 64, 128, 192):
            front, back = mixed[base:base + 32], mixed[base + 32:base + 64]
            out_ref[base:base + 32, span] = (front * cos - back * sin).astype(bf16)
            out_ref[base + 32:base + 64, span] = (back * cos + front * sin).astype(bf16)
        out_ref[256:384, span] = mixed[256:384].astype(bf16)
        start += count


def qkv_rope(ctx, pieces, weights, cos_t, sin_t, first):
    rows = sum(p.shape[0] for p in pieces)
    return run(partial(qkv_kernel, first=first), jax.ShapeDtypeStruct((384, rows), bf16), "qkv_rope", 1)(
        ctx, cos_t, sin_t, weights, *pieces)


def row_places(order, packed, lengths, dest):
    rows = order.shape[0]
    first_len = lengths[0]
    digit = jnp.arange(64, dtype=jnp.int32)
    high = (order // 64)[None, :] == digit[:, None]
    low = ((order % 64)[None, :] == digit[:, None]).astype(bf16)
    parts = jnp.stack([packed // 64, packed % 64]).astype(f32)
    left = jnp.where(high[None], parts[:, None, :], 0.0).astype(bf16).reshape(128, rows)
    table = nt(left, low)
    table = (table[:64] * 64.0 + table[64:]).reshape(8, rows // 8)
    picked = dest[:, None, None] == jnp.arange(8, dtype=jnp.int32)[None, :, None]
    place = jnp.sum(jnp.where(picked, table[None], 0.0), axis=1).reshape(rows).astype(jnp.int32)
    in_first = place < first_len
    position = jnp.where(in_first, place, place - first_len)
    flags = in_first.astype(f32).reshape(rows // 128, 128)
    before = jnp.arange(128)[:, None] < jnp.arange(128)[None, :]
    within = jnp.dot(flags.astype(bf16), before.astype(bf16), preferred_element_type=f32)
    sums = jnp.sum(flags, axis=1)
    n = rows // 128
    earlier = jnp.arange(n)[None, :] < jnp.arange(n)[:, None]
    offset = jnp.sum(jnp.where(earlier, sums[None, :], 0.0), axis=1)
    firsts = (within + offset[:, None]).reshape(rows).astype(jnp.int32)
    index = jnp.arange(rows, dtype=jnp.int32)
    rank = jnp.where(in_first, firsts, first_len + index - firsts)
    counts = jnp.sum(in_first.astype(jnp.int32).reshape(4, rows // 4), axis=1)
    d = jnp.arange(4)
    lo0 = jnp.sum(jnp.where(d[None, :] < d[:, None], counts[None, :], 0), axis=1)
    hi0 = lo0 + counts
    lo1 = first_len + d * (rows // 4) - lo0
    hi1 = lo1 + rows // 4 - counts
    t0 = jnp.arange(rows // TS)[:, None] * TS
    t1 = t0 + TS
    meet = (((lo0[None] < t1) & (hi0[None] > t0) & (hi0 > lo0)[None])
            | ((lo1[None] < t1) & (hi1[None] > t0) & (hi1 > lo1)[None])).astype(jnp.int32)
    return position, rank, meet.reshape(-1)


def rope_tables_t(position):
    frequency = jnp.exp(jnp.arange(32, dtype=f32) * (-2.0 * math.log(10000.0) / 64))
    angles = frequency[:, None] * position.astype(f32)[None, :]
    return jnp.cos(angles), jnp.sin(angles)


norm_eps = 1e-05
embed_eps = 1e-06
WIDTHS = (128, 96, 64)
CT = ("cx", "core", "tp")
CTX = ("cx", "core")


def tn(a, b):
    return lax.dot_general(a, b, (((0,), (0,)), ((), ())), preferred_element_type=f32)


def head_rows_of(device):
    return ((device & 1) * 4 + (device >> 1)) * 128


def row_mean(v):
    return jnp.mean(v, axis=1, keepdims=True)


def norm_parts(v):
    centred = v - row_mean(v)
    rstd = lax.rsqrt(row_mean(centred * centred) + norm_eps)
    return centred * rstd, rstd


def norm_back(grad, x_hat, rstd, gain):
    e = grad * gain
    return (e - row_mean(e) - x_hat * row_mean(e * x_hat)) * rstd


def col_sum(v):
    return jnp.sum(v, axis=0, keepdims=True)


def out_proj_kernel(tp_ref, w_ref, x_ref, att_ref, vec_ref, normed_ref, hat_ref, rstd_ref, low_ref):
    half = normed_ref.shape[0]
    own = pl.ds(pl.multiple_of(tp_ref[0] * half, half), half)
    acc = x_ref[own, :].astype(f32) + vec_ref[0:1]
    for j in range(8):
        at = head_rows_of(j)
        acc = acc + nn(att_ref[j], w_ref[at:at + 128, 0:acc.shape[1]])
    x_hat, rstd = norm_parts(acc)
    normed = x_hat * vec_ref[1:2] + vec_ref[2:3]
    normed_ref[...] = normed
    hat_ref[...] = x_hat
    rstd_ref[...] = rstd
    low_ref[...] = normed.astype(bf16)


def hidden_refs(refs):
    return [(lambda f, r=r: (r, f)) for r in refs[0:4]]


def up_rows(block, f, shard):
    ref, i = block(f)
    return ref[i, 0:shard]


def down_rows(block, group, strip, shard, side):
    parts = []
    for f in group:
        ref, i = block(f)
        at = shard + side * strip
        parts.append(ref[i, at:at + strip])
    return jnp.concatenate(parts, axis=0) if len(parts) > 1 else parts[0]


def hidden_sizes(refs, width):
    size, _, units = refs[0].shape
    strip = units // size
    step = max(1, 256 // strip)
    groups = [range(g, g + step) for g in range(0, size, step)]
    return size, units, strip, width // size, width // units, groups


def mlp_kernel(own_ref, peer_ref, bias_ref, *refs):
    act_ref, slope_ref, own_out, peer_out = refs[4:]
    half, width = own_ref.shape
    size, units, strip, shard, sides, groups = hidden_sizes(refs, width)
    blocks = hidden_refs(refs)
    for r, x_ref in enumerate((own_ref, peer_ref)):
        rows = slice(r * half, (r + 1) * half)
        out = [jnp.zeros((half, units), f32) for _ in range(sides)]
        for v in range(4):
            cols = slice(v * units, (v + 1) * units)
            up = jnp.broadcast_to(bias_ref[:, cols], (half, units))
            for f in range(size):
                up = up + nn(x_ref[:, f * shard:(f + 1) * shard], up_rows(blocks[v], f, shard))
            phi_int = 0.5 * (1.0 + lax.erf(up * (0.5 ** 0.5)))
            density = jnp.exp(-0.5 * up * up) * ((2.0 * math.pi) ** -0.5)
            act = (up * phi_int).astype(bf16)
            act_ref[rows, cols] = act
            slope_ref[rows, cols] = (phi_int + up * density).astype(bf16)
            for g in groups:
                at = g[0] * strip
                part = act[:, at:at + len(g) * strip]
                for s in range(sides):
                    out[s] = out[s] + nn(part, down_rows(blocks[v], g, strip, shard, s))
        for s in range(sides):
            if r == 0:
                own_out[:, s * units:(s + 1) * units] = out[s]
            else:
                peer_out[:, s * units:(s + 1) * units] = out[s].astype(bf16)


def head_kernel(strip_rows, tp_ref, normed_ref, own_ref, recv_ref, all_vec_ref, dense_ref, cot_ref, cot_embed_ref,
                final_ref, embed_ref, grad_ref, low_ref, proj_grad_ref, vec_ref, proj_ref):
    width, emb = proj_ref.shape
    strip = strip_rows
    for f in range(width // (2 * strip)):
        for t in range(2):
            at = (f * 2 + t) * strip
            src = (t * (width // (2 * strip)) + f) * strip
            proj_ref[at:at + strip, :] = dense_ref[src:src + strip, width:width + emb]
    half = normed_ref.shape[0]
    mine = pl.ds(pl.multiple_of(tp_ref[0] * half, half), half)
    gain = all_vec_ref[4:5]
    second = normed_ref[...] + own_ref[...] + recv_ref[...].astype(f32) + all_vec_ref[3:4]
    x_hat, rstd = norm_parts(second)
    final = (x_hat * gain + all_vec_ref[5:6]).astype(bf16)
    final_ref[...] = final
    projected = nn(final, proj_ref[...])
    cot = cot_embed_ref[mine, :].astype(f32)
    col = lax.broadcasted_iota(jnp.int32, projected.shape, 1)
    embedded = jnp.zeros(projected.shape, f32)
    grad_proj = jnp.zeros(projected.shape, f32)
    start = 0
    for width in WIDTHS:
        here = (col >= start) & (col < start + width)
        part = jnp.where(here, projected, 0.0)
        r = lax.rsqrt(jnp.sum(part * part, axis=1, keepdims=True) + embed_eps)
        n = part * r
        along = jnp.sum(n * cot, axis=1, keepdims=True)
        embedded = embedded + n
        grad_proj = jnp.where(here, r * (cot - n * along), grad_proj)
        start += width
    embed_ref[...] = embedded.astype(bf16)
    proj_low = grad_proj.astype(bf16)
    proj_grad_ref[...] = tn(final, proj_low).astype(bf16)
    grad_final = cot_ref[mine, :].astype(f32) + nt(proj_low, proj_ref[...])
    grad_second = norm_back(grad_final, x_hat, rstd, gain)
    grad_ref[...] = grad_second
    low_ref[...] = grad_second.astype(bf16)
    vec_ref[...] = jnp.zeros(vec_ref.shape, f32)
    vec_ref[0:1] = col_sum(grad_final * x_hat)
    vec_ref[1:2] = col_sum(grad_final)
    vec_ref[2:3] = col_sum(grad_second)


def mlp_back_kernel(own_ref, peer_ref, slope_ref, *refs):
    g1_ref, bias_ref, own_out, peer_out = refs[4:]
    half, width = own_ref.shape
    size, units, strip, shard, sides, groups = hidden_sizes(refs, width)
    blocks = hidden_refs(refs)
    for r, g_ref in enumerate((own_ref, peer_ref)):
        rows = slice(r * half, (r + 1) * half)
        out = [jnp.zeros((half, shard), f32) for _ in range(size)]
        for v in range(4):
            for g in groups:
                at = v * units + g[0] * strip
                cols = slice(at, at + len(g) * strip)
                grad_up = nt(g_ref[:, 0:units], down_rows(blocks[v], g, strip, shard, 0))
                for s in range(1, sides):
                    grad_up = grad_up + nt(
                        g_ref[:, s * units:(s + 1) * units], down_rows(blocks[v], g, strip, shard, s))
                grad_up = grad_up * slope_ref[rows, cols].astype(f32)
                sums = col_sum(grad_up)
                bias_ref[:, cols] = sums if r == 0 else bias_ref[:, cols] + sums
                g1_ref[rows, cols] = grad_up.astype(bf16)
            g1 = g1_ref[rows, v * units:(v + 1) * units]
            for f in range(size):
                out[f] = out[f] + nt(g1, up_rows(blocks[v], f, shard))
        for f in range(size):
            if r == 0:
                own_out[:, f * shard:(f + 1) * shard] = out[f]
            else:
                peer_out[:, f * shard:(f + 1) * shard] = out[f].astype(bf16)


def mlp_weights_kernel(place_ref, own_n, peer_n, own_g, peer_g, act_ref, g1_ref, bias_ref, dense_ref, recv_ref,
                       up0, up1, up2, up3, down_ref):
    size, _, units = up0.shape
    strip, shard = down_ref.shape[2], own_n.shape[1] // size
    normed = jnp.concatenate([own_n[...], peer_n[...]], axis=0)
    g2 = jnp.concatenate([own_g[...], peer_g[...]], axis=0)
    for v, up_ref in enumerate((up0, up1, up2, up3)):
        q = place_ref[0] ^ v
        cols = slice(v * units, (v + 1) * units)
        up = tn(normed, g1_ref[:, cols]).astype(bf16)
        down = tn(act_ref[:, cols], g2).astype(bf16)
        bias = jnp.broadcast_to(bias_ref[:, cols], (16, units)).astype(bf16)
        for f in range(size):
            up_ref[f, 0:shard] = up[f * shard:(f + 1) * shard]
            up_ref[f, shard:shard + 16] = bias
            up_ref[f, shard + 16:] = (dense_ref[q, f].astype(f32) + recv_ref[q, f].astype(f32)).astype(bf16)
            down_ref[f, q] = down[f * strip:(f + 1) * strip]


def sum_kernel(index_ref, p0, p1, p2, p3, down_ref, up_out, *down_outs):
    size = up_out.shape[0]
    for f in range(size):
        total = p0[f].astype(f32) + p1[f].astype(f32) + p2[f].astype(f32) + p3[f].astype(f32)
        up_out[(f - index_ref[0] + size) % size] = total.astype(bf16)
    for v, out in enumerate(down_outs):
        total = down_ref[0, index_ref[1] ^ v].astype(f32)
        for f in range(1, size):
            total = total + down_ref[f, index_ref[1] ^ v].astype(f32)
        out[...] = total.astype(bf16)


def pick_kernel(place_ref, up_ref, down_ref, *outs):
    strip = down_ref.shape[0] // 4
    shard, units = up_ref.shape[0], up_ref.shape[1] // 4
    for n in range(2):
        q = place_ref[0] ^ n
        for f in range(units // strip):
            at = pl.multiple_of((f * 4 + q) * strip, strip)
            outs[n][0:shard, f * strip:(f + 1) * strip] = up_ref[:, pl.ds(at, strip)]
        rows = pl.multiple_of(q * strip, strip)
        for s in range(down_ref.shape[1] // units):
            at = shard + s * strip
            outs[n][at:at + strip] = down_ref[pl.ds(rows, strip), s * units:(s + 1) * units]


def dense_half_kernel(index_ref, dense_ref, proj_ref, *refs):
    vecs, half = refs[:7], refs[7]
    core, tp = (index_ref[i] for i in range(2))
    count, width = dense_ref.shape[0] // 2, dense_ref.shape[1]
    half[0:count, 0:width] = dense_ref[pl.ds(pl.multiple_of(core * count, count), count), :]
    half[0:count, width:] = proj_ref[pl.ds(pl.multiple_of((tp * 2 + core) * count, count), count), :]
    lines, line = [], []
    for v in vecs:
        line.append(v[...].astype(f32))
        if sum(p.shape[1] for p in line) == width:
            lines.append(jnp.concatenate(line, axis=1))
            line = []
    block = jnp.concatenate(lines + [jnp.zeros((16 - len(lines), width), f32)], axis=0)
    half[count:count + 16, 0:width] = block.astype(bf16)
    half[count:count + 16, width:] = jnp.zeros((16, half.shape[1] - width), bf16)


def dense_natural_kernel(index_ref, own_ref, core_ref, out_ref, vec_ref, up_ref):
    core, place, tp = (index_ref[i] for i in range(3))
    size, rows = own_ref.shape[0], own_ref.shape[2] - 16
    units = up_ref.shape[1] // 4
    strip, quarter = units // size, vec_ref.shape[1] // size
    for f in range(size):
        for t in range(2):
            own, other = own_ref[f, tp ^ t, 0:rows], core_ref[f, tp ^ t, 0:rows]
            for k in range(2):
                at = ((t * size + f) * 2 + k) * rows
                out_ref[at:at + rows, :] = jnp.where(core == k, own, other)
        vecs = own_ref[f, 0, rows:rows + 16].astype(f32)
        wanted = own_ref[f, tp ^ core, rows:rows + 16].astype(f32)
        cut = 4 * strip
        ups = wanted[0:1, 0:cut]
        for i in range(6):
            r, c = divmod(cut + i * quarter, 4 * quarter)
            vec_ref[i:i + 1, f * quarter:(f + 1) * quarter] = vecs[r:r + 1, c:c + quarter]
        for v in range(4):
            picked = jnp.zeros((1, strip), f32)
            for q in range(4):
                picked = jnp.where((place ^ v) == q, ups[:, q * strip:(q + 1) * strip], picked)
            up_ref[:, v * units + f * strip:v * units + (f + 1) * strip] = picked


def hidden_split_kernel(core_ref, *refs):
    keep_ref, away_ref, dense_ref = refs[-3:]
    ups, downs = refs[:-7], refs[-7:-3]
    rows, units = keep_ref.shape
    strip, width = downs[0].shape

    def total(parts, where):
        out = parts[0][where].astype(f32)
        for p in parts[1:]:
            out = out + p[where].astype(f32)
        return out.astype(bf16)

    def store(up_ref, down_ref):
        up_ref[...] = total(ups, (slice(0, rows), slice(None)))
        down_ref[...] = jnp.zeros(down_ref.shape, bf16)
        for s in range(width // units):
            down_ref[s * strip:(s + 1) * strip] = total(downs, (slice(None), slice(s * units, (s + 1) * units)))

    dense_ref[...] = total(ups, (slice(rows, None), slice(None)))

    @pl.when(core_ref[0] == 0)
    def _():
        store(keep_ref, away_ref)

    @pl.when(core_ref[0] == 1)
    def _():
        store(away_ref, keep_ref)


def hidden_join_kernel(core_ref, own_ref, core_peer_ref, up_ref, down_ref, bias_ref):
    strip = down_ref.shape[0] // 4
    shard, units = up_ref.shape[0], own_ref.shape[2]

    def store(ups, downs):
        for q in range(4):
            for f in range(units // strip):
                at = (f * 4 + q) * strip
                up_ref[:, at:at + strip] = ups[q, 0:shard, f * strip:(f + 1) * strip].astype(f32)
            bias_ref[q] = ups[q, shard:shard + 16].astype(f32)
            for s in range(down_ref.shape[1] // units):
                down_ref[q * strip:(q + 1) * strip, s * units:(s + 1) * units] = (
                    downs[q, s * strip:(s + 1) * strip].astype(f32))

    @pl.when(core_ref[0] == 0)
    def _():
        store(own_ref, core_peer_ref)

    @pl.when(core_ref[0] == 1)
    def _():
        store(core_peer_ref, own_ref)


def first_back_kernel(second_ref, own_ref, recv_ref, hat_ref, rstd_ref, all_vec_ref, w_ref,
                      grad_ref, low_ref, att_grad_ref, vec_ref):
    grad_normed = second_ref[...] + own_ref[...] + recv_ref[...].astype(f32)
    x_hat = hat_ref[...]
    grad_first = norm_back(grad_normed, x_hat, rstd_ref[...], all_vec_ref[1:2])
    grad_ref[...] = grad_first
    low = grad_first.astype(bf16)
    low_ref[...] = low
    for j in range(8):
        at = head_rows_of(j)
        att_grad_ref[j] = nt(low, w_ref[at:at + 128, 0:low.shape[1]]).astype(bf16)
    vec_ref[...] = jnp.zeros(vec_ref.shape, f32)
    vec_ref[0:1] = col_sum(grad_normed * x_hat)
    vec_ref[1:2] = col_sum(grad_normed)
    vec_ref[2:3] = col_sum(grad_first)


def out_weight_kernel(low_ref, att_ref, proj_grad_ref, vec2_ref, vec1_ref, out_ref):
    width = low_ref.shape[1]
    _, _, size, rows, cols = out_ref.shape
    shard = width // (2 * size)
    thin, tail_rows = shard // 4, shard // 8
    sides = width // cols

    def store(t, f, part, at, value):
        for s in range(sides):
            first = at * sides + s * value.shape[0]
            out_ref[part % 2, part // 2 * 2 + t, f, first:first + value.shape[0]] = value[:, s * cols:(s + 1) * cols]

    for j in range(8):
        grad = tn(att_ref[j], low_ref[...]).astype(bf16)
        for start in range(0, 128, thin):
            block, rest = divmod(head_rows_of(j) + start, shard)
            store(block // size, block % size, rest // thin, 0, grad[start:start + thin])
    vecs = jnp.concatenate([vec2_ref[0:3], vec1_ref[0:3], jnp.zeros((122, width), f32)], axis=0).T
    tail = jnp.concatenate([proj_grad_ref[...].astype(f32), vecs[:, 0:96]], axis=1).astype(bf16)
    for f in range(size):
        for t in range(2):
            part = tail[(f * 2 + t) * shard:(f * 2 + t + 1) * shard]
            for b in range(4):
                if b < 3:
                    value = jnp.concatenate(
                        [part[g * tail_rows:(g + 1) * tail_rows, b * 128:(b + 1) * 128] for g in range(8)], axis=1)
                else:
                    value = jnp.zeros((tail_rows, width), bf16)
                store(t, f, b, thin, value)


def qkv_weight_kernel(dest_ref, d_ref, bias_ref, *refs):
    out_ref = refs[-1]
    size, _, lanes = out_ref.shape
    acc = jnp.zeros((384, size * lanes), f32)
    start, part = 0, d_ref.shape[2]
    for x_ref in refs[:-1]:
        done = 0
        while done < x_ref.shape[0]:
            count = min(x_ref.shape[0] - done, part)
            u, at = start // part, start % part
            acc = acc + nn(d_ref[dest_ref[u], :, at:at + count], x_ref[done:done + count])
            start, done = start + count, done + count
    row = jnp.broadcast_to(bias_ref[...], (384, 128)).T[0:1]
    row = jnp.concatenate([row, jnp.zeros((1, max(0, -(-384 // lanes) * lanes - 384)), f32)], axis=1) if 384 % lanes else row
    count = row.shape[1] // lanes
    lines = [row[:, i * lanes:(i + 1) * lanes] for i in range(count)]
    block = jnp.concatenate(lines + [jnp.zeros((16 - count, lanes), f32)], axis=0).astype(bf16)
    for f in range(size):
        s = (f - dest_ref[8] + size) % size
        out_ref[s, 0:384] = acc[:, f * lanes:(f + 1) * lanes].astype(bf16)
        out_ref[s, 384:400] = block


def input_grad_kernel(dev_ref, first_ref, d_ref, *refs):
    out_ref = refs[-1]
    parts, _, lanes = refs[0].shape
    for f in range(parts):
        cols = slice(f * lanes, (f + 1) * lanes)
        acc = first_ref[:, cols]
        for n, w_ref in enumerate(refs[:-1]):
            mask = (0, 1, 4, 5, 2, 3, 6, 7)[n]
            acc = acc + tn(d_ref[dev_ref[0] ^ mask], w_ref[f, 0:384])
        out_ref[:, cols] = acc.astype(bf16)


def hop(value, u):
    return lax.ppermute(value, CT, [(i, i ^ u) for i in range(8)])


def hop_core(value):
    return lax.ppermute(value, "core", [(0, 1), (1, 0)])


def hop_x(value):
    return lax.ppermute(value, "cx", [(0, 1), (1, 0)])


def hop_y(value):
    return lax.ppermute(value, "tp", [(0, 1), (1, 0)])


def shift_z(value, count, size):
    return lax.ppermute(value, "fsdp", [(i, (i + count) % size) for i in range(size)])


def trade(value, axes):
    return lax.all_to_all(value, axes, 0, 0, tiled=True)


def gather(value, axes, count):
    return trade(jnp.broadcast_to(value[None], (count,) + value.shape), axes)


def add_all(parts):
    total = parts[0].astype(f32)
    for p in parts[1:]:
        total = total + p.astype(f32)
    return total.astype(bf16)


def send_z(value):
    size = lax.axis_size("fsdp")
    if size > 4:
        return list(trade(value, "fsdp"))
    return [value[0]] + [
        lax.ppermute(value[s], "fsdp", [(i, (i + s) % size) for i in range(size)]) for s in range(1, size)]


def around_ctx(value, ctx):
    far = hop_x(value)
    return by_xor([value, hop_core(value), far, hop_core(far)], ctx)


def by_xor(parts, own):
    stacked = jnp.stack(parts)
    return jnp.stack([lax.dynamic_index_in_dim(stacked, own ^ i, 0, keepdims=False) for i in range(len(parts))])


def pair_rows(own, peers, tp):
    half = own.shape[0]
    out = jnp.concatenate([own, own], axis=0)
    at = (1 - tp) * half
    for p in peers:
        out = lax.dynamic_update_slice_in_dim(out, p, at, axis=0)
        at = at + p.shape[0]
    return out


def shards(
    layer_input,
    seq_lengths,
    deal_order,
    qkv_weight,
    qkv_bias,
    out_weight,
    out_bias,
    first_gain,
    first_shift,
    up_weight,
    up_bias,
    down_weight,
    down_bias,
    second_gain,
    second_shift,
    proj_weight,
    cot_output,
    cot_embed,
):
    own_rows, width = layer_input.shape
    half = own_rows // 2
    rows = own_rows * 4
    fs, cx, core, tp = (lax.axis_index(n) for n in ("fsdp", "cx", "core", "tp"))
    size = lax.axis_size("fsdp")
    ctx = cx * 2 + core
    dev = ctx * 2 + tp
    dev_ref = dev.astype(jnp.int32).reshape(1)
    shape = jax.ShapeDtypeStruct

    def own_half(value, which):
        return lax.dynamic_slice_in_dim(value, which * half, half, axis=0)

    def after(value, *others):
        return lax.optimization_barrier((value,) + others)[0]

    place = cx * 2 + tp
    strip = down_weight.shape[0] // 4
    units = size * strip
    shard = up_weight.shape[0]
    place_ref = place.astype(jnp.int32).reshape(1)
    tp_ref = tp.astype(jnp.int32).reshape(1)
    ctx_ref = ctx.astype(jnp.int32).reshape(1)
    sides = width // units
    hidden_rows = shard + sides * strip
    emb = proj_weight.shape[1]
    shard_rows = out_weight.shape[0]
    vectors = [up_bias, out_bias, first_gain, first_shift, down_bias, second_gain, second_shift]
    if size > 4:
        def hidden_block(q):
            wide = up_weight.reshape(shard, size, 4, strip)
            up = lax.dynamic_index_in_dim(wide, q, 2, keepdims=False).reshape(shard, units)
            down = lax.dynamic_slice_in_dim(down_weight, q * strip, strip, axis=0)
            return jnp.concatenate([up] + [down[:, s * units:(s + 1) * units] for s in range(sides)], axis=0)

        blocks = [hidden_block(place), hidden_block(place ^ 1)]
        half_rows = shard_rows // 2
        part = lax.dynamic_slice_in_dim(proj_weight, tp * shard_rows, shard_rows, axis=0)
        vec_block = jnp.concatenate(vectors).reshape(-1, 4 * shard)
        vec_block = jnp.pad(vec_block, ((0, 16 - vec_block.shape[0]), (0, width + emb - 4 * shard)))
        beside = jnp.concatenate([out_weight, part], axis=1)
        dense_half = jnp.concatenate(
            [lax.dynamic_slice_in_dim(beside, core * half_rows, half_rows, axis=0), vec_block], axis=0)
    else:
        blocks = run(pick_kernel, (shape((hidden_rows, units), bf16),) * 2, "pick", 1)(place_ref, up_weight, down_weight)
    lanes = shard
    own_qkv = lax.dynamic_slice_in_dim(qkv_weight, ctx * 128, 128, axis=2)
    own_qkv = jnp.transpose(own_qkv, (1, 2, 0)).reshape(384, lanes)
    spare = 16 * lanes
    if size == 4:
        bias_own = qkv_bias.reshape(-1)
    else:
        bias_all = lax.all_gather(qkv_bias, "fsdp", axis=1, tiled=True)
        bias_own = lax.dynamic_slice_in_dim(bias_all, ctx * 128, 128, axis=1).reshape(-1)
    bias_block = jnp.pad(bias_own, (0, spare - 384)).reshape(16, lanes)
    weights = gather(jnp.concatenate([own_qkv, bias_block], axis=0), "fsdp", size)
    if size > 4:
        weights = jnp.concatenate(
            [jnp.transpose(weights[:, :384], (1, 0, 2)).reshape(384, width),
             jnp.pad(bias_own, (0, 16 * width - 384)).reshape(16, width)], axis=0)[None]

    x0 = own_half(layer_input, tp)
    quarter = half // 2
    x4 = [hop_x(x0[:quarter]), hop_x(x0[quarter:])]
    other = hop_y(blocks[1])
    hidden_own = jnp.where(tp == core, blocks[0], other)
    pair = jnp.stack([deal_order, hop_core(deal_order)])
    order = jnp.concatenate([pair, hop_x(pair)]).reshape(-1) % rows
    near = [layer_input, hop_core(layer_input)]
    hidden_own, weights = lax.optimization_barrier((hidden_own, weights))
    hidden0 = gather(hidden_own, "fsdp", size)
    x5 = [hop_y(p) for p in x4]
    far = x4 + x5 + [hop_core(p) for p in x4 + x5]
    u = jnp.arange(8, dtype=jnp.int32)
    dest = dev ^ jnp.where(u < 4, (u & 6) | ((u & 1) ^ tp), u)
    slot = jnp.arange(rows, dtype=jnp.int32)
    first_len = seq_lengths[0, :1]
    packed_index = (ctx ^ (slot // own_rows)) * own_rows + slot % own_rows
    position, rank, meet = row_places(order, packed_index, seq_lengths[0], dest)
    rank = rank[None]
    cos_t, sin_t = rope_tables_t(position)

    near_mixed = qkv_rope(ctx_ref, near, weights, cos_t, sin_t, 0)
    far, near_mixed = lax.optimization_barrier((far, near_mixed))
    if size <= 4:
        dense_half = run(dense_half_kernel, shape((shard_rows // 2 + 16, width + emb), bf16), "dense_half", 1)(
            jnp.stack([core, tp]).astype(jnp.int32), after(out_weight, near_mixed), proj_weight,
            *[v.reshape(1, -1) for v in vectors])
    dense_pair = jnp.stack([dense_half, hop_y(dense_half)])
    far_mixed = qkv_rope(ctx_ref, far, weights, cos_t, sin_t, rows // 2)
    hidden0, far_mixed, dense_pair = lax.optimization_barrier((hidden0, far_mixed, dense_pair))
    dense_parts = gather(dense_pair, "fsdp", size)
    hiddens = [hidden0, hop_y(hidden0), hop_x(hidden0), hop(hidden0, 5)]
    att, sorted_t, att_t, lse = attention_forward(first_len, meet, dest, rank, near_mixed, far_mixed)
    att, dense_parts, hiddens[1:3] = lax.optimization_barrier((att, dense_parts, hiddens[1:3]))
    att = trade(att, CT)
    dense, vec, up_b = run(
        dense_natural_kernel,
        (shape((width, width + emb), bf16), shape((8, width), f32), shape((1, 4 * units), f32)), "dense_natural", 1)(
        jnp.stack([core, place, tp]).astype(jnp.int32), dense_parts, hop_core(dense_parts))
    att, dense, vec, up_b = lax.optimization_barrier((att, dense, vec, up_b))

    f_rows, b_rows = shape((half, width), f32), shape((half, width), bf16)
    normed, hat1, rstd1, normed_low = run(
        out_proj_kernel, (f_rows, f_rows, shape((half, 1), f32), b_rows), "out_proj", 1)(
        tp_ref, dense, layer_input, att, vec)
    normed_peer = hop_core(normed_low)
    hidden = shape((own_rows, 4 * units), bf16)
    act, slope, own_down, peer_down = run(mlp_kernel, (hidden, hidden, f_rows, b_rows), "mlp")(
        normed_low, normed_peer, up_b, *hiddens)
    w_own = after(weights, hiddens[3])
    w_y, w_x = hop_y(w_own), hop_x(w_own)
    act, slope, own_down, peer_down, w_y, w_x = lax.optimization_barrier((act, slope, own_down, peer_down, w_y, w_x))
    w_cut = max(1, w_own.shape[0] // 2)
    w_xy = [hop(after(w_own[:w_cut], own_down), 5)]
    vec_shape = shape((8, width), f32)
    final_low, embed_low, grad_second, g2, proj_grad, vec2 = run(
        partial(head_kernel, shard_rows),
        (b_rows, shape((half, emb), bf16), f_rows, b_rows, shape((width, emb), bf16), vec_shape), "heads", 1,
        scratch=[pltpu.VMEM((width, emb), bf16)], flops=2_000_000_000)(
        tp_ref, normed, own_down, hop_core(peer_down), vec, dense, cot_output, cot_embed)
    final_low, embed_low, grad_second, g2, proj_grad, vec2, w_xy[0] = lax.optimization_barrier(
        (final_low, embed_low, grad_second, g2, proj_grad, vec2, w_xy[0]))
    g2_peer = hop_core(g2)
    if w_cut < w_own.shape[0]:
        w_xy.append(hop(after(w_own[w_cut:], w_xy[0]), 5))
    final_halves = [hop_y(after(final_low[:half // 2], g2))]
    g1, up_bias_part, own_normed, peer_normed = run(
        mlp_back_kernel, (hidden, shape((1, 4 * units), f32), f_rows, b_rows), "mlp_back")(
        g2, g2_peer, slope, *hiddens)
    g1, up_bias_part, own_normed, peer_normed, final_halves[0], w_xy = lax.optimization_barrier(
        (g1, up_bias_part, own_normed, peer_normed, final_halves[0], w_xy))
    w_near = [w_own, w_y, w_x, jnp.concatenate(w_xy, axis=0)]
    w_all = w_near + [hop_core(after(w, own_normed)) for w in w_near]
    grad_first, g0, att_grad, vec1 = run(
        first_back_kernel, (f_rows, b_rows, shape((8, half, 128), bf16), vec_shape), "first_back")(
        grad_second, own_normed, hop_core(peer_normed), hat1, rstd1, vec, dense)
    grad_first, g0, att_grad, vec1, w_all = lax.optimization_barrier((grad_first, g0, att_grad, vec1, w_all))
    att_grad = lax.all_to_all(att_grad, CT, 0, 0, tiled=True)
    dense_rows = (shard_rows // 4 + shard_rows // 8) * sides
    dense_grad = run(out_weight_kernel, shape((2, 4, size, dense_rows, units), bf16), "out_weight")(
        g0, att, proj_grad, vec2, vec1)
    dense_own = lax.dynamic_index_in_dim(dense_grad, core, 0, keepdims=False)
    dense_recv = hop_core(lax.dynamic_index_in_dim(dense_grad, 1 - core, 0, keepdims=False))
    *up_grads, down_grad = run(
        mlp_weights_kernel,
        (shape((size, shard + 16 + dense_rows, units), bf16),) * 4 + (shape((size, 4, strip, width), bf16),),
        "mlp_weights", 1)(
        place_ref, normed_low, normed_peer, g2, g2_peer, act, g1, up_bias_part, dense_own, dense_recv)
    att_grad, up_grads, down_grad = lax.optimization_barrier((att_grad, up_grads, down_grad))
    XY = ("cx", "tp")
    down_parts = trade(down_grad, "fsdp")
    up_parts = [up_grads[0], hop_y(up_grads[1]), hop_x(up_grads[2]), hop(up_grads[3], 5)]
    final_rest, embed_late = after(final_low[half // 2:], att_grad), after(embed_low, att_grad)
    final_halves.append(hop_y(final_rest))
    embed_peer = hop_y(embed_late)
    grad_qkv, qkv_bias_part = attention_backward(
        first_len, meet, dest, rank, sorted_t, att_t, lse, cos_t, sin_t, att_grad)
    grad_qkv, up_parts, down_parts, final_halves, embed_peer = lax.optimization_barrier(
        (grad_qkv, up_parts, down_parts, final_halves, embed_peer))
    grad_rows = trade(grad_qkv, CT)

    base = fs if size <= 4 else jnp.zeros_like(fs)
    qkv_sums = run(qkv_weight_kernel, shape((size, 400, lanes), bf16), "qkv_weight", 1)(
        jnp.concatenate([dest, base[None]]).astype(jnp.int32), grad_qkv, qkv_bias_part, *near, *far)
    qkv_sums, up_parts, down_parts = lax.optimization_barrier((qkv_sums, up_parts, down_parts))
    up_sum, *down_sums = run(
        sum_kernel, (shape(up_grads[0].shape, bf16),) + (shape((strip, width), bf16),) * 4, "sums", 1)(
        jnp.stack([base, place]).astype(jnp.int32), *up_parts, down_parts)
    up_parts = send_z(up_sum)
    down_parts = [down_sums[0], hop_y(down_sums[1]), hop_x(down_sums[2]), hop(down_sums[3], 5)]

    qkv_sums, grad_rows = lax.optimization_barrier((qkv_sums, grad_rows))
    input_low = run(input_grad_kernel, b_rows, "input_grad", 1)(dev_ref, grad_first, grad_rows, *w_all)
    input_peer = hop_y(input_low)
    up_parts, down_parts, qkv_sums, final_low, embed_low = lax.optimization_barrier(
        (up_parts, down_parts, qkv_sums, final_low, embed_low, input_low))[:5]
    own_q = add_all(send_z(qkv_sums))
    q_all = around_ctx(own_q, ctx)

    side_rows = shape((shard + 16, units), bf16)
    send, away, dense_own = run(
        hidden_split_kernel, (side_rows, side_rows, shape((dense_rows, units), bf16)), "hidden_split", 1)(
        core.astype(jnp.int32).reshape(1), *up_parts, *down_parts)
    recv = hop_core(away)
    dense_all = around_ctx(dense_own, ctx)
    halves = jnp.stack([jnp.where(core == 0, send, recv), jnp.where(core == 0, recv, send)])
    joined = trade(jnp.concatenate([halves, halves], axis=0), XY)
    joined, input_peer = lax.optimization_barrier((joined, input_peer))
    joined_core = hop_core(joined)
    up_weight_grad, down_weight_grad, bias_rows = run(
        hidden_join_kernel, (shape(up_weight.shape, f32), shape(down_weight.shape, f32), shape((4, 16, units), f32)),
        "hidden_join", 1)(core.astype(jnp.int32).reshape(1), joined, joined_core)
    up_bias_grad = lax.dynamic_slice_in_dim(bias_rows[:, 0], fs * strip, strip, axis=1).reshape(-1)

    q_all = q_all.reshape(4, 400, lanes)
    qkv_weight_grad = jnp.transpose(q_all[:, :384].reshape(4, 3, 128, lanes), (3, 1, 0, 2)).reshape(
        lanes, 3, 512).astype(f32)
    qb = jnp.transpose(q_all[:, 384:].reshape(4, -1)[:, :384].reshape(4, 3, 128), (1, 0, 2)).reshape(3, 512)
    bias_width = qkv_bias.shape[1]
    qkv_bias_grad = lax.dynamic_slice_in_dim(qb, fs * bias_width, bias_width, axis=1).astype(f32)

    thin, tail_rows = shard_rows // 4, shard_rows // 8
    out_weight_grad = jnp.transpose(
        dense_all[:, :thin * sides].reshape(4, sides, thin, units), (0, 2, 1, 3)).reshape(shard_rows, width).astype(f32)
    rest = dense_all[:, thin * sides:].reshape(4, sides, tail_rows, units // 128, 128)[:3]
    rest = jnp.transpose(rest, (1, 3, 2, 0, 4)).reshape(shard_rows, 384)
    rest = pair_rows(rest, [hop_y(rest)], tp).astype(f32)
    proj_weight_grad = rest[:, :emb]
    sums = jnp.transpose(rest[:, emb:emb + 6])

    return (
        pair_rows(final_low, final_halves, tp),
        pair_rows(embed_low, [embed_peer], tp),
        pair_rows(after(input_low, send), [input_peer], tp),
        qkv_weight_grad,
        qkv_bias_grad,
        out_weight_grad,
        sums[5],
        sums[3],
        sums[4],
        up_weight_grad,
        up_bias_grad,
        down_weight_grad,
        sums[2],
        sums[0],
        sums[1],
        proj_weight_grad,
    )


def solution(mesh):
    fine = Mesh(
        mesh.devices.reshape(mesh.shape["fsdp"], mesh.shape["ctx"] // 2, 2, mesh.shape["tp"]),
        ("fsdp", "cx", "core", "tp"))
    by_rows = ("fsdp", "cx", "core")
    placed = (
        P(by_rows, None),
        P("fsdp", None),
        P(by_rows),
        P("fsdp", None, "tp"),
        P(None, ("tp", "fsdp")),
        P(("tp", "fsdp"), None),
        P("fsdp"),
        P("fsdp"),
        P("fsdp"),
        P("fsdp", "tp"),
        P(("tp", "fsdp")),
        P(("tp", "fsdp"), None),
        P("fsdp"),
        P("fsdp"),
        P("fsdp"),
        P("fsdp", None),
        P(by_rows, None),
        P(by_rows, None),
    )
    outs = (P(by_rows, None), P(by_rows, None), P(by_rows, None)) + placed[3:16]
    return jax.shard_map(shards, mesh=fine, in_specs=placed, out_specs=outs, check_vma=False)
```

```python
import math
from functools import partial
import jax, jax.numpy as jnp
from jax import lax
from jax.experimental import pallas as pl
from jax.experimental.pallas import tpu as pltpu
from jax.sharding import Mesh
from jax.sharding import PartitionSpec as P

f32, bf16 = jnp.float32, jnp.bfloat16
HEAD_DIM = 64
VMEM_CAP = 56 * 1024 * 1024
MASKED = -1e30
SMALL_GRANT = ("mlp", "mlp_weights", "out_proj", "sums", "out_weight", "dense_natural")
SPARE = 14
TS = 256
FQ, FK = 1024, 512
BQ, BK = 512, 512


def nt(a, b):
    return lax.dot_general(a, b, (((1,), (1,)), ((), ())), preferred_element_type=f32)


def nn(a, b):
    return lax.dot_general(a, b, (((1,), (0,)), ((), ())), preferred_element_type=f32)


def run(kernel, out_shape, name, scalars=0, scratch=(), flops=1_000_000):
    def call(*args):
        vm = pl.BlockSpec(memory_space=pltpu.VMEM)
        sm = pl.BlockSpec(memory_space=pltpu.SMEM)
        outs = jax.tree.map(lambda _: vm, out_shape)
        need = sum(x.size * x.dtype.itemsize for x in list(args) + jax.tree.leaves(out_shape))
        limit = min(VMEM_CAP, need + (SPARE << 20)) if name in SMALL_GRANT else VMEM_CAP
        return pl.pallas_call(
            kernel, out_shape=out_shape,
            in_specs=[sm] * scalars + [vm] * (len(args) - scalars), out_specs=outs,
            scratch_shapes=list(scratch),
            compiler_params=pltpu.CompilerParams(vmem_limit_bytes=limit),
            cost_estimate=pl.CostEstimate(flops=flops, transcendentals=0, bytes_accessed=10_000 if flops < 2_000_000 else 8_000_000),
            name=name)(*args)
    return call


def one_hot(rank_ref, tile, start, width):
    want = lax.broadcasted_iota(jnp.int32, (TS, width), 0) + tile * TS
    return jnp.where(rank_ref[:, pl.ds(start, width)] == want, 1.0, 0.0).astype(bf16)


def key_span(start, size, first_len, tile, total):
    lo = jnp.where(start >= first_len, first_len // tile, 0)
    hi = jnp.where(start + size <= first_len, (first_len + tile - 1) // tile, total // tile)
    return lo, hi


def code_lanes(base, rows, first_len):
    row = lax.broadcasted_iota(jnp.int32, (rows, 128), 0) + base
    lane = lax.broadcasted_iota(jnp.int32, (rows, 128), 1)
    bad = jnp.where(row < first_len, 1, 0)
    return jnp.where(lane == bad, MASKED, jnp.where((lane >= 2) & (lane < 5), 1.0, 0.0)).astype(bf16)


def code_rows(base, cols, first_len):
    row = lax.broadcasted_iota(jnp.int32, (128, cols), 0)
    col = lax.broadcasted_iota(jnp.int32, (128, cols), 1) + base
    return (jnp.where(row == jnp.where(col < first_len, 0, 1), 1.0, 0.0), row)


def head_rows(values, head):
    row = lax.broadcasted_iota(jnp.int32, values.shape, 0)
    return jnp.where((row // HEAD_DIM) == head, values, 0.0)


def head_lanes(values, head):
    lane = lax.broadcasted_iota(jnp.int32, values.shape, 1)
    return jnp.where((lane // HEAD_DIM) == head, values, 0.0)


def forward_kernel(len_ref, meet_ref, dest_ref, rank_ref, near_ref, far_ref, att_ref, sorted_ref, att_t_ref, lse_ref,
                   k_ext, q_ext, arr_t):
    rows = rank_ref.shape[1]
    block = rows // 4
    first_len = len_ref[0]
    scale = HEAD_DIM ** -0.5

    def sort_tile(tile, carry):
        at = pl.multiple_of(tile * TS, TS)
        arr_t[:, pl.ds(0, TS)] = jnp.zeros((384, TS), f32)
        for d in range(4):
            @pl.when(meet_ref[tile * 4 + d] > 0)
            def _():
                hot = one_hot(rank_ref, tile, d * block, block)
                mixed_ref = near_ref if d < 2 else far_ref
                arr_t[:, pl.ds(0, TS)] += nt(mixed_ref[:, pl.ds((d % 2) * block, block)], hot)
        low = arr_t[:, pl.ds(0, TS)].astype(bf16)
        sorted_ref[:, pl.ds(at, TS)] = low
        wide = low.astype(f32)
        query = wide[0:128] * scale
        code, _ = code_rows(at, TS, first_len)
        for h in range(2):
            q_ext[h, 0:128, pl.ds(at, TS)] = head_rows(query, h).astype(bf16)
            q_ext[h, 128:256, pl.ds(at, TS)] = code.astype(bf16)
        k_ext[pl.ds(at, TS), 0:128] = wide[128:256].T.astype(bf16)
        k_ext[pl.ds(at, TS), 128:256] = code_lanes(at, TS, first_len)
        return carry

    lax.fori_loop(0, rows // TS, sort_tile, 0)

    def query_tile(i, carry):
        at = pl.multiple_of(i * FQ, FQ)
        lo, hi = key_span(at, FQ, first_len, FK, rows)

        def key_tile(j, state):
            kat = pl.multiple_of(j * FK, FK)
            keys = k_ext[pl.ds(kat, FK), :]
            out = []
            for h in range(2):
                top, total, acc = state[h]
                scores = nn(keys, q_ext[h, :, pl.ds(at, FQ)])
                new_top = jnp.maximum(top, jnp.max(scores, axis=0, keepdims=True))
                fade = jnp.exp(top - new_top)
                weights = jnp.exp(scores - new_top)
                total = total * fade + jnp.sum(weights, axis=0, keepdims=True)
                value = sorted_ref[256 + h * 64:320 + h * 64, pl.ds(kat, FK)]
                acc = acc * fade + nn(value, weights.astype(bf16))
                out.append((new_top, total, acc))
            return tuple(out)

        start = (jnp.full((1, FQ), MASKED, f32), jnp.zeros((1, FQ), f32), jnp.zeros((64, FQ), f32))
        state = lax.fori_loop(lo, hi, key_tile, (start, start))
        lse_rows = []
        for h in range(2):
            top, total, acc = state[h]
            att_t_ref[h * 64:(h + 1) * 64, pl.ds(at, FQ)] = (acc / total).astype(bf16)
            lse_ref[h:h + 1, pl.ds(at, FQ)] = top + jnp.log(total)
        return carry

    lax.fori_loop(0, rows // FQ, query_tile, 0)

    for d in range(4):
        arr_t[0:128, :] = jnp.zeros((128, block), f32)

        def back_tile(tile, carry):
            @pl.when(meet_ref[tile * 4 + d] > 0)
            def _():
                at = pl.multiple_of(tile * TS, TS)
                hot = one_hot(rank_ref, tile, d * block, block)
                arr_t[0:128, :] += nn(att_t_ref[:, pl.ds(at, TS)], hot)
            return carry

        lax.fori_loop(0, rows // TS, back_tile, 0)
        low = arr_t[0:128, :].T.astype(bf16)
        att_ref[dest_ref[2 * d]] = low[:block // 2]
        att_ref[dest_ref[2 * d + 1]] = low[block // 2:]


def attention_forward(first_len, meet, dest, rank, near, far):
    rows = rank.shape[1]
    return pl.pallas_call(
        forward_kernel,
        out_shape=(
            jax.ShapeDtypeStruct((8, rows // 8, 128), bf16),
            jax.ShapeDtypeStruct((384, rows), bf16),
            jax.ShapeDtypeStruct((128, rows), bf16),
            jax.ShapeDtypeStruct((8, rows), f32),
        ),
        in_specs=[
            pl.BlockSpec(memory_space=pltpu.SMEM),
            pl.BlockSpec(memory_space=pltpu.SMEM),
            pl.BlockSpec(memory_space=pltpu.SMEM),
            pl.BlockSpec(memory_space=pltpu.VMEM),
            pl.BlockSpec(memory_space=pltpu.VMEM),
            pl.BlockSpec(memory_space=pltpu.VMEM),
        ],
        out_specs=tuple(pl.BlockSpec(memory_space=pltpu.VMEM) for _ in range(4)),
        scratch_shapes=[
            pltpu.VMEM((rows, 256), bf16),
            pltpu.VMEM((2, 256, rows), bf16),
            pltpu.VMEM((384, rows // 4), f32),
        ],
        compiler_params=pltpu.CompilerParams(vmem_limit_bytes=VMEM_CAP),
        cost_estimate=pl.CostEstimate(flops=60_000_000_000, transcendentals=0, bytes_accessed=10_000),
        name="attention_forward",
    )(first_len, meet, dest, rank, near, far)


def split3(v):
    hi = v.astype(bf16).astype(f32)
    mid = (v - hi).astype(bf16).astype(f32)
    return hi, mid, v - hi - mid


def backward_kernel(len_ref, meet_ref, dest_ref, rank_ref, sorted_ref, att_t_ref, lse_ref, cos_ref, sin_ref,
                    grad_ref, *refs):
    (out_ref, bias_ref, k_ext, q_ext, v_ext, g_ext, q_nat, g_nat, dq_t, arr_t, ds_low) = refs
    rows = rank_ref.shape[1]
    block = rows // 4
    first_len = len_ref[0]
    scale = HEAD_DIM ** -0.5

    def sort_tile(tile, carry):
        at = pl.multiple_of(tile * TS, TS)
        q_t = sorted_ref[0:128, pl.ds(at, TS)].astype(f32) * scale
        k_ext[pl.ds(at, TS), 0:128] = sorted_ref[128:256, pl.ds(at, TS)].astype(f32).T.astype(bf16)
        k_ext[pl.ds(at, TS), 128:256] = code_lanes(at, TS, first_len)
        v_ext[pl.ds(at, TS), 0:128] = sorted_ref[256:384, pl.ds(at, TS)].astype(f32).T.astype(bf16)
        v_ext[pl.ds(at, TS), 128:256] = code_lanes(at, TS, first_len)
        arr_t[0:TS, 0:128] = jnp.zeros((TS, 128), f32)
        for d in range(4):
            @pl.when(meet_ref[tile * 4 + d] > 0)
            def _():
                hot = one_hot(rank_ref, tile, d * block, block)
                half = block // 2
                arr_t[0:TS, 0:128] += (nn(hot[:, :half], grad_ref[dest_ref[2 * d]])
                                       + nn(hot[:, half:], grad_ref[dest_ref[2 * d + 1]]))
        grad = arr_t[0:TS, 0:128]
        grad_t = grad.T
        q = q_t.T
        code, row = code_rows(at, TS, first_len)
        prod = grad_t * att_t_ref[:, pl.ds(at, TS)].astype(f32)
        for h in range(2):
            delta = jnp.sum(prod[h * 64:(h + 1) * 64], axis=0, keepdims=True)
            lse = lse_ref[h:h + 1, pl.ds(at, TS)]
            l0, l1, l2 = split3(-lse)
            d0, d1, d2 = split3(-delta)
            q_ext[h, 0:128, pl.ds(at, TS)] = head_rows(q_t, h).astype(bf16)
            q_ext[h, 128:256, pl.ds(at, TS)] = jnp.where(
                row == 2, l0, jnp.where(row == 3, l1, jnp.where(row == 4, l2, code))).astype(bf16)
            g_ext[h, 0:128, pl.ds(at, TS)] = head_rows(grad_t, h).astype(bf16)
            g_ext[h, 128:256, pl.ds(at, TS)] = jnp.where(
                row == 2, d0, jnp.where(row == 3, d1, jnp.where(row == 4, d2, 0.0))).astype(bf16)
            q_nat[h, pl.ds(at, TS), :] = head_lanes(q, h).astype(bf16)
            g_nat[h, pl.ds(at, TS), :] = head_lanes(grad, h).astype(bf16)
        return carry

    lax.fori_loop(0, rows // TS, sort_tile, 0)
    dq_t[...] = jnp.zeros(dq_t.shape, f32)

    def key_tile(j, carry):
        kat = pl.multiple_of(j * BK, BK)
        lo, hi = key_span(kat, BK, first_len, BQ, rows)

        def query_tile(i, state):
            dk, dv = state
            at = pl.multiple_of(i * BQ, BQ)
            keys = k_ext[pl.ds(kat, BK), :]
            values = v_ext[pl.ds(kat, BK), :]
            for h in range(2):
                probs = jnp.exp(nn(keys, q_ext[h, :, pl.ds(at, BQ)]))
                dprob = nn(values, g_ext[h, :, pl.ds(at, BQ)])
                dscore = (probs * dprob).astype(bf16)
                dv = dv + nn(probs.astype(bf16), g_nat[h, pl.ds(at, BQ), :])
                dk = dk + nn(dscore, q_nat[h, pl.ds(at, BQ), :])
                dq_t[h * 64:(h + 1) * 64, pl.ds(at, BQ)] += nn(
                    sorted_ref[128 + h * 64:192 + h * 64, pl.ds(kat, BK)], dscore)
            return dk, dv

        zero = jnp.zeros((BK, 128), f32)
        dk, dv = lax.fori_loop(lo, hi, query_tile, (zero, zero))
        ds_low[128:256, pl.ds(kat, BK)] = dk.T.astype(bf16)
        ds_low[256:384, pl.ds(kat, BK)] = dv.T.astype(bf16)
        return carry

    lax.fori_loop(0, rows // BK, key_tile, 0)
    ds_low[0:128, :] = (dq_t[...] * scale).astype(bf16)
    bias = jnp.zeros((384, 1), f32)
    for d in range(4):
        arr_t[...] = jnp.zeros((384, block), f32)

        def back_tile(tile, carry):
            @pl.when(meet_ref[tile * 4 + d] > 0)
            def _():
                at = pl.multiple_of(tile * TS, TS)
                hot = one_hot(rank_ref, tile, d * block, block)
                arr_t[...] += nn(ds_low[:, pl.ds(at, TS)], hot)
            return carry

        lax.fori_loop(0, rows // TS, back_tile, 0)
        cos, sin = cos_ref[:, pl.ds(d * block, block)], sin_ref[:, pl.ds(d * block, block)]
        for base in (0, 64, 128, 192):
            front, back = arr_t[base:base + 32, :], arr_t[base + 32:base + 64, :]
            arr_t[base:base + 32, :] = front * cos + back * sin
            arr_t[base + 32:base + 64, :] = back * cos - front * sin
        bias = bias + jnp.sum(arr_t[...], axis=1, keepdims=True)
        out_ref[dest_ref[2 * d]] = arr_t[:, 0:block // 2].astype(bf16)
        out_ref[dest_ref[2 * d + 1]] = arr_t[:, block // 2:block].astype(bf16)
    bias_ref[...] = bias


def attention_backward(first_len, meet, dest, rank, sorted_t, att_t, lse, cos_t, sin_t, grad):
    rows = rank.shape[1]
    vm = pl.BlockSpec(memory_space=pltpu.VMEM)
    sm = pl.BlockSpec(memory_space=pltpu.SMEM)
    return pl.pallas_call(
        backward_kernel,
        out_shape=(
            jax.ShapeDtypeStruct((8, 384, rows // 8), bf16),
            jax.ShapeDtypeStruct((384, 1), f32),
        ),
        in_specs=[sm, sm, sm] + [vm] * 7,
        out_specs=(vm, vm),
        scratch_shapes=[
            pltpu.VMEM((rows, 256), bf16),
            pltpu.VMEM((2, 256, rows), bf16),
            pltpu.VMEM((rows, 256), bf16),
            pltpu.VMEM((2, 256, rows), bf16),
            pltpu.VMEM((2, rows, 128), bf16),
            pltpu.VMEM((2, rows, 128), bf16),
            pltpu.VMEM((128, rows), f32),
            pltpu.VMEM((384, rows // 4), f32),
            pltpu.VMEM((384, rows), bf16),
        ],
        compiler_params=pltpu.CompilerParams(vmem_limit_bytes=VMEM_CAP),
        cost_estimate=pl.CostEstimate(flops=90_000_000_000, transcendentals=0, bytes_accessed=10_000),
        name="attention_backward",
    )(first_len, meet, dest, rank, sorted_t, att_t, lse, cos_t, sin_t, grad)


def qkv_kernel(ctx_ref, cos_ref, sin_ref, w_ref, *refs, first):
    out_ref = refs[-1]
    size, _, lanes = w_ref.shape
    bias = jnp.zeros((1, 384), f32)
    for f in range(size):
        bias_row = jnp.concatenate(
            [w_ref[f, 384 + i:385 + i, :].astype(f32) for i in range(-(-384 // lanes))], axis=1)[:, :384]
        bias = jnp.where(ctx_ref[0] == f, bias_row, bias) if size == 4 else jnp.where(f == 0, bias_row, bias)
    bias = jnp.broadcast_to(bias, (128, 384)).T[:, 0:1]
    start = 0
    for x_ref in refs[:-1]:
        count = x_ref.shape[0]
        span = slice(start, start + count)
        mixed = jnp.broadcast_to(bias, (384, count))
        for f in range(size):
            mixed = mixed + nt(w_ref[f, 0:384], x_ref[:, f * lanes:(f + 1) * lanes])
        table = slice(first + start, first + start + count)
        cos, sin = cos_ref[:, table], sin_ref[:, table]
        for base in (0, 64, 128, 192):
            front, back = mixed[base:base + 32], mixed[base + 32:base + 64]
            out_ref[base:base + 32, span] = (front * cos - back * sin).astype(bf16)
            out_ref[base + 32:base + 64, span] = (back * cos + front * sin).astype(bf16)
        out_ref[256:384, span] = mixed[256:384].astype(bf16)
        start += count


def qkv_rope(ctx, pieces, weights, cos_t, sin_t, first):
    rows = sum(p.shape[0] for p in pieces)
    return run(partial(qkv_kernel, first=first), jax.ShapeDtypeStruct((384, rows), bf16), "qkv_rope", 1)(
        ctx, cos_t, sin_t, weights, *pieces)


def row_places(order, packed, lengths, dest):
    rows = order.shape[0]
    first_len = lengths[0]
    digit = jnp.arange(64, dtype=jnp.int32)
    high = (order // 64)[None, :] == digit[:, None]
    low = ((order % 64)[None, :] == digit[:, None]).astype(bf16)
    parts = jnp.stack([packed // 64, packed % 64]).astype(f32)
    left = jnp.where(high[None], parts[:, None, :], 0.0).astype(bf16).reshape(128, rows)
    table = nt(left, low)
    table = (table[:64] * 64.0 + table[64:]).reshape(8, rows // 8)
    picked = dest[:, None, None] == jnp.arange(8, dtype=jnp.int32)[None, :, None]
    place = jnp.sum(jnp.where(picked, table[None], 0.0), axis=1).reshape(rows).astype(jnp.int32)
    in_first = place < first_len
    position = jnp.where(in_first, place, place - first_len)
    flags = in_first.astype(f32).reshape(rows // 128, 128)
    before = jnp.arange(128)[:, None] < jnp.arange(128)[None, :]
    within = jnp.dot(flags.astype(bf16), before.astype(bf16), preferred_element_type=f32)
    sums = jnp.sum(flags, axis=1)
    n = rows // 128
    earlier = jnp.arange(n)[None, :] < jnp.arange(n)[:, None]
    offset = jnp.sum(jnp.where(earlier, sums[None, :], 0.0), axis=1)
    firsts = (within + offset[:, None]).reshape(rows).astype(jnp.int32)
    index = jnp.arange(rows, dtype=jnp.int32)
    rank = jnp.where(in_first, firsts, first_len + index - firsts)
    counts = jnp.sum(in_first.astype(jnp.int32).reshape(4, rows // 4), axis=1)
    d = jnp.arange(4)
    lo0 = jnp.sum(jnp.where(d[None, :] < d[:, None], counts[None, :], 0), axis=1)
    hi0 = lo0 + counts
    lo1 = first_len + d * (rows // 4) - lo0
    hi1 = lo1 + rows // 4 - counts
    t0 = jnp.arange(rows // TS)[:, None] * TS
    t1 = t0 + TS
    meet = (((lo0[None] < t1) & (hi0[None] > t0) & (hi0 > lo0)[None])
            | ((lo1[None] < t1) & (hi1[None] > t0) & (hi1 > lo1)[None])).astype(jnp.int32)
    return position, rank, meet.reshape(-1)


def rope_tables_t(position):
    frequency = jnp.exp(jnp.arange(32, dtype=f32) * (-2.0 * math.log(10000.0) / 64))
    angles = frequency[:, None] * position.astype(f32)[None, :]
    return jnp.cos(angles), jnp.sin(angles)


norm_eps = 1e-05
embed_eps = 1e-06
WIDTHS = (128, 96, 64)
CT = ("cx", "core", "tp")
CTX = ("cx", "core")


def tn(a, b):
    return lax.dot_general(a, b, (((0,), (0,)), ((), ())), preferred_element_type=f32)


def head_rows_of(device):
    return ((device & 1) * 4 + (device >> 1)) * 128


def row_mean(v):
    return jnp.mean(v, axis=1, keepdims=True)


def norm_parts(v):
    centred = v - row_mean(v)
    rstd = lax.rsqrt(row_mean(centred * centred) + norm_eps)
    return centred * rstd, rstd


def norm_back(grad, x_hat, rstd, gain):
    e = grad * gain
    return (e - row_mean(e) - x_hat * row_mean(e * x_hat)) * rstd


def col_sum(v):
    return jnp.sum(v, axis=0, keepdims=True)


def out_proj_kernel(tp_ref, w_ref, x_ref, att_ref, vec_ref, normed_ref, hat_ref, rstd_ref, low_ref):
    half = normed_ref.shape[0]
    own = pl.ds(pl.multiple_of(tp_ref[0] * half, half), half)
    acc = x_ref[own, :].astype(f32) + vec_ref[0:1]
    for j in range(8):
        at = head_rows_of(j)
        acc = acc + nn(att_ref[j], w_ref[at:at + 128, 0:acc.shape[1]])
    x_hat, rstd = norm_parts(acc)
    normed = x_hat * vec_ref[1:2] + vec_ref[2:3]
    normed_ref[...] = normed
    hat_ref[...] = x_hat
    rstd_ref[...] = rstd
    low_ref[...] = normed.astype(bf16)


def hidden_refs(refs):
    return [(lambda f, r=r: (r, f)) for r in refs[0:4]]


def up_rows(block, f, shard):
    ref, i = block(f)
    return ref[i, 0:shard]


def down_rows(block, group, strip, shard, side):
    parts = []
    for f in group:
        ref, i = block(f)
        at = shard + side * strip
        parts.append(ref[i, at:at + strip])
    return jnp.concatenate(parts, axis=0) if len(parts) > 1 else parts[0]


def hidden_sizes(refs, width):
    size, _, units = refs[0].shape
    strip = units // size
    step = max(1, 256 // strip)
    groups = [range(g, g + step) for g in range(0, size, step)]
    return size, units, strip, width // size, width // units, groups


def mlp_kernel(own_ref, peer_ref, bias_ref, *refs):
    act_ref, slope_ref, own_out, peer_out = refs[4:]
    half, width = own_ref.shape
    size, units, strip, shard, sides, groups = hidden_sizes(refs, width)
    blocks = hidden_refs(refs)
    for r, x_ref in enumerate((own_ref, peer_ref)):
        rows = slice(r * half, (r + 1) * half)
        out = [jnp.zeros((half, units), f32) for _ in range(sides)]
        for v in range(4):
            cols = slice(v * units, (v + 1) * units)
            up = jnp.broadcast_to(bias_ref[:, cols], (half, units))
            for f in range(size):
                up = up + nn(x_ref[:, f * shard:(f + 1) * shard], up_rows(blocks[v], f, shard))
            phi_int = 0.5 * (1.0 + lax.erf(up * (0.5 ** 0.5)))
            density = jnp.exp(-0.5 * up * up) * ((2.0 * math.pi) ** -0.5)
            act = (up * phi_int).astype(bf16)
            act_ref[rows, cols] = act
            slope_ref[rows, cols] = (phi_int + up * density).astype(bf16)
            for g in groups:
                at = g[0] * strip
                part = act[:, at:at + len(g) * strip]
                for s in range(sides):
                    out[s] = out[s] + nn(part, down_rows(blocks[v], g, strip, shard, s))
        for s in range(sides):
            if r == 0:
                own_out[:, s * units:(s + 1) * units] = out[s]
            else:
                peer_out[:, s * units:(s + 1) * units] = out[s].astype(bf16)


def head_kernel(tp_ref, normed_ref, own_ref, recv_ref, all_vec_ref, proj_ref, cot_ref, cot_embed_ref,
                first_ref, last_ref, embed_ref, grad_ref, low_ref, proj_grad_ref, vec_ref):
    half = normed_ref.shape[0]
    mine = pl.ds(pl.multiple_of(tp_ref[0] * half, half), half)
    gain = all_vec_ref[4:5]
    second = normed_ref[...] + own_ref[...] + recv_ref[...].astype(f32) + all_vec_ref[3:4]
    x_hat, rstd = norm_parts(second)
    final = (x_hat * gain + all_vec_ref[5:6]).astype(bf16)
    first_ref[...] = final[:half // 2]
    last_ref[...] = final[half // 2:]
    projected = nn(final, proj_ref[...])
    cot = cot_embed_ref[...].astype(f32)
    col = lax.broadcasted_iota(jnp.int32, projected.shape, 1)
    embedded = jnp.zeros(projected.shape, f32)
    grad_proj = jnp.zeros(projected.shape, f32)
    start = 0
    for width in WIDTHS:
        here = (col >= start) & (col < start + width)
        part = jnp.where(here, projected, 0.0)
        r = lax.rsqrt(jnp.sum(part * part, axis=1, keepdims=True) + embed_eps)
        n = part * r
        along = jnp.sum(n * cot, axis=1, keepdims=True)
        embedded = embedded + n
        grad_proj = jnp.where(here, r * (cot - n * along), grad_proj)
        start += width
    embed_ref[...] = embedded.astype(bf16)
    proj_low = grad_proj.astype(bf16)
    proj_grad_ref[...] = tn(final, proj_low).astype(bf16)
    grad_final = cot_ref[mine, :].astype(f32) + nt(proj_low, proj_ref[...])
    grad_second = norm_back(grad_final, x_hat, rstd, gain)
    grad_ref[...] = grad_second
    low_ref[...] = grad_second.astype(bf16)
    vec_ref[...] = jnp.zeros(vec_ref.shape, f32)
    vec_ref[0:1] = col_sum(grad_final * x_hat)
    vec_ref[1:2] = col_sum(grad_final)
    vec_ref[2:3] = col_sum(grad_second)


def mlp_back_kernel(own_ref, peer_ref, slope_ref, *refs):
    g1_ref, bias_ref, own_out, peer_out = refs[4:]
    half, width = own_ref.shape
    size, units, strip, shard, sides, groups = hidden_sizes(refs, width)
    blocks = hidden_refs(refs)
    for r, g_ref in enumerate((own_ref, peer_ref)):
        rows = slice(r * half, (r + 1) * half)
        out = [jnp.zeros((half, shard), f32) for _ in range(size)]
        for v in range(4):
            for g in groups:
                at = v * units + g[0] * strip
                cols = slice(at, at + len(g) * strip)
                grad_up = nt(g_ref[:, 0:units], down_rows(blocks[v], g, strip, shard, 0))
                for s in range(1, sides):
                    grad_up = grad_up + nt(
                        g_ref[:, s * units:(s + 1) * units], down_rows(blocks[v], g, strip, shard, s))
                grad_up = grad_up * slope_ref[rows, cols].astype(f32)
                sums = col_sum(grad_up)
                bias_ref[:, cols] = sums if r == 0 else bias_ref[:, cols] + sums
                g1_ref[rows, cols] = grad_up.astype(bf16)
            g1 = g1_ref[rows, v * units:(v + 1) * units]
            for f in range(size):
                out[f] = out[f] + nt(g1, up_rows(blocks[v], f, shard))
        for f in range(size):
            if r == 0:
                own_out[:, f * shard:(f + 1) * shard] = out[f]
            else:
                peer_out[:, f * shard:(f + 1) * shard] = out[f].astype(bf16)


def mlp_weights_kernel(place_ref, own_n, peer_n, own_g, peer_g, act_ref, g1_ref, bias_ref, dense_ref, recv_ref,
                       up0, up1, up2, up3, down_ref):
    size, _, units = up0.shape
    strip, shard = down_ref.shape[2], own_n.shape[1] // size
    normed = jnp.concatenate([own_n[...], peer_n[...]], axis=0)
    g2 = jnp.concatenate([own_g[...], peer_g[...]], axis=0)
    for v, up_ref in enumerate((up0, up1, up2, up3)):
        q = place_ref[0] ^ v
        cols = slice(v * units, (v + 1) * units)
        up = tn(normed, g1_ref[:, cols]).astype(bf16)
        down = tn(act_ref[:, cols], g2).astype(bf16)
        bias = jnp.broadcast_to(bias_ref[:, cols], (16, units)).astype(bf16)
        for f in range(size):
            up_ref[f, 0:shard] = up[f * shard:(f + 1) * shard]
            up_ref[f, shard:shard + 16] = bias
            up_ref[f, shard + 16:] = (dense_ref[q, f].astype(f32) + recv_ref[q, f].astype(f32)).astype(bf16)
            down_ref[f, q] = down[f * strip:(f + 1) * strip]


def sum_kernel(index_ref, p0, p1, p2, p3, down_ref, up_out, *down_outs):
    size = up_out.shape[0]
    for f in range(size):
        total = p0[f].astype(f32) + p1[f].astype(f32) + p2[f].astype(f32) + p3[f].astype(f32)
        up_out[(f - index_ref[0] + size) % size] = total.astype(bf16)
    for v, out in enumerate(down_outs):
        total = down_ref[0, index_ref[1] ^ v].astype(f32)
        for f in range(1, size):
            total = total + down_ref[f, index_ref[1] ^ v].astype(f32)
        out[...] = total.astype(bf16)


def pick_kernel(place_ref, up_ref, down_ref, *outs):
    strip = down_ref.shape[0] // 4
    shard, units = up_ref.shape[0], up_ref.shape[1] // 4
    for n in range(2):
        q = place_ref[0] ^ n
        for f in range(units // strip):
            at = pl.multiple_of((f * 4 + q) * strip, strip)
            outs[n][0:shard, f * strip:(f + 1) * strip] = up_ref[:, pl.ds(at, strip)]
        rows = pl.multiple_of(q * strip, strip)
        for s in range(down_ref.shape[1] // units):
            at = shard + s * strip
            outs[n][at:at + strip] = down_ref[pl.ds(rows, strip), s * units:(s + 1) * units]


def dense_half_kernel(index_ref, dense_ref, proj_ref, *refs):
    vecs, half = refs[:7], refs[7]
    core, tp = (index_ref[i] for i in range(2))
    count, width = dense_ref.shape[0] // 2, dense_ref.shape[1]
    half[0:count, 0:width] = dense_ref[pl.ds(pl.multiple_of(core * count, count), count), :]
    half[0:count, width:] = proj_ref[pl.ds(pl.multiple_of((tp * 2 + core) * count, count), count), :]
    lines, line = [], []
    for v in vecs:
        line.append(v[...].astype(f32))
        if sum(p.shape[1] for p in line) == width:
            lines.append(jnp.concatenate(line, axis=1))
            line = []
    block = jnp.concatenate(lines + [jnp.zeros((16 - len(lines), width), f32)], axis=0)
    half[count:count + 16, 0:width] = block.astype(bf16)
    half[count:count + 16, width:] = jnp.zeros((16, half.shape[1] - width), bf16)


def dense_natural_kernel(index_ref, own_ref, core_ref, out_ref, proj_ref, vec_ref, up_ref):
    core, place, tp = (index_ref[i] for i in range(3))
    size, rows = own_ref.shape[0], own_ref.shape[2] - 16
    units = up_ref.shape[1] // 4
    strip, quarter = units // size, vec_ref.shape[1] // size
    for f in range(size):
        for t in range(2):
            own, other = own_ref[f, tp ^ t, 0:rows], core_ref[f, tp ^ t, 0:rows]
            for k in range(2):
                at = ((t * size + f) * 2 + k) * rows
                value = jnp.where(core == k, own, other)
                out_ref[at:at + rows, :] = value[:, 0:out_ref.shape[1]]
                at = ((f * 2 + t) * 2 + k) * rows
                proj_ref[at:at + rows, :] = value[:, out_ref.shape[1]:]
        vecs = own_ref[f, 0, rows:rows + 16].astype(f32)
        wanted = own_ref[f, tp ^ core, rows:rows + 16].astype(f32)
        cut = 4 * strip
        ups = wanted[0:1, 0:cut]
        for i in range(6):
            r, c = divmod(cut + i * quarter, 4 * quarter)
            vec_ref[i:i + 1, f * quarter:(f + 1) * quarter] = vecs[r:r + 1, c:c + quarter]
        for v in range(4):
            picked = jnp.zeros((1, strip), f32)
            for q in range(4):
                picked = jnp.where((place ^ v) == q, ups[:, q * strip:(q + 1) * strip], picked)
            up_ref[:, v * units + f * strip:v * units + (f + 1) * strip] = picked


def hidden_split_kernel(core_ref, *refs):
    keep_ref, away_ref, dense_ref = refs[-3:]
    ups, downs = refs[:-7], refs[-7:-3]
    rows, units = keep_ref.shape
    strip, width = downs[0].shape

    def total(parts, where):
        out = parts[0][where].astype(f32)
        for p in parts[1:]:
            out = out + p[where].astype(f32)
        return out.astype(bf16)

    def store(up_ref, down_ref):
        up_ref[...] = total(ups, (slice(0, rows), slice(None)))
        down_ref[...] = jnp.zeros(down_ref.shape, bf16)
        for s in range(width // units):
            down_ref[s * strip:(s + 1) * strip] = total(downs, (slice(None), slice(s * units, (s + 1) * units)))

    dense_ref[...] = total(ups, (slice(rows, None), slice(None)))

    @pl.when(core_ref[0] == 0)
    def _():
        store(keep_ref, away_ref)

    @pl.when(core_ref[0] == 1)
    def _():
        store(away_ref, keep_ref)


def hidden_join_kernel(core_ref, own_ref, core_peer_ref, up_ref, down_ref, bias_ref):
    strip = down_ref.shape[0] // 4
    shard, units = up_ref.shape[0], own_ref.shape[2]

    def store(ups, downs):
        for q in range(4):
            for f in range(units // strip):
                at = (f * 4 + q) * strip
                up_ref[:, at:at + strip] = ups[q, 0:shard, f * strip:(f + 1) * strip].astype(f32)
            bias_ref[q] = ups[q, shard:shard + 16].astype(f32)
            for s in range(down_ref.shape[1] // units):
                down_ref[q * strip:(q + 1) * strip, s * units:(s + 1) * units] = (
                    downs[q, s * strip:(s + 1) * strip].astype(f32))

    @pl.when(core_ref[0] == 0)
    def _():
        store(own_ref, core_peer_ref)

    @pl.when(core_ref[0] == 1)
    def _():
        store(core_peer_ref, own_ref)


def first_back_kernel(second_ref, own_ref, recv_ref, hat_ref, rstd_ref, all_vec_ref, w_ref,
                      grad_ref, low_ref, att_grad_ref, vec_ref):
    grad_normed = second_ref[...] + own_ref[...] + recv_ref[...].astype(f32)
    x_hat = hat_ref[...]
    grad_first = norm_back(grad_normed, x_hat, rstd_ref[...], all_vec_ref[1:2])
    grad_ref[...] = grad_first
    low = grad_first.astype(bf16)
    low_ref[...] = low
    for j in range(8):
        at = head_rows_of(j)
        att_grad_ref[j] = nt(low, w_ref[at:at + 128, 0:low.shape[1]]).astype(bf16)
    vec_ref[...] = jnp.zeros(vec_ref.shape, f32)
    vec_ref[0:1] = col_sum(grad_normed * x_hat)
    vec_ref[1:2] = col_sum(grad_normed)
    vec_ref[2:3] = col_sum(grad_first)


def out_weight_kernel(low_ref, att_ref, proj_grad_ref, vec2_ref, vec1_ref, out_ref):
    width = low_ref.shape[1]
    _, _, size, rows, cols = out_ref.shape
    shard = width // (2 * size)
    thin, tail_rows = shard // 4, shard // 8
    sides = width // cols

    def store(t, f, part, at, value):
        for s in range(sides):
            first = at * sides + s * value.shape[0]
            out_ref[part % 2, part // 2 * 2 + t, f, first:first + value.shape[0]] = value[:, s * cols:(s + 1) * cols]

    for j in range(8):
        grad = tn(att_ref[j], low_ref[...]).astype(bf16)
        for start in range(0, 128, thin):
            block, rest = divmod(head_rows_of(j) + start, shard)
            store(block // size, block % size, rest // thin, 0, grad[start:start + thin])
    vecs = jnp.concatenate([vec2_ref[0:3], vec1_ref[0:3], jnp.zeros((122, width), f32)], axis=0).T
    tail = jnp.concatenate([proj_grad_ref[...].astype(f32), vecs[:, 0:96]], axis=1).astype(bf16)
    for f in range(size):
        for t in range(2):
            part = tail[(f * 2 + t) * shard:(f * 2 + t + 1) * shard]
            for b in range(4):
                if b < 3:
                    value = jnp.concatenate(
                        [part[g * tail_rows:(g + 1) * tail_rows, b * 128:(b + 1) * 128] for g in range(8)], axis=1)
                else:
                    value = jnp.zeros((tail_rows, width), bf16)
                store(t, f, b, thin, value)


def qkv_weight_kernel(dest_ref, d_ref, bias_ref, *refs):
    out_ref = refs[-1]
    size, _, lanes = out_ref.shape
    acc = jnp.zeros((384, size * lanes), f32)
    start, part = 0, d_ref.shape[2]
    for x_ref in refs[:-1]:
        done = 0
        while done < x_ref.shape[0]:
            count = min(x_ref.shape[0] - done, part)
            u, at = start // part, start % part
            acc = acc + nn(d_ref[dest_ref[u], :, at:at + count], x_ref[done:done + count])
            start, done = start + count, done + count
    row = jnp.broadcast_to(bias_ref[...], (384, 128)).T[0:1]
    row = jnp.concatenate([row, jnp.zeros((1, max(0, -(-384 // lanes) * lanes - 384)), f32)], axis=1) if 384 % lanes else row
    count = row.shape[1] // lanes
    lines = [row[:, i * lanes:(i + 1) * lanes] for i in range(count)]
    block = jnp.concatenate(lines + [jnp.zeros((16 - count, lanes), f32)], axis=0).astype(bf16)
    for f in range(size):
        s = (f - dest_ref[8] + size) % size
        out_ref[s, 0:384] = acc[:, f * lanes:(f + 1) * lanes].astype(bf16)
        out_ref[s, 384:400] = block


def input_grad_kernel(dev_ref, first_ref, d_ref, *refs):
    out_ref = refs[-1]
    parts, _, lanes = refs[0].shape
    for f in range(parts):
        cols = slice(f * lanes, (f + 1) * lanes)
        acc = first_ref[:, cols]
        for n, w_ref in enumerate(refs[:-1]):
            mask = (0, 1, 4, 5, 2, 3, 6, 7)[n]
            acc = acc + tn(d_ref[dev_ref[0] ^ mask], w_ref[f, 0:384])
        out_ref[:, cols] = acc.astype(bf16)


def hop(value, u):
    return lax.ppermute(value, CT, [(i, i ^ u) for i in range(8)])


def hop_core(value):
    return lax.ppermute(value, "core", [(0, 1), (1, 0)])


def hop_x(value):
    return lax.ppermute(value, "cx", [(0, 1), (1, 0)])


def hop_y(value):
    return lax.ppermute(value, "tp", [(0, 1), (1, 0)])


def shift_z(value, count, size):
    return lax.ppermute(value, "fsdp", [(i, (i + count) % size) for i in range(size)])


def trade(value, axes):
    return lax.all_to_all(value, axes, 0, 0, tiled=True)


def gather(value, axes, count):
    return trade(jnp.broadcast_to(value[None], (count,) + value.shape), axes)


def add_all(parts):
    total = parts[0].astype(f32)
    for p in parts[1:]:
        total = total + p.astype(f32)
    return total.astype(bf16)


def send_z(value):
    size = lax.axis_size("fsdp")
    if size > 4:
        return list(trade(value, "fsdp"))
    return [value[0]] + [
        lax.ppermute(value[s], "fsdp", [(i, (i + s) % size) for i in range(size)]) for s in range(1, size)]


def around_ctx(value, ctx):
    far = hop_x(value)
    return by_xor([value, hop_core(value), far, hop_core(far)], ctx)


def by_xor(parts, own):
    stacked = jnp.stack(parts)
    return jnp.stack([lax.dynamic_index_in_dim(stacked, own ^ i, 0, keepdims=False) for i in range(len(parts))])


def pair_rows(own, peers, tp):
    own = own if isinstance(own, list) else [own]
    half = sum(p.shape[0] for p in own)
    out = jnp.concatenate(own + own, axis=0)
    at = (1 - tp) * half
    for p in peers:
        out = lax.dynamic_update_slice_in_dim(out, p, at, axis=0)
        at = at + p.shape[0]
    return out


def shards(
    layer_input,
    seq_lengths,
    deal_order,
    qkv_weight,
    qkv_bias,
    out_weight,
    out_bias,
    first_gain,
    first_shift,
    up_weight,
    up_bias,
    down_weight,
    down_bias,
    second_gain,
    second_shift,
    proj_weight,
    cot_output,
    cot_embed,
):
    own_rows, width = layer_input.shape
    half = own_rows // 2
    rows = own_rows * 4
    fs, cx, core, tp = (lax.axis_index(n) for n in ("fsdp", "cx", "core", "tp"))
    size = lax.axis_size("fsdp")
    ctx = cx * 2 + core
    dev = ctx * 2 + tp
    dev_ref = dev.astype(jnp.int32).reshape(1)
    shape = jax.ShapeDtypeStruct

    def own_half(value, which):
        return lax.dynamic_slice_in_dim(value, which * half, half, axis=0)

    def after(value, *others):
        return lax.optimization_barrier((value,) + others)[0]

    place = cx * 2 + tp
    strip = down_weight.shape[0] // 4
    units = size * strip
    shard = up_weight.shape[0]
    place_ref = place.astype(jnp.int32).reshape(1)
    tp_ref = tp.astype(jnp.int32).reshape(1)
    ctx_ref = ctx.astype(jnp.int32).reshape(1)
    sides = width // units
    hidden_rows = shard + sides * strip
    emb = proj_weight.shape[1]
    shard_rows = out_weight.shape[0]
    vectors = [up_bias, out_bias, first_gain, first_shift, down_bias, second_gain, second_shift]
    if size > 4:
        def hidden_block(q):
            wide = up_weight.reshape(shard, size, 4, strip)
            up = lax.dynamic_index_in_dim(wide, q, 2, keepdims=False).reshape(shard, units)
            down = lax.dynamic_slice_in_dim(down_weight, q * strip, strip, axis=0)
            return jnp.concatenate([up] + [down[:, s * units:(s + 1) * units] for s in range(sides)], axis=0)

        blocks = [hidden_block(place), hidden_block(place ^ 1)]
        half_rows = shard_rows // 2
        part = lax.dynamic_slice_in_dim(proj_weight, tp * shard_rows, shard_rows, axis=0)
        vec_block = jnp.concatenate(vectors).reshape(-1, 4 * shard)
        vec_block = jnp.pad(vec_block, ((0, 16 - vec_block.shape[0]), (0, width + emb - 4 * shard)))
        beside = jnp.concatenate([out_weight, part], axis=1)
        dense_half = jnp.concatenate(
            [lax.dynamic_slice_in_dim(beside, core * half_rows, half_rows, axis=0), vec_block], axis=0)
    else:
        blocks = run(pick_kernel, (shape((hidden_rows, units), bf16),) * 2, "pick", 1)(place_ref, up_weight, down_weight)
    lanes = shard
    own_qkv = lax.dynamic_slice_in_dim(qkv_weight, ctx * 128, 128, axis=2)
    own_qkv = jnp.transpose(own_qkv, (1, 2, 0)).reshape(384, lanes)
    spare = 16 * lanes
    if size == 4:
        bias_own = qkv_bias.reshape(-1)
    else:
        bias_all = lax.all_gather(qkv_bias, "fsdp", axis=1, tiled=True)
        bias_own = lax.dynamic_slice_in_dim(bias_all, ctx * 128, 128, axis=1).reshape(-1)
    bias_block = jnp.pad(bias_own, (0, spare - 384)).reshape(16, lanes)
    weights = gather(jnp.concatenate([own_qkv, bias_block], axis=0), "fsdp", size)
    if size > 4:
        weights = jnp.concatenate(
            [jnp.transpose(weights[:, :384], (1, 0, 2)).reshape(384, width),
             jnp.pad(bias_own, (0, 16 * width - 384)).reshape(16, width)], axis=0)[None]

    x0 = own_half(layer_input, tp)
    quarter = half // 2
    x4 = [hop_x(x0[:quarter]), hop_x(x0[quarter:])]
    other = hop_y(blocks[1])
    hidden_own = jnp.where(tp == core, blocks[0], other)
    pair = jnp.stack([deal_order, hop_core(deal_order)])
    order = jnp.concatenate([pair, hop_x(pair)]).reshape(-1) % rows
    near = [layer_input, hop_core(layer_input)]
    hidden_own, weights = lax.optimization_barrier((hidden_own, weights))
    hidden0 = gather(hidden_own, "fsdp", size)
    x5 = [hop_y(p) for p in x4]
    far = x4 + x5 + [hop_core(p) for p in x4 + x5]
    u = jnp.arange(8, dtype=jnp.int32)
    dest = dev ^ jnp.where(u < 4, (u & 6) | ((u & 1) ^ tp), u)
    slot = jnp.arange(rows, dtype=jnp.int32)
    first_len = seq_lengths[0, :1]
    packed_index = (ctx ^ (slot // own_rows)) * own_rows + slot % own_rows
    position, rank, meet = row_places(order, packed_index, seq_lengths[0], dest)
    rank = rank[None]
    cos_t, sin_t = rope_tables_t(position)

    near_mixed = qkv_rope(ctx_ref, near, weights, cos_t, sin_t, 0)
    cot_embed_own = own_half(cot_embed, tp)
    far, near_mixed, cot_embed_own = lax.optimization_barrier((far, near_mixed, cot_embed_own))
    if size <= 4:
        dense_half = run(dense_half_kernel, shape((shard_rows // 2 + 16, width + emb), bf16), "dense_half", 1)(
            jnp.stack([core, tp]).astype(jnp.int32), after(out_weight, near_mixed), proj_weight,
            *[v.reshape(1, -1) for v in vectors])
    dense_pair = jnp.stack([dense_half, hop_y(dense_half)])
    far_mixed = qkv_rope(ctx_ref, far, weights, cos_t, sin_t, rows // 2)
    dense_copies = jnp.broadcast_to(dense_pair[None], (size,) + dense_pair.shape)
    hidden0, far_mixed, dense_copies = lax.optimization_barrier((hidden0, far_mixed, dense_copies))
    dense_parts = trade(dense_copies, "fsdp")
    hiddens = [hidden0, hop_y(hidden0), hop_x(hidden0), hop(hidden0, 5)]
    att, sorted_t, att_t, lse = attention_forward(first_len, meet, dest, rank, near_mixed, far_mixed)
    att, dense_parts, hiddens[1:3] = lax.optimization_barrier((att, dense_parts, hiddens[1:3]))
    att = trade(att, CT)
    dense, proj_full, vec, up_b = run(
        dense_natural_kernel,
        (shape((width, width), bf16), shape((width, emb), bf16), shape((8, width), f32), shape((1, 4 * units), f32)),
        "dense_natural", 1)(
        jnp.stack([core, place, tp]).astype(jnp.int32), dense_parts, hop_core(dense_parts))
    att, dense, proj_full, vec, up_b = lax.optimization_barrier((att, dense, proj_full, vec, up_b))

    f_rows, b_rows = shape((half, width), f32), shape((half, width), bf16)
    normed, hat1, rstd1, normed_low = run(
        out_proj_kernel, (f_rows, f_rows, shape((half, 1), f32), b_rows), "out_proj", 1)(
        tp_ref, dense, layer_input, att, vec)
    normed_peer = hop_core(normed_low)
    hidden = shape((own_rows, 4 * units), bf16)
    act, slope, own_down, peer_down = run(mlp_kernel, (hidden, hidden, f_rows, b_rows), "mlp")(
        normed_low, normed_peer, up_b, *hiddens)
    w_own = after(weights, hiddens[3])
    w_y, w_x = hop_y(w_own), hop_x(w_own)
    act, slope, own_down, peer_down, w_y, w_x = lax.optimization_barrier((act, slope, own_down, peer_down, w_y, w_x))
    w_cut = max(1, w_own.shape[0] // 2)
    w_xy = [hop(after(w_own[:w_cut], own_down), 5)]
    vec_shape = shape((8, width), f32)
    final_top, final_end, embed_low, grad_second, g2, proj_grad, vec2 = run(
        head_kernel,
        (shape((half // 2, width), bf16),) * 2
        + (shape((half, emb), bf16), f_rows, b_rows, shape((width, emb), bf16), vec_shape), "heads", 1,
        flops=2_000_000_000)(
        tp_ref, normed, own_down, hop_core(peer_down), vec, proj_full, cot_output, cot_embed_own)
    final_top, final_end, embed_low, grad_second, g2, proj_grad, vec2, w_xy[0] = lax.optimization_barrier(
        (final_top, final_end, embed_low, grad_second, g2, proj_grad, vec2, w_xy[0]))
    g2_peer = hop_core(g2)
    if w_cut < w_own.shape[0]:
        w_xy.append(hop(after(w_own[w_cut:], w_xy[0]), 5))
    final_halves = [hop_y(after(final_top, g2))]
    g1, up_bias_part, own_normed, peer_normed = run(
        mlp_back_kernel, (hidden, shape((1, 4 * units), f32), f_rows, b_rows), "mlp_back")(
        g2, g2_peer, slope, *hiddens)
    g1, up_bias_part, own_normed, peer_normed, final_halves[0], w_xy = lax.optimization_barrier(
        (g1, up_bias_part, own_normed, peer_normed, final_halves[0], w_xy))
    w_near = [w_own, w_y, w_x, jnp.concatenate(w_xy, axis=0)]
    w_all = w_near + [hop_core(after(w, own_normed)) for w in w_near]
    grad_first, g0, att_grad, vec1 = run(
        first_back_kernel, (f_rows, b_rows, shape((8, half, 128), bf16), vec_shape), "first_back")(
        grad_second, own_normed, hop_core(peer_normed), hat1, rstd1, vec, dense)
    grad_first, g0, att_grad, vec1, w_all = lax.optimization_barrier((grad_first, g0, att_grad, vec1, w_all))
    att_grad = lax.all_to_all(att_grad, CT, 0, 0, tiled=True)
    dense_rows = (shard_rows // 4 + shard_rows // 8) * sides
    dense_grad = run(out_weight_kernel, shape((2, 4, size, dense_rows, units), bf16), "out_weight")(
        g0, att, proj_grad, vec2, vec1)
    dense_own = lax.dynamic_index_in_dim(dense_grad, core, 0, keepdims=False)
    dense_recv = hop_core(lax.dynamic_index_in_dim(dense_grad, 1 - core, 0, keepdims=False))
    *up_grads, down_grad = run(
        mlp_weights_kernel,
        (shape((size, shard + 16 + dense_rows, units), bf16),) * 4 + (shape((size, 4, strip, width), bf16),),
        "mlp_weights", 1)(
        place_ref, normed_low, normed_peer, g2, g2_peer, act, g1, up_bias_part, dense_own, dense_recv)
    att_grad, up_grads, down_grad = lax.optimization_barrier((att_grad, up_grads, down_grad))
    XY = ("cx", "tp")
    down_parts = trade(down_grad, "fsdp")
    up_parts = [up_grads[0], hop_y(up_grads[1]), hop_x(up_grads[2]), hop(up_grads[3], 5)]
    final_rest, embed_late = after(final_end, att_grad), after(embed_low, att_grad)
    final_halves.append(hop_y(final_rest))
    embed_peer = hop_y(embed_late)
    grad_qkv, qkv_bias_part = attention_backward(
        first_len, meet, dest, rank, sorted_t, att_t, lse, cos_t, sin_t, att_grad)
    grad_qkv, up_parts, down_parts, final_halves, embed_peer = lax.optimization_barrier(
        (grad_qkv, up_parts, down_parts, final_halves, embed_peer))
    grad_rows = trade(grad_qkv, CT)

    base = fs if size <= 4 else jnp.zeros_like(fs)
    qkv_sums = run(qkv_weight_kernel, shape((size, 400, lanes), bf16), "qkv_weight", 1)(
        jnp.concatenate([dest, base[None]]).astype(jnp.int32), grad_qkv, qkv_bias_part, *near, *far)
    qkv_sums, up_parts, down_parts = lax.optimization_barrier((qkv_sums, up_parts, down_parts))
    up_sum, *down_sums = run(
        sum_kernel, (shape(up_grads[0].shape, bf16),) + (shape((strip, width), bf16),) * 4, "sums", 1)(
        jnp.stack([base, place]).astype(jnp.int32), *up_parts, down_parts)
    up_parts = send_z(up_sum)
    down_parts = [down_sums[0], hop_y(down_sums[1]), hop_x(down_sums[2]), hop(down_sums[3], 5)]

    qkv_sums, grad_rows = lax.optimization_barrier((qkv_sums, grad_rows))
    input_low = run(input_grad_kernel, b_rows, "input_grad", 1)(dev_ref, grad_first, grad_rows, *w_all)
    input_peer = hop_y(input_low)
    up_parts, down_parts, qkv_sums, final_top, final_end, embed_low = lax.optimization_barrier(
        (up_parts, down_parts, qkv_sums, final_top, final_end, embed_low, input_low))[:6]
    own_q = add_all(send_z(qkv_sums))
    q_all = around_ctx(own_q, ctx)

    side_rows = shape((shard + 16, units), bf16)
    send, away, dense_own = run(
        hidden_split_kernel, (side_rows, side_rows, shape((dense_rows, units), bf16)), "hidden_split", 1)(
        core.astype(jnp.int32).reshape(1), *up_parts, *down_parts)
    recv = hop_core(away)
    dense_all = around_ctx(dense_own, ctx)
    halves = jnp.stack([jnp.where(core == 0, send, recv), jnp.where(core == 0, recv, send)])
    joined = trade(jnp.concatenate([halves, halves], axis=0), XY)
    joined, input_peer = lax.optimization_barrier((joined, input_peer))
    joined_core = hop_core(joined)
    up_weight_grad, down_weight_grad, bias_rows = run(
        hidden_join_kernel, (shape(up_weight.shape, f32), shape(down_weight.shape, f32), shape((4, 16, units), f32)),
        "hidden_join", 1)(core.astype(jnp.int32).reshape(1), joined, joined_core)
    up_bias_grad = lax.dynamic_slice_in_dim(bias_rows[:, 0], fs * strip, strip, axis=1).reshape(-1)

    q_all = q_all.reshape(4, 400, lanes)
    qkv_weight_grad = jnp.transpose(q_all[:, :384].reshape(4, 3, 128, lanes), (3, 1, 0, 2)).reshape(
        lanes, 3, 512).astype(f32)
    qb = jnp.transpose(q_all[:, 384:].reshape(4, -1)[:, :384].reshape(4, 3, 128), (1, 0, 2)).reshape(3, 512)
    bias_width = qkv_bias.shape[1]
    qkv_bias_grad = lax.dynamic_slice_in_dim(qb, fs * bias_width, bias_width, axis=1).astype(f32)

    thin, tail_rows = shard_rows // 4, shard_rows // 8
    out_weight_grad = jnp.transpose(
        dense_all[:, :thin * sides].reshape(4, sides, thin, units), (0, 2, 1, 3)).reshape(shard_rows, width).astype(f32)
    rest = dense_all[:, thin * sides:].reshape(4, sides, tail_rows, units // 128, 128)[:3]
    rest = jnp.transpose(rest, (1, 3, 2, 0, 4)).reshape(shard_rows, 384)
    rest = pair_rows(rest, [hop_y(rest)], tp).astype(f32)
    proj_weight_grad = rest[:, :emb]
    sums = jnp.transpose(rest[:, emb:emb + 6])

    return (
        pair_rows([final_top, final_end], final_halves, tp),
        pair_rows(embed_low, [embed_peer], tp),
        pair_rows(after(input_low, send), [input_peer], tp),
        qkv_weight_grad,
        qkv_bias_grad,
        out_weight_grad,
        sums[5],
        sums[3],
        sums[4],
        up_weight_grad,
        up_bias_grad,
        down_weight_grad,
        sums[2],
        sums[0],
        sums[1],
        proj_weight_grad,
    )


def solution(mesh):
    fine = Mesh(
        mesh.devices.reshape(mesh.shape["fsdp"], mesh.shape["ctx"] // 2, 2, mesh.shape["tp"]),
        ("fsdp", "cx", "core", "tp"))
    by_rows = ("fsdp", "cx", "core")
    placed = (
        P(by_rows, None),
        P("fsdp", None),
        P(by_rows),
        P("fsdp", None, "tp"),
        P(None, ("tp", "fsdp")),
        P(("tp", "fsdp"), None),
        P("fsdp"),
        P("fsdp"),
        P("fsdp"),
        P("fsdp", "tp"),
        P(("tp", "fsdp")),
        P(("tp", "fsdp"), None),
        P("fsdp"),
        P("fsdp"),
        P("fsdp"),
        P("fsdp", None),
        P(by_rows, None),
        P(by_rows, None),
    )
    outs = (P(by_rows, None), P(by_rows, None), P(by_rows, None)) + placed[3:16]
    return jax.shard_map(shards, mesh=fine, in_specs=placed, out_specs=outs, check_vma=False)
```

```python
import math
from functools import partial
import jax, jax.numpy as jnp
from jax import lax
from jax.experimental import pallas as pl
from jax.experimental.pallas import tpu as pltpu
from jax.sharding import Mesh
from jax.sharding import PartitionSpec as P

f32, bf16 = jnp.float32, jnp.bfloat16
HEAD_DIM = 64
VMEM_CAP = 56 * 1024 * 1024
MASKED = -1e30
SMALL_GRANT = ("mlp", "mlp_weights", "out_proj", "sums", "out_weight", "dense_natural", "hidden_join", "hidden_split", "dense_half", "pick")
SPARE = 14
TS = 256
FQ, FK = 1024, 512
BQ, BK = 512, 512


def nt(a, b):
    return lax.dot_general(a, b, (((1,), (1,)), ((), ())), preferred_element_type=f32)


def nn(a, b):
    return lax.dot_general(a, b, (((1,), (0,)), ((), ())), preferred_element_type=f32)


def run(kernel, out_shape, name, scalars=0, scratch=(), flops=1_000_000):
    def call(*args):
        vm = pl.BlockSpec(memory_space=pltpu.VMEM)
        sm = pl.BlockSpec(memory_space=pltpu.SMEM)
        outs = jax.tree.map(lambda _: vm, out_shape)
        need = sum(x.size * x.dtype.itemsize for x in list(args) + jax.tree.leaves(out_shape))
        limit = min(VMEM_CAP, need + (SPARE << 20)) if name in SMALL_GRANT else VMEM_CAP
        return pl.pallas_call(
            kernel, out_shape=out_shape,
            in_specs=[sm] * scalars + [vm] * (len(args) - scalars), out_specs=outs,
            scratch_shapes=list(scratch),
            compiler_params=pltpu.CompilerParams(vmem_limit_bytes=limit),
            cost_estimate=pl.CostEstimate(flops=flops, transcendentals=0, bytes_accessed=10_000 if flops < 2_000_000 else 8_000_000),
            name=name)(*args)
    return call


def one_hot(rank_ref, tile, start, width):
    want = lax.broadcasted_iota(jnp.int32, (TS, width), 0) + tile * TS
    return jnp.where(rank_ref[:, pl.ds(start, width)] == want, 1.0, 0.0).astype(bf16)


def key_span(start, size, first_len, tile, total):
    lo = jnp.where(start >= first_len, first_len // tile, 0)
    hi = jnp.where(start + size <= first_len, (first_len + tile - 1) // tile, total // tile)
    return lo, hi


def code_lanes(base, rows, first_len):
    row = lax.broadcasted_iota(jnp.int32, (rows, 128), 0) + base
    lane = lax.broadcasted_iota(jnp.int32, (rows, 128), 1)
    bad = jnp.where(row < first_len, 1, 0)
    return jnp.where(lane == bad, MASKED, jnp.where((lane >= 2) & (lane < 5), 1.0, 0.0)).astype(bf16)


def code_rows(base, cols, first_len):
    row = lax.broadcasted_iota(jnp.int32, (128, cols), 0)
    col = lax.broadcasted_iota(jnp.int32, (128, cols), 1) + base
    return (jnp.where(row == jnp.where(col < first_len, 0, 1), 1.0, 0.0), row)


def head_rows(values, head):
    row = lax.broadcasted_iota(jnp.int32, values.shape, 0)
    return jnp.where((row // HEAD_DIM) == head, values, 0.0)


def head_lanes(values, head):
    lane = lax.broadcasted_iota(jnp.int32, values.shape, 1)
    return jnp.where((lane // HEAD_DIM) == head, values, 0.0)


def forward_kernel(len_ref, meet_ref, dest_ref, rank_ref, near_ref, far_ref, att_ref, sorted_ref, att_t_ref, lse_ref,
                   k_ext, q_ext, arr_t):
    rows = rank_ref.shape[1]
    block = rows // 4
    first_len = len_ref[0]
    scale = HEAD_DIM ** -0.5

    def sort_tile(tile, carry):
        at = pl.multiple_of(tile * TS, TS)
        arr_t[:, pl.ds(0, TS)] = jnp.zeros((384, TS), f32)
        for d in range(4):
            @pl.when(meet_ref[tile * 4 + d] > 0)
            def _():
                hot = one_hot(rank_ref, tile, d * block, block)
                mixed_ref = near_ref if d < 2 else far_ref
                arr_t[:, pl.ds(0, TS)] += nt(mixed_ref[:, pl.ds((d % 2) * block, block)], hot)
        low = arr_t[:, pl.ds(0, TS)].astype(bf16)
        sorted_ref[:, pl.ds(at, TS)] = low
        wide = low.astype(f32)
        query = wide[0:128] * scale
        code, _ = code_rows(at, TS, first_len)
        for h in range(2):
            q_ext[h, 0:128, pl.ds(at, TS)] = head_rows(query, h).astype(bf16)
            q_ext[h, 128:256, pl.ds(at, TS)] = code.astype(bf16)
        k_ext[pl.ds(at, TS), 0:128] = wide[128:256].T.astype(bf16)
        k_ext[pl.ds(at, TS), 128:256] = code_lanes(at, TS, first_len)
        return carry

    lax.fori_loop(0, rows // TS, sort_tile, 0)

    def query_tile(i, carry):
        at = pl.multiple_of(i * FQ, FQ)
        lo, hi = key_span(at, FQ, first_len, FK, rows)

        def key_tile(j, state):
            kat = pl.multiple_of(j * FK, FK)
            keys = k_ext[pl.ds(kat, FK), :]
            out = []
            for h in range(2):
                top, total, acc = state[h]
                scores = nn(keys, q_ext[h, :, pl.ds(at, FQ)])
                new_top = jnp.maximum(top, jnp.max(scores, axis=0, keepdims=True))
                fade = jnp.exp(top - new_top)
                weights = jnp.exp(scores - new_top)
                total = total * fade + jnp.sum(weights, axis=0, keepdims=True)
                value = sorted_ref[256 + h * 64:320 + h * 64, pl.ds(kat, FK)]
                acc = acc * fade + nn(value, weights.astype(bf16))
                out.append((new_top, total, acc))
            return tuple(out)

        start = (jnp.full((1, FQ), MASKED, f32), jnp.zeros((1, FQ), f32), jnp.zeros((64, FQ), f32))
        state = lax.fori_loop(lo, hi, key_tile, (start, start))
        lse_rows = []
        for h in range(2):
            top, total, acc = state[h]
            att_t_ref[h * 64:(h + 1) * 64, pl.ds(at, FQ)] = (acc / total).astype(bf16)
            lse_ref[h:h + 1, pl.ds(at, FQ)] = top + jnp.log(total)
        return carry

    lax.fori_loop(0, rows // FQ, query_tile, 0)

    for d in range(4):
        arr_t[0:128, :] = jnp.zeros((128, block), f32)

        def back_tile(tile, carry):
            @pl.when(meet_ref[tile * 4 + d] > 0)
            def _():
                at = pl.multiple_of(tile * TS, TS)
                hot = one_hot(rank_ref, tile, d * block, block)
                arr_t[0:128, :] += nn(att_t_ref[:, pl.ds(at, TS)], hot)
            return carry

        lax.fori_loop(0, rows // TS, back_tile, 0)
        low = arr_t[0:128, :].T.astype(bf16)
        att_ref[dest_ref[2 * d]] = low[:block // 2]
        att_ref[dest_ref[2 * d + 1]] = low[block // 2:]


def attention_forward(first_len, meet, dest, rank, near, far):
    rows = rank.shape[1]
    return pl.pallas_call(
        forward_kernel,
        out_shape=(
            jax.ShapeDtypeStruct((8, rows // 8, 128), bf16),
            jax.ShapeDtypeStruct((384, rows), bf16),
            jax.ShapeDtypeStruct((128, rows), bf16),
            jax.ShapeDtypeStruct((8, rows), f32),
        ),
        in_specs=[
            pl.BlockSpec(memory_space=pltpu.SMEM),
            pl.BlockSpec(memory_space=pltpu.SMEM),
            pl.BlockSpec(memory_space=pltpu.SMEM),
            pl.BlockSpec(memory_space=pltpu.VMEM),
            pl.BlockSpec(memory_space=pltpu.VMEM),
            pl.BlockSpec(memory_space=pltpu.VMEM),
        ],
        out_specs=tuple(pl.BlockSpec(memory_space=pltpu.VMEM) for _ in range(4)),
        scratch_shapes=[
            pltpu.VMEM((rows, 256), bf16),
            pltpu.VMEM((2, 256, rows), bf16),
            pltpu.VMEM((384, rows // 4), f32),
        ],
        compiler_params=pltpu.CompilerParams(vmem_limit_bytes=VMEM_CAP),
        cost_estimate=pl.CostEstimate(flops=60_000_000_000, transcendentals=0, bytes_accessed=10_000),
        name="attention_forward",
    )(first_len, meet, dest, rank, near, far)


def split3(v):
    hi = v.astype(bf16).astype(f32)
    mid = (v - hi).astype(bf16).astype(f32)
    return hi, mid, v - hi - mid


def backward_kernel(len_ref, meet_ref, dest_ref, rank_ref, sorted_ref, att_t_ref, lse_ref, cos_ref, sin_ref,
                    grad_ref, *refs):
    (out_ref, bias_ref, k_ext, q_ext, v_ext, g_ext, q_nat, g_nat, dq_t, arr_t, ds_low) = refs
    rows = rank_ref.shape[1]
    block = rows // 4
    first_len = len_ref[0]
    scale = HEAD_DIM ** -0.5

    def sort_tile(tile, carry):
        at = pl.multiple_of(tile * TS, TS)
        q_t = sorted_ref[0:128, pl.ds(at, TS)].astype(f32) * scale
        k_ext[pl.ds(at, TS), 0:128] = sorted_ref[128:256, pl.ds(at, TS)].astype(f32).T.astype(bf16)
        k_ext[pl.ds(at, TS), 128:256] = code_lanes(at, TS, first_len)
        v_ext[pl.ds(at, TS), 0:128] = sorted_ref[256:384, pl.ds(at, TS)].astype(f32).T.astype(bf16)
        v_ext[pl.ds(at, TS), 128:256] = code_lanes(at, TS, first_len)
        arr_t[0:TS, 0:128] = jnp.zeros((TS, 128), f32)
        for d in range(4):
            @pl.when(meet_ref[tile * 4 + d] > 0)
            def _():
                hot = one_hot(rank_ref, tile, d * block, block)
                half = block // 2
                arr_t[0:TS, 0:128] += (nn(hot[:, :half], grad_ref[dest_ref[2 * d]])
                                       + nn(hot[:, half:], grad_ref[dest_ref[2 * d + 1]]))
        grad = arr_t[0:TS, 0:128]
        grad_t = grad.T
        q = q_t.T
        code, row = code_rows(at, TS, first_len)
        prod = grad_t * att_t_ref[:, pl.ds(at, TS)].astype(f32)
        for h in range(2):
            delta = jnp.sum(prod[h * 64:(h + 1) * 64], axis=0, keepdims=True)
            lse = lse_ref[h:h + 1, pl.ds(at, TS)]
            l0, l1, l2 = split3(-lse)
            d0, d1, d2 = split3(-delta)
            q_ext[h, 0:128, pl.ds(at, TS)] = head_rows(q_t, h).astype(bf16)
            q_ext[h, 128:256, pl.ds(at, TS)] = jnp.where(
                row == 2, l0, jnp.where(row == 3, l1, jnp.where(row == 4, l2, code))).astype(bf16)
            g_ext[h, 0:128, pl.ds(at, TS)] = head_rows(grad_t, h).astype(bf16)
            g_ext[h, 128:256, pl.ds(at, TS)] = jnp.where(
                row == 2, d0, jnp.where(row == 3, d1, jnp.where(row == 4, d2, 0.0))).astype(bf16)
            q_nat[h, pl.ds(at, TS), :] = head_lanes(q, h).astype(bf16)
            g_nat[h, pl.ds(at, TS), :] = head_lanes(grad, h).astype(bf16)
        return carry

    lax.fori_loop(0, rows // TS, sort_tile, 0)
    dq_t[...] = jnp.zeros(dq_t.shape, f32)

    def key_tile(j, carry):
        kat = pl.multiple_of(j * BK, BK)
        lo, hi = key_span(kat, BK, first_len, BQ, rows)

        def query_tile(i, state):
            dk, dv = state
            at = pl.multiple_of(i * BQ, BQ)
            keys = k_ext[pl.ds(kat, BK), :]
            values = v_ext[pl.ds(kat, BK), :]
            for h in range(2):
                probs = jnp.exp(nn(keys, q_ext[h, :, pl.ds(at, BQ)]))
                dprob = nn(values, g_ext[h, :, pl.ds(at, BQ)])
                dscore = (probs * dprob).astype(bf16)
                dv = dv + nn(probs.astype(bf16), g_nat[h, pl.ds(at, BQ), :])
                dk = dk + nn(dscore, q_nat[h, pl.ds(at, BQ), :])
                dq_t[h * 64:(h + 1) * 64, pl.ds(at, BQ)] += nn(
                    sorted_ref[128 + h * 64:192 + h * 64, pl.ds(kat, BK)], dscore)
            return dk, dv

        zero = jnp.zeros((BK, 128), f32)
        dk, dv = lax.fori_loop(lo, hi, query_tile, (zero, zero))
        ds_low[128:256, pl.ds(kat, BK)] = dk.T.astype(bf16)
        ds_low[256:384, pl.ds(kat, BK)] = dv.T.astype(bf16)
        return carry

    lax.fori_loop(0, rows // BK, key_tile, 0)
    ds_low[0:128, :] = (dq_t[...] * scale).astype(bf16)
    bias = jnp.zeros((384, 1), f32)
    for d in range(4):
        arr_t[...] = jnp.zeros((384, block), f32)

        def back_tile(tile, carry):
            @pl.when(meet_ref[tile * 4 + d] > 0)
            def _():
                at = pl.multiple_of(tile * TS, TS)
                hot = one_hot(rank_ref, tile, d * block, block)
                arr_t[...] += nn(ds_low[:, pl.ds(at, TS)], hot)
            return carry

        lax.fori_loop(0, rows // TS, back_tile, 0)
        cos, sin = cos_ref[:, pl.ds(d * block, block)], sin_ref[:, pl.ds(d * block, block)]
        for base in (0, 64, 128, 192):
            front, back = arr_t[base:base + 32, :], arr_t[base + 32:base + 64, :]
            arr_t[base:base + 32, :] = front * cos + back * sin
            arr_t[base + 32:base + 64, :] = back * cos - front * sin
        bias = bias + jnp.sum(arr_t[...], axis=1, keepdims=True)
        out_ref[dest_ref[2 * d]] = arr_t[:, 0:block // 2].astype(bf16)
        out_ref[dest_ref[2 * d + 1]] = arr_t[:, block // 2:block].astype(bf16)
    bias_ref[...] = bias


def attention_backward(first_len, meet, dest, rank, sorted_t, att_t, lse, cos_t, sin_t, grad):
    rows = rank.shape[1]
    vm = pl.BlockSpec(memory_space=pltpu.VMEM)
    sm = pl.BlockSpec(memory_space=pltpu.SMEM)
    return pl.pallas_call(
        backward_kernel,
        out_shape=(
            jax.ShapeDtypeStruct((8, 384, rows // 8), bf16),
            jax.ShapeDtypeStruct((384, 1), f32),
        ),
        in_specs=[sm, sm, sm] + [vm] * 7,
        out_specs=(vm, vm),
        scratch_shapes=[
            pltpu.VMEM((rows, 256), bf16),
            pltpu.VMEM((2, 256, rows), bf16),
            pltpu.VMEM((rows, 256), bf16),
            pltpu.VMEM((2, 256, rows), bf16),
            pltpu.VMEM((2, rows, 128), bf16),
            pltpu.VMEM((2, rows, 128), bf16),
            pltpu.VMEM((128, rows), f32),
            pltpu.VMEM((384, rows // 4), f32),
            pltpu.VMEM((384, rows), bf16),
        ],
        compiler_params=pltpu.CompilerParams(vmem_limit_bytes=VMEM_CAP),
        cost_estimate=pl.CostEstimate(flops=90_000_000_000, transcendentals=0, bytes_accessed=10_000),
        name="attention_backward",
    )(first_len, meet, dest, rank, sorted_t, att_t, lse, cos_t, sin_t, grad)


def qkv_kernel(ctx_ref, cos_ref, sin_ref, w_ref, *refs, first):
    out_ref = refs[-1]
    size, _, lanes = w_ref.shape
    bias = jnp.zeros((1, 384), f32)
    for f in range(size):
        bias_row = jnp.concatenate(
            [w_ref[f, 384 + i:385 + i, :].astype(f32) for i in range(-(-384 // lanes))], axis=1)[:, :384]
        bias = jnp.where(ctx_ref[0] == f, bias_row, bias) if size == 4 else jnp.where(f == 0, bias_row, bias)
    bias = jnp.broadcast_to(bias, (128, 384)).T[:, 0:1]
    start = 0
    for x_ref in refs[:-1]:
        count = x_ref.shape[0]
        span = slice(start, start + count)
        mixed = jnp.broadcast_to(bias, (384, count))
        for f in range(size):
            mixed = mixed + nt(w_ref[f, 0:384], x_ref[:, f * lanes:(f + 1) * lanes])
        table = slice(first + start, first + start + count)
        cos, sin = cos_ref[:, table], sin_ref[:, table]
        for base in (0, 64, 128, 192):
            front, back = mixed[base:base + 32], mixed[base + 32:base + 64]
            out_ref[base:base + 32, span] = (front * cos - back * sin).astype(bf16)
            out_ref[base + 32:base + 64, span] = (back * cos + front * sin).astype(bf16)
        out_ref[256:384, span] = mixed[256:384].astype(bf16)
        start += count


def qkv_rope(ctx, pieces, weights, cos_t, sin_t, first):
    rows = sum(p.shape[0] for p in pieces)
    return run(partial(qkv_kernel, first=first), jax.ShapeDtypeStruct((384, rows), bf16), "qkv_rope", 1)(
        ctx, cos_t, sin_t, weights, *pieces)


def row_places(order, packed, lengths, dest):
    rows = order.shape[0]
    first_len = lengths[0]
    digit = jnp.arange(64, dtype=jnp.int32)
    high = (order // 64)[None, :] == digit[:, None]
    low = ((order % 64)[None, :] == digit[:, None]).astype(bf16)
    parts = jnp.stack([packed // 64, packed % 64]).astype(f32)
    left = jnp.where(high[None], parts[:, None, :], 0.0).astype(bf16).reshape(128, rows)
    table = nt(left, low)
    table = (table[:64] * 64.0 + table[64:]).reshape(8, rows // 8)
    picked = dest[:, None, None] == jnp.arange(8, dtype=jnp.int32)[None, :, None]
    place = jnp.sum(jnp.where(picked, table[None], 0.0), axis=1).reshape(rows).astype(jnp.int32)
    in_first = place < first_len
    position = jnp.where(in_first, place, place - first_len)
    flags = in_first.astype(f32).reshape(rows // 128, 128)
    before = jnp.arange(128)[:, None] < jnp.arange(128)[None, :]
    within = jnp.dot(flags.astype(bf16), before.astype(bf16), preferred_element_type=f32)
    sums = jnp.sum(flags, axis=1)
    n = rows // 128
    earlier = jnp.arange(n)[None, :] < jnp.arange(n)[:, None]
    offset = jnp.sum(jnp.where(earlier, sums[None, :], 0.0), axis=1)
    firsts = (within + offset[:, None]).reshape(rows).astype(jnp.int32)
    index = jnp.arange(rows, dtype=jnp.int32)
    rank = jnp.where(in_first, firsts, first_len + index - firsts)
    counts = jnp.sum(in_first.astype(jnp.int32).reshape(4, rows // 4), axis=1)
    d = jnp.arange(4)
    lo0 = jnp.sum(jnp.where(d[None, :] < d[:, None], counts[None, :], 0), axis=1)
    hi0 = lo0 + counts
    lo1 = first_len + d * (rows // 4) - lo0
    hi1 = lo1 + rows // 4 - counts
    t0 = jnp.arange(rows // TS)[:, None] * TS
    t1 = t0 + TS
    meet = (((lo0[None] < t1) & (hi0[None] > t0) & (hi0 > lo0)[None])
            | ((lo1[None] < t1) & (hi1[None] > t0) & (hi1 > lo1)[None])).astype(jnp.int32)
    return position, rank, meet.reshape(-1)


def rope_tables_t(position):
    frequency = jnp.exp(jnp.arange(32, dtype=f32) * (-2.0 * math.log(10000.0) / 64))
    angles = frequency[:, None] * position.astype(f32)[None, :]
    return jnp.cos(angles), jnp.sin(angles)


norm_eps = 1e-05
embed_eps = 1e-06
WIDTHS = (128, 96, 64)
CT = ("cx", "core", "tp")
CTX = ("cx", "core")


def tn(a, b):
    return lax.dot_general(a, b, (((0,), (0,)), ((), ())), preferred_element_type=f32)


def head_rows_of(device):
    return ((device & 1) * 4 + (device >> 1)) * 128


def row_mean(v):
    return jnp.mean(v, axis=1, keepdims=True)


def norm_parts(v):
    centred = v - row_mean(v)
    rstd = lax.rsqrt(row_mean(centred * centred) + norm_eps)
    return centred * rstd, rstd


def norm_back(grad, x_hat, rstd, gain):
    e = grad * gain
    return (e - row_mean(e) - x_hat * row_mean(e * x_hat)) * rstd


def col_sum(v):
    return jnp.sum(v, axis=0, keepdims=True)


def out_proj_kernel(tp_ref, w_ref, x_ref, att_ref, vec_ref, normed_ref, hat_ref, rstd_ref, low_ref):
    half = normed_ref.shape[0]
    own = pl.ds(pl.multiple_of(tp_ref[0] * half, half), half)
    acc = x_ref[own, :].astype(f32) + vec_ref[0:1]
    for j in range(8):
        at = head_rows_of(j)
        acc = acc + nn(att_ref[j], w_ref[at:at + 128, 0:acc.shape[1]])
    x_hat, rstd = norm_parts(acc)
    normed = x_hat * vec_ref[1:2] + vec_ref[2:3]
    normed_ref[...] = normed
    hat_ref[...] = x_hat
    rstd_ref[...] = rstd
    low_ref[...] = normed.astype(bf16)


def hidden_refs(refs):
    return [(lambda f, r=r: (r, f)) for r in refs[0:4]]


def up_rows(block, f, shard):
    ref, i = block(f)
    return ref[i, 0:shard]


def down_rows(block, group, strip, shard, side):
    parts = []
    for f in group:
        ref, i = block(f)
        at = shard + side * strip
        parts.append(ref[i, at:at + strip])
    return jnp.concatenate(parts, axis=0) if len(parts) > 1 else parts[0]


def hidden_sizes(refs, width):
    size, _, units = refs[0].shape
    strip = units // size
    step = max(1, 256 // strip)
    groups = [range(g, g + step) for g in range(0, size, step)]
    return size, units, strip, width // size, width // units, groups


def mlp_kernel(own_ref, peer_ref, bias_ref, *refs):
    act_ref, slope_ref, own_out, peer_out = refs[4:]
    half, width = own_ref.shape
    size, units, strip, shard, sides, groups = hidden_sizes(refs, width)
    blocks = hidden_refs(refs)
    for r, x_ref in enumerate((own_ref, peer_ref)):
        rows = slice(r * half, (r + 1) * half)
        out = [jnp.zeros((half, units), f32) for _ in range(sides)]
        for v in range(4):
            cols = slice(v * units, (v + 1) * units)
            up = jnp.broadcast_to(bias_ref[:, cols], (half, units))
            for f in range(size):
                up = up + nn(x_ref[:, f * shard:(f + 1) * shard], up_rows(blocks[v], f, shard))
            phi_int = 0.5 * (1.0 + lax.erf(up * (0.5 ** 0.5)))
            density = jnp.exp(-0.5 * up * up) * ((2.0 * math.pi) ** -0.5)
            act = (up * phi_int).astype(bf16)
            act_ref[rows, cols] = act
            slope_ref[rows, cols] = (phi_int + up * density).astype(bf16)
            for g in groups:
                at = g[0] * strip
                part = act[:, at:at + len(g) * strip]
                for s in range(sides):
                    out[s] = out[s] + nn(part, down_rows(blocks[v], g, strip, shard, s))
        for s in range(sides):
            if r == 0:
                own_out[:, s * units:(s + 1) * units] = out[s]
            else:
                peer_out[:, s * units:(s + 1) * units] = out[s].astype(bf16)


def head_kernel(tp_ref, normed_ref, own_ref, recv_ref, all_vec_ref, proj_ref, cot_ref, cot_embed_ref,
                first_ref, last_ref, embed_ref, grad_ref, low_ref, proj_grad_ref, vec_ref):
    half = normed_ref.shape[0]
    mine = pl.ds(pl.multiple_of(tp_ref[0] * half, half), half)
    gain = all_vec_ref[4:5]
    second = normed_ref[...] + own_ref[...] + recv_ref[...].astype(f32) + all_vec_ref[3:4]
    x_hat, rstd = norm_parts(second)
    final = (x_hat * gain + all_vec_ref[5:6]).astype(bf16)
    first_ref[...] = final[:half // 2]
    last_ref[...] = final[half // 2:]
    projected = nn(final, proj_ref[...])
    cot = cot_embed_ref[...].astype(f32)
    col = lax.broadcasted_iota(jnp.int32, projected.shape, 1)
    embedded = jnp.zeros(projected.shape, f32)
    grad_proj = jnp.zeros(projected.shape, f32)
    start = 0
    for width in WIDTHS:
        here = (col >= start) & (col < start + width)
        part = jnp.where(here, projected, 0.0)
        r = lax.rsqrt(jnp.sum(part * part, axis=1, keepdims=True) + embed_eps)
        n = part * r
        along = jnp.sum(n * cot, axis=1, keepdims=True)
        embedded = embedded + n
        grad_proj = jnp.where(here, r * (cot - n * along), grad_proj)
        start += width
    embed_ref[...] = embedded.astype(bf16)
    proj_low = grad_proj.astype(bf16)
    proj_grad_ref[...] = tn(final, proj_low).astype(bf16)
    grad_final = cot_ref[mine, :].astype(f32) + nt(proj_low, proj_ref[...])
    grad_second = norm_back(grad_final, x_hat, rstd, gain)
    grad_ref[...] = grad_second
    low_ref[...] = grad_second.astype(bf16)
    vec_ref[...] = jnp.zeros(vec_ref.shape, f32)
    vec_ref[0:1] = col_sum(grad_final * x_hat)
    vec_ref[1:2] = col_sum(grad_final)
    vec_ref[2:3] = col_sum(grad_second)


def mlp_back_kernel(own_ref, peer_ref, slope_ref, *refs):
    g1_ref, bias_ref, own_out, peer_out = refs[4:]
    half, width = own_ref.shape
    size, units, strip, shard, sides, groups = hidden_sizes(refs, width)
    blocks = hidden_refs(refs)
    for r, g_ref in enumerate((own_ref, peer_ref)):
        rows = slice(r * half, (r + 1) * half)
        out = [jnp.zeros((half, shard), f32) for _ in range(size)]
        for v in range(4):
            for g in groups:
                at = v * units + g[0] * strip
                cols = slice(at, at + len(g) * strip)
                grad_up = nt(g_ref[:, 0:units], down_rows(blocks[v], g, strip, shard, 0))
                for s in range(1, sides):
                    grad_up = grad_up + nt(
                        g_ref[:, s * units:(s + 1) * units], down_rows(blocks[v], g, strip, shard, s))
                grad_up = grad_up * slope_ref[rows, cols].astype(f32)
                sums = col_sum(grad_up)
                bias_ref[:, cols] = sums if r == 0 else bias_ref[:, cols] + sums
                g1_ref[rows, cols] = grad_up.astype(bf16)
            g1 = g1_ref[rows, v * units:(v + 1) * units]
            for f in range(size):
                out[f] = out[f] + nt(g1, up_rows(blocks[v], f, shard))
        for f in range(size):
            if r == 0:
                own_out[:, f * shard:(f + 1) * shard] = out[f]
            else:
                peer_out[:, f * shard:(f + 1) * shard] = out[f].astype(bf16)


def mlp_weights_kernel(place_ref, own_n, peer_n, own_g, peer_g, act_ref, g1_ref, bias_ref, dense_ref, recv_ref,
                       up0, up1, up2, up3, down_ref):
    size, _, units = up0.shape
    strip, shard = down_ref.shape[2], own_n.shape[1] // size
    normed = jnp.concatenate([own_n[...], peer_n[...]], axis=0)
    g2 = jnp.concatenate([own_g[...], peer_g[...]], axis=0)
    for v, up_ref in enumerate((up0, up1, up2, up3)):
        q = place_ref[0] ^ v
        cols = slice(v * units, (v + 1) * units)
        up = tn(normed, g1_ref[:, cols]).astype(bf16)
        down = tn(act_ref[:, cols], g2).astype(bf16)
        bias = jnp.broadcast_to(bias_ref[:, cols], (16, units)).astype(bf16)
        for f in range(size):
            up_ref[f, 0:shard] = up[f * shard:(f + 1) * shard]
            up_ref[f, shard:shard + 16] = bias
            up_ref[f, shard + 16:] = (dense_ref[q, f].astype(f32) + recv_ref[q, f].astype(f32)).astype(bf16)
            down_ref[f, q] = down[f * strip:(f + 1) * strip]


def sum_kernel(index_ref, p0, p1, p2, p3, down_ref, up_out, *down_outs):
    size = up_out.shape[0]
    for f in range(size):
        total = p0[f].astype(f32) + p1[f].astype(f32) + p2[f].astype(f32) + p3[f].astype(f32)
        up_out[(f - index_ref[0] + size) % size] = total.astype(bf16)
    for v, out in enumerate(down_outs):
        total = down_ref[0, index_ref[1] ^ v].astype(f32)
        for f in range(1, size):
            total = total + down_ref[f, index_ref[1] ^ v].astype(f32)
        out[...] = total.astype(bf16)


def pick_kernel(place_ref, up_ref, down_ref, *outs):
    strip = down_ref.shape[0] // 4
    shard, units = up_ref.shape[0], up_ref.shape[1] // 4
    for n in range(2):
        q = place_ref[0] ^ n
        for f in range(units // strip):
            at = pl.multiple_of((f * 4 + q) * strip, strip)
            outs[n][0:shard, f * strip:(f + 1) * strip] = up_ref[:, pl.ds(at, strip)]
        rows = pl.multiple_of(q * strip, strip)
        for s in range(down_ref.shape[1] // units):
            at = shard + s * strip
            outs[n][at:at + strip] = down_ref[pl.ds(rows, strip), s * units:(s + 1) * units]


def dense_half_kernel(index_ref, dense_ref, proj_ref, *refs):
    vecs, half = refs[:7], refs[7]
    core, tp = (index_ref[i] for i in range(2))
    count, width = dense_ref.shape[0] // 2, dense_ref.shape[1]
    half[0:count, 0:width] = dense_ref[pl.ds(pl.multiple_of(core * count, count), count), :]
    half[0:count, width:] = proj_ref[pl.ds(pl.multiple_of((tp * 2 + core) * count, count), count), :]
    lines, line = [], []
    for v in vecs:
        line.append(v[...].astype(f32))
        if sum(p.shape[1] for p in line) == width:
            lines.append(jnp.concatenate(line, axis=1))
            line = []
    block = jnp.concatenate(lines + [jnp.zeros((16 - len(lines), width), f32)], axis=0)
    half[count:count + 16, 0:width] = block.astype(bf16)
    half[count:count + 16, width:] = jnp.zeros((16, half.shape[1] - width), bf16)


def dense_natural_kernel(index_ref, own_ref, core_ref, out_ref, proj_ref, vec_ref, up_ref):
    core, place, tp = (index_ref[i] for i in range(3))
    size, rows = own_ref.shape[0], own_ref.shape[2] - 16
    units = up_ref.shape[1] // 4
    strip, quarter = units // size, vec_ref.shape[1] // size
    for f in range(size):
        for t in range(2):
            own, other = own_ref[f, tp ^ t, 0:rows], core_ref[f, tp ^ t, 0:rows]
            for k in range(2):
                at = ((t * size + f) * 2 + k) * rows
                value = jnp.where(core == k, own, other)
                out_ref[at:at + rows, :] = value[:, 0:out_ref.shape[1]]
                at = ((f * 2 + t) * 2 + k) * rows
                proj_ref[at:at + rows, :] = value[:, out_ref.shape[1]:]
        vecs = own_ref[f, 0, rows:rows + 16].astype(f32)
        wanted = own_ref[f, tp ^ core, rows:rows + 16].astype(f32)
        cut = 4 * strip
        ups = wanted[0:1, 0:cut]
        for i in range(6):
            r, c = divmod(cut + i * quarter, 4 * quarter)
            vec_ref[i:i + 1, f * quarter:(f + 1) * quarter] = vecs[r:r + 1, c:c + quarter]
        for v in range(4):
            picked = jnp.zeros((1, strip), f32)
            for q in range(4):
                picked = jnp.where((place ^ v) == q, ups[:, q * strip:(q + 1) * strip], picked)
            up_ref[:, v * units + f * strip:v * units + (f + 1) * strip] = picked


def hidden_split_kernel(core_ref, *refs):
    keep_ref, away_ref, dense_ref = refs[-3:]
    ups, downs = refs[:-7], refs[-7:-3]
    rows, units = keep_ref.shape
    strip, width = downs[0].shape

    def total(parts, where):
        out = parts[0][where].astype(f32)
        for p in parts[1:]:
            out = out + p[where].astype(f32)
        return out.astype(bf16)

    def store(up_ref, down_ref):
        up_ref[...] = total(ups, (slice(0, rows), slice(None)))
        down_ref[...] = jnp.zeros(down_ref.shape, bf16)
        for s in range(width // units):
            down_ref[s * strip:(s + 1) * strip] = total(downs, (slice(None), slice(s * units, (s + 1) * units)))

    dense_ref[...] = total(ups, (slice(rows, None), slice(None)))

    @pl.when(core_ref[0] == 0)
    def _():
        store(keep_ref, away_ref)

    @pl.when(core_ref[0] == 1)
    def _():
        store(away_ref, keep_ref)


def hidden_join_kernel(core_ref, own_ref, core_peer_ref, up_ref, down_ref, bias_ref):
    strip = down_ref.shape[0] // 4
    shard, units = up_ref.shape[0], own_ref.shape[2]

    def store(ups, downs):
        for q in range(4):
            for f in range(units // strip):
                at = (f * 4 + q) * strip
                up_ref[:, at:at + strip] = ups[q, 0:shard, f * strip:(f + 1) * strip].astype(f32)
            bias_ref[q] = ups[q, shard:shard + 16].astype(f32)
            for s in range(down_ref.shape[1] // units):
                down_ref[q * strip:(q + 1) * strip, s * units:(s + 1) * units] = (
                    downs[q, s * strip:(s + 1) * strip].astype(f32))

    @pl.when(core_ref[0] == 0)
    def _():
        store(own_ref, core_peer_ref)

    @pl.when(core_ref[0] == 1)
    def _():
        store(core_peer_ref, own_ref)


def first_back_kernel(second_ref, own_ref, recv_ref, hat_ref, rstd_ref, all_vec_ref, w_ref,
                      grad_ref, low_ref, att_grad_ref, vec_ref):
    grad_normed = second_ref[...] + own_ref[...] + recv_ref[...].astype(f32)
    x_hat = hat_ref[...]
    grad_first = norm_back(grad_normed, x_hat, rstd_ref[...], all_vec_ref[1:2])
    grad_ref[...] = grad_first
    low = grad_first.astype(bf16)
    low_ref[...] = low
    for j in range(8):
        at = head_rows_of(j)
        att_grad_ref[j] = nt(low, w_ref[at:at + 128, 0:low.shape[1]]).astype(bf16)
    vec_ref[...] = jnp.zeros(vec_ref.shape, f32)
    vec_ref[0:1] = col_sum(grad_normed * x_hat)
    vec_ref[1:2] = col_sum(grad_normed)
    vec_ref[2:3] = col_sum(grad_first)


def out_weight_kernel(low_ref, att_ref, proj_grad_ref, vec2_ref, vec1_ref, out_ref):
    width = low_ref.shape[1]
    _, _, size, rows, cols = out_ref.shape
    shard = width // (2 * size)
    thin, tail_rows = shard // 4, shard // 8
    sides = width // cols

    def store(t, f, part, at, value):
        for s in range(sides):
            first = at * sides + s * value.shape[0]
            out_ref[part % 2, part // 2 * 2 + t, f, first:first + value.shape[0]] = value[:, s * cols:(s + 1) * cols]

    for j in range(8):
        grad = tn(att_ref[j], low_ref[...]).astype(bf16)
        for start in range(0, 128, thin):
            block, rest = divmod(head_rows_of(j) + start, shard)
            store(block // size, block % size, rest // thin, 0, grad[start:start + thin])
    vecs = jnp.concatenate([vec2_ref[0:3], vec1_ref[0:3], jnp.zeros((122, width), f32)], axis=0).T
    tail = jnp.concatenate([proj_grad_ref[...].astype(f32), vecs[:, 0:96]], axis=1).astype(bf16)
    for f in range(size):
        for t in range(2):
            part = tail[(f * 2 + t) * shard:(f * 2 + t + 1) * shard]
            for b in range(4):
                if b < 3:
                    value = jnp.concatenate(
                        [part[g * tail_rows:(g + 1) * tail_rows, b * 128:(b + 1) * 128] for g in range(8)], axis=1)
                else:
                    value = jnp.zeros((tail_rows, width), bf16)
                store(t, f, b, thin, value)


def qkv_weight_kernel(dest_ref, d_ref, bias_ref, *refs):
    out_ref = refs[-1]
    size, _, lanes = out_ref.shape
    acc = jnp.zeros((384, size * lanes), f32)
    start, part = 0, d_ref.shape[2]
    for x_ref in refs[:-1]:
        done = 0
        while done < x_ref.shape[0]:
            count = min(x_ref.shape[0] - done, part)
            u, at = start // part, start % part
            acc = acc + nn(d_ref[dest_ref[u], :, at:at + count], x_ref[done:done + count])
            start, done = start + count, done + count
    row = jnp.broadcast_to(bias_ref[...], (384, 128)).T[0:1]
    row = jnp.concatenate([row, jnp.zeros((1, max(0, -(-384 // lanes) * lanes - 384)), f32)], axis=1) if 384 % lanes else row
    count = row.shape[1] // lanes
    lines = [row[:, i * lanes:(i + 1) * lanes] for i in range(count)]
    block = jnp.concatenate(lines + [jnp.zeros((16 - count, lanes), f32)], axis=0).astype(bf16)
    for f in range(size):
        s = (f - dest_ref[8] + size) % size
        out_ref[s, 0:384] = acc[:, f * lanes:(f + 1) * lanes].astype(bf16)
        out_ref[s, 384:400] = block


def input_grad_kernel(dev_ref, first_ref, d_ref, *refs):
    out_ref = refs[-1]
    parts, _, lanes = refs[0].shape
    for f in range(parts):
        cols = slice(f * lanes, (f + 1) * lanes)
        acc = first_ref[:, cols]
        for n, w_ref in enumerate(refs[:-1]):
            mask = (0, 1, 4, 5, 2, 3, 6, 7)[n]
            acc = acc + tn(d_ref[dev_ref[0] ^ mask], w_ref[f, 0:384])
        out_ref[:, cols] = acc.astype(bf16)


def hop(value, u):
    return lax.ppermute(value, CT, [(i, i ^ u) for i in range(8)])


def hop_core(value):
    return lax.ppermute(value, "core", [(0, 1), (1, 0)])


def hop_x(value):
    return lax.ppermute(value, "cx", [(0, 1), (1, 0)])


def hop_y(value):
    return lax.ppermute(value, "tp", [(0, 1), (1, 0)])


def shift_z(value, count, size):
    return lax.ppermute(value, "fsdp", [(i, (i + count) % size) for i in range(size)])


def trade(value, axes):
    return lax.all_to_all(value, axes, 0, 0, tiled=True)


def gather(value, axes, count):
    return trade(jnp.broadcast_to(value[None], (count,) + value.shape), axes)


def add_all(parts):
    total = parts[0].astype(f32)
    for p in parts[1:]:
        total = total + p.astype(f32)
    return total.astype(bf16)


def send_z(value):
    size = lax.axis_size("fsdp")
    if size > 4:
        return list(trade(value, "fsdp"))
    return [value[0]] + [
        lax.ppermute(value[s], "fsdp", [(i, (i + s) % size) for i in range(size)]) for s in range(1, size)]


def around_ctx(value, ctx):
    far = hop_x(value)
    return by_xor([value, hop_core(value), far, hop_core(far)], ctx)


def by_xor(parts, own):
    stacked = jnp.stack(parts)
    return jnp.stack([lax.dynamic_index_in_dim(stacked, own ^ i, 0, keepdims=False) for i in range(len(parts))])


def pair_rows(own, peers, tp):
    own = own if isinstance(own, list) else [own]
    half = sum(p.shape[0] for p in own)
    out = jnp.concatenate(own + own, axis=0)
    at = (1 - tp) * half
    for p in peers:
        out = lax.dynamic_update_slice_in_dim(out, p, at, axis=0)
        at = at + p.shape[0]
    return out


def shards(
    layer_input,
    seq_lengths,
    deal_order,
    qkv_weight,
    qkv_bias,
    out_weight,
    out_bias,
    first_gain,
    first_shift,
    up_weight,
    up_bias,
    down_weight,
    down_bias,
    second_gain,
    second_shift,
    proj_weight,
    cot_output,
    cot_embed,
):
    own_rows, width = layer_input.shape
    half = own_rows // 2
    rows = own_rows * 4
    fs, cx, core, tp = (lax.axis_index(n) for n in ("fsdp", "cx", "core", "tp"))
    size = lax.axis_size("fsdp")
    ctx = cx * 2 + core
    dev = ctx * 2 + tp
    dev_ref = dev.astype(jnp.int32).reshape(1)
    shape = jax.ShapeDtypeStruct

    def own_half(value, which):
        return lax.dynamic_slice_in_dim(value, which * half, half, axis=0)

    def after(value, *others):
        return lax.optimization_barrier((value,) + others)[0]

    place = cx * 2 + tp
    strip = down_weight.shape[0] // 4
    units = size * strip
    shard = up_weight.shape[0]
    place_ref = place.astype(jnp.int32).reshape(1)
    tp_ref = tp.astype(jnp.int32).reshape(1)
    ctx_ref = ctx.astype(jnp.int32).reshape(1)
    sides = width // units
    hidden_rows = shard + sides * strip
    emb = proj_weight.shape[1]
    shard_rows = out_weight.shape[0]
    vectors = [up_bias, out_bias, first_gain, first_shift, down_bias, second_gain, second_shift]
    if size > 4:
        def hidden_block(q):
            wide = up_weight.reshape(shard, size, 4, strip)
            up = lax.dynamic_index_in_dim(wide, q, 2, keepdims=False).reshape(shard, units)
            down = lax.dynamic_slice_in_dim(down_weight, q * strip, strip, axis=0)
            return jnp.concatenate([up] + [down[:, s * units:(s + 1) * units] for s in range(sides)], axis=0)

        blocks = [hidden_block(place), hidden_block(place ^ 1)]
        half_rows = shard_rows // 2
        part = lax.dynamic_slice_in_dim(proj_weight, tp * shard_rows, shard_rows, axis=0)
        vec_block = jnp.concatenate(vectors).reshape(-1, 4 * shard)
        vec_block = jnp.pad(vec_block, ((0, 16 - vec_block.shape[0]), (0, width + emb - 4 * shard)))
        beside = jnp.concatenate([out_weight, part], axis=1)
        dense_half = jnp.concatenate(
            [lax.dynamic_slice_in_dim(beside, core * half_rows, half_rows, axis=0), vec_block], axis=0)
    else:
        blocks = run(pick_kernel, (shape((hidden_rows, units), bf16),) * 2, "pick", 1)(place_ref, up_weight, down_weight)
    lanes = shard
    own_qkv = lax.dynamic_slice_in_dim(qkv_weight, ctx * 128, 128, axis=2)
    own_qkv = jnp.transpose(own_qkv, (1, 2, 0)).reshape(384, lanes)
    spare = 16 * lanes
    if size == 4:
        bias_own = qkv_bias.reshape(-1)
    else:
        bias_all = lax.all_gather(qkv_bias, "fsdp", axis=1, tiled=True)
        bias_own = lax.dynamic_slice_in_dim(bias_all, ctx * 128, 128, axis=1).reshape(-1)
    bias_block = jnp.pad(bias_own, (0, spare - 384)).reshape(16, lanes)
    weights = gather(jnp.concatenate([own_qkv, bias_block], axis=0), "fsdp", size)
    if size > 4:
        weights = jnp.concatenate(
            [jnp.transpose(weights[:, :384], (1, 0, 2)).reshape(384, width),
             jnp.pad(bias_own, (0, 16 * width - 384)).reshape(16, width)], axis=0)[None]

    x0 = own_half(layer_input, tp)
    quarter = half // 2
    x4 = [hop_x(x0[:quarter]), hop_x(x0[quarter:])]
    other = hop_y(blocks[1])
    hidden_own = jnp.where(tp == core, blocks[0], other)
    pair = jnp.stack([deal_order, hop_core(deal_order)])
    order = jnp.concatenate([pair, hop_x(pair)]).reshape(-1) % rows
    near = [layer_input, hop_core(layer_input)]
    hidden_own, weights = lax.optimization_barrier((hidden_own, weights))
    hidden0 = gather(hidden_own, "fsdp", size)
    x5 = [hop_y(p) for p in x4]
    far = x4 + x5 + [hop_core(p) for p in x4 + x5]
    u = jnp.arange(8, dtype=jnp.int32)
    dest = dev ^ jnp.where(u < 4, (u & 6) | ((u & 1) ^ tp), u)
    slot = jnp.arange(rows, dtype=jnp.int32)
    first_len = seq_lengths[0, :1]
    packed_index = (ctx ^ (slot // own_rows)) * own_rows + slot % own_rows
    position, rank, meet = row_places(order, packed_index, seq_lengths[0], dest)
    rank = rank[None]
    cos_t, sin_t = rope_tables_t(position)

    near_mixed = qkv_rope(ctx_ref, near, weights, cos_t, sin_t, 0)
    cot_embed_own = own_half(cot_embed, tp)
    far, near_mixed, cot_embed_own = lax.optimization_barrier((far, near_mixed, cot_embed_own))
    if size <= 4:
        dense_half = run(dense_half_kernel, shape((shard_rows // 2 + 16, width + emb), bf16), "dense_half", 1)(
            jnp.stack([core, tp]).astype(jnp.int32), after(out_weight, near_mixed), proj_weight,
            *[v.reshape(1, -1) for v in vectors])
    dense_pair = jnp.stack([dense_half, hop_y(dense_half)])
    far_mixed = qkv_rope(ctx_ref, far, weights, cos_t, sin_t, rows // 2)
    dense_copies = jnp.broadcast_to(dense_pair[None], (size,) + dense_pair.shape)
    hidden0, far_mixed, dense_copies = lax.optimization_barrier((hidden0, far_mixed, dense_copies))
    dense_parts = trade(dense_copies, "fsdp")
    hiddens = [hidden0, hop_y(hidden0), hop_x(hidden0), hop(hidden0, 5)]
    att, sorted_t, att_t, lse = attention_forward(first_len, meet, dest, rank, near_mixed, far_mixed)
    att, dense_parts, hiddens[1:3] = lax.optimization_barrier((att, dense_parts, hiddens[1:3]))
    att = trade(att, CT)
    dense, proj_full, vec, up_b = run(
        dense_natural_kernel,
        (shape((width, width), bf16), shape((width, emb), bf16), shape((8, width), f32), shape((1, 4 * units), f32)),
        "dense_natural", 1)(
        jnp.stack([core, place, tp]).astype(jnp.int32), dense_parts, hop_core(dense_parts))
    att, dense, proj_full, vec, up_b = lax.optimization_barrier((att, dense, proj_full, vec, up_b))

    f_rows, b_rows = shape((half, width), f32), shape((half, width), bf16)
    normed, hat1, rstd1, normed_low = run(
        out_proj_kernel, (f_rows, f_rows, shape((half, 1), f32), b_rows), "out_proj", 1)(
        tp_ref, dense, layer_input, att, vec)
    normed_peer = hop_core(normed_low)
    hidden = shape((own_rows, 4 * units), bf16)
    act, slope, own_down, peer_down = run(mlp_kernel, (hidden, hidden, f_rows, b_rows), "mlp")(
        normed_low, normed_peer, up_b, *hiddens)
    w_own = after(weights, hiddens[3])
    w_y, w_x = hop_y(w_own), hop_x(w_own)
    act, slope, own_down, peer_down, w_y, w_x = lax.optimization_barrier((act, slope, own_down, peer_down, w_y, w_x))
    w_cut = max(1, w_own.shape[0] // 2)
    w_xy = [hop(after(w_own[:w_cut], own_down), 5)]
    vec_shape = shape((8, width), f32)
    final_top, final_end, embed_low, grad_second, g2, proj_grad, vec2 = run(
        head_kernel,
        (shape((half // 2, width), bf16),) * 2
        + (shape((half, emb), bf16), f_rows, b_rows, shape((width, emb), bf16), vec_shape), "heads", 1,
        flops=2_000_000_000)(
        tp_ref, normed, own_down, hop_core(peer_down), vec, proj_full, cot_output, cot_embed_own)
    final_top, final_end, embed_low, grad_second, g2, proj_grad, vec2, w_xy[0] = lax.optimization_barrier(
        (final_top, final_end, embed_low, grad_second, g2, proj_grad, vec2, w_xy[0]))
    g2_peer = hop_core(g2)
    if w_cut < w_own.shape[0]:
        w_xy.append(hop(after(w_own[w_cut:], w_xy[0]), 5))
    final_halves = [hop_y(after(final_top, g2))]
    g1, up_bias_part, own_normed, peer_normed = run(
        mlp_back_kernel, (hidden, shape((1, 4 * units), f32), f_rows, b_rows), "mlp_back")(
        g2, g2_peer, slope, *hiddens)
    g1, up_bias_part, own_normed, peer_normed, final_halves[0], w_xy = lax.optimization_barrier(
        (g1, up_bias_part, own_normed, peer_normed, final_halves[0], w_xy))
    w_near = [w_own, w_y, w_x, jnp.concatenate(w_xy, axis=0)]
    w_all = w_near + [hop_core(after(w, own_normed)) for w in w_near]
    grad_first, g0, att_grad, vec1 = run(
        first_back_kernel, (f_rows, b_rows, shape((8, half, 128), bf16), vec_shape), "first_back")(
        grad_second, own_normed, hop_core(peer_normed), hat1, rstd1, vec, dense)
    grad_first, g0, att_grad, vec1, w_all = lax.optimization_barrier((grad_first, g0, att_grad, vec1, w_all))
    att_grad = lax.all_to_all(att_grad, CT, 0, 0, tiled=True)
    dense_rows = (shard_rows // 4 + shard_rows // 8) * sides
    dense_grad = run(out_weight_kernel, shape((2, 4, size, dense_rows, units), bf16), "out_weight")(
        g0, att, proj_grad, vec2, vec1)
    dense_own = lax.dynamic_index_in_dim(dense_grad, core, 0, keepdims=False)
    dense_recv = hop_core(lax.dynamic_index_in_dim(dense_grad, 1 - core, 0, keepdims=False))
    *up_grads, down_grad = run(
        mlp_weights_kernel,
        (shape((size, shard + 16 + dense_rows, units), bf16),) * 4 + (shape((size, 4, strip, width), bf16),),
        "mlp_weights", 1)(
        place_ref, normed_low, normed_peer, g2, g2_peer, act, g1, up_bias_part, dense_own, dense_recv)
    att_grad, up_grads, down_grad = lax.optimization_barrier((att_grad, up_grads, down_grad))
    XY = ("cx", "tp")
    down_parts = trade(down_grad, "fsdp")
    up_parts = [up_grads[0], hop_y(up_grads[1]), hop_x(up_grads[2]), hop(up_grads[3], 5)]
    final_rest, embed_late = after(final_end, att_grad), after(embed_low, att_grad)
    final_halves.append(hop_y(final_rest))
    embed_peer = hop_y(embed_late)
    grad_qkv, qkv_bias_part = attention_backward(
        first_len, meet, dest, rank, sorted_t, att_t, lse, cos_t, sin_t, att_grad)
    grad_qkv, up_parts, down_parts, final_halves, embed_peer = lax.optimization_barrier(
        (grad_qkv, up_parts, down_parts, final_halves, embed_peer))
    grad_rows = trade(grad_qkv, CT)

    base = fs if size <= 4 else jnp.zeros_like(fs)
    qkv_sums = run(qkv_weight_kernel, shape((size, 400, lanes), bf16), "qkv_weight", 1)(
        jnp.concatenate([dest, base[None]]).astype(jnp.int32), grad_qkv, qkv_bias_part, *near, *far)
    qkv_sums, up_parts, down_parts = lax.optimization_barrier((qkv_sums, up_parts, down_parts))
    up_sum, *down_sums = run(
        sum_kernel, (shape(up_grads[0].shape, bf16),) + (shape((strip, width), bf16),) * 4, "sums", 1)(
        jnp.stack([base, place]).astype(jnp.int32), *up_parts, down_parts)
    up_parts = send_z(up_sum)
    down_parts = [down_sums[0], hop_y(down_sums[1]), hop_x(down_sums[2]), hop(down_sums[3], 5)]

    qkv_sums, grad_rows = lax.optimization_barrier((qkv_sums, grad_rows))
    input_low = run(input_grad_kernel, b_rows, "input_grad", 1)(dev_ref, grad_first, grad_rows, *w_all)
    input_peer = hop_y(input_low)
    up_parts, down_parts, qkv_sums, final_top, final_end, embed_low = lax.optimization_barrier(
        (up_parts, down_parts, qkv_sums, final_top, final_end, embed_low, input_low))[:6]
    own_q = add_all(send_z(qkv_sums))
    q_all = around_ctx(own_q, ctx)

    side_rows = shape((shard + 16, units), bf16)
    send, away, dense_own = run(
        hidden_split_kernel, (side_rows, side_rows, shape((dense_rows, units), bf16)), "hidden_split", 1)(
        core.astype(jnp.int32).reshape(1), *up_parts, *down_parts)
    recv = hop_core(away)
    dense_all = around_ctx(dense_own, ctx)
    halves = jnp.stack([jnp.where(core == 0, send, recv), jnp.where(core == 0, recv, send)])
    joined = trade(jnp.concatenate([halves, halves], axis=0), XY)
    joined, input_peer = lax.optimization_barrier((joined, input_peer))
    joined_core = hop_core(joined)
    up_weight_grad, down_weight_grad, bias_rows = run(
        hidden_join_kernel, (shape(up_weight.shape, f32), shape(down_weight.shape, f32), shape((4, 16, units), f32)),
        "hidden_join", 1)(core.astype(jnp.int32).reshape(1), joined, joined_core)
    up_bias_grad = lax.dynamic_slice_in_dim(bias_rows[:, 0], fs * strip, strip, axis=1).reshape(-1)

    q_all = q_all.reshape(4, 400, lanes)
    qkv_weight_grad = jnp.transpose(q_all[:, :384].reshape(4, 3, 128, lanes), (3, 1, 0, 2)).reshape(
        lanes, 3, 512).astype(f32)
    qb = jnp.transpose(q_all[:, 384:].reshape(4, -1)[:, :384].reshape(4, 3, 128), (1, 0, 2)).reshape(3, 512)
    bias_width = qkv_bias.shape[1]
    qkv_bias_grad = lax.dynamic_slice_in_dim(qb, fs * bias_width, bias_width, axis=1).astype(f32)

    thin, tail_rows = shard_rows // 4, shard_rows // 8
    out_weight_grad = jnp.transpose(
        dense_all[:, :thin * sides].reshape(4, sides, thin, units), (0, 2, 1, 3)).reshape(shard_rows, width).astype(f32)
    rest = dense_all[:, thin * sides:].reshape(4, sides, tail_rows, units // 128, 128)[:3]
    rest = jnp.transpose(rest, (1, 3, 2, 0, 4)).reshape(shard_rows, 384)
    rest = pair_rows(rest, [hop_y(rest)], tp).astype(f32)
    proj_weight_grad = rest[:, :emb]
    sums = jnp.transpose(rest[:, emb:emb + 6])

    return (
        pair_rows([final_top, final_end], final_halves, tp),
        pair_rows(embed_low, [embed_peer], tp),
        pair_rows(after(input_low, send), [input_peer], tp),
        qkv_weight_grad,
        qkv_bias_grad,
        out_weight_grad,
        sums[5],
        sums[3],
        sums[4],
        up_weight_grad,
        up_bias_grad,
        down_weight_grad,
        sums[2],
        sums[0],
        sums[1],
        proj_weight_grad,
    )


def solution(mesh):
    fine = Mesh(
        mesh.devices.reshape(mesh.shape["fsdp"], mesh.shape["ctx"] // 2, 2, mesh.shape["tp"]),
        ("fsdp", "cx", "core", "tp"))
    by_rows = ("fsdp", "cx", "core")
    placed = (
        P(by_rows, None),
        P("fsdp", None),
        P(by_rows),
        P("fsdp", None, "tp"),
        P(None, ("tp", "fsdp")),
        P(("tp", "fsdp"), None),
        P("fsdp"),
        P("fsdp"),
        P("fsdp"),
        P("fsdp", "tp"),
        P(("tp", "fsdp")),
        P(("tp", "fsdp"), None),
        P("fsdp"),
        P("fsdp"),
        P("fsdp"),
        P("fsdp", None),
        P(by_rows, None),
        P(by_rows, None),
    )
    outs = (P(by_rows, None), P(by_rows, None), P(by_rows, None)) + placed[3:16]
    return jax.shard_map(shards, mesh=fine, in_specs=placed, out_specs=outs, check_vma=False)
```
